32 devices in a mesh: wide: 8 (over z, x), narrow: 4 (over y, core).
Axes of the slice: x: 2, y: 2, z: 4, core: 2. Of those that a mesh axis runs over, the one named last changes fastest.
Arguments:
- solution: float32 [2, 3, 64, 192, 384], P(None, None, 'wide', 'narrow'), may hold values from -4 to 4
- source_term: float32 [2, 3, 64, 192, 384], P(None, None, 'wide', 'narrow'), may hold values from -6 to 6
- permittivity: bfloat16 [64, 192, 384], P('wide', 'narrow'), may hold values from 1 to 12
- inv_top: bfloat16 [16384, 16384], P('wide', 'narrow'), may hold values from -0.015625 to 0.015625
- inv_mid: bfloat16 [2, 8192, 8192], P(None, 'wide', 'narrow'), may hold values from -0.0234375 to 0.0234375
- inv_low: bfloat16 [4, 8192, 8192], P(None, 'wide', 'narrow'), may hold values from -0.0234375 to 0.0234375
- sep_tile: int32 [512, 1], replicated, may hold values from 0 to 31; in each aligned block of 512 rows (0 to 511, 512 to 1023, ...) at most 32 rows name the same one
- sep_cell: int32 [512, 128], replicated, may hold values from 0 to 442367, as said below
Outputs:
- new_solution: float32 [2, 3, 64, 192, 384], P(None, None, 'wide', 'narrow')
- new_residual: float32 [2, 3, 64, 192, 384], P(None, None, 'wide', 'narrow')
The draws below stay inside these ranges and needn't reach their ends.
Inputs may be any that keep to these rules, and one draw needn't show every extreme that they name: `sep_tile`: the tile index w * 4 + n of the tile at wide index w and narrow index n that holds the block; every tile holds at least one block and at most 32, and some tile holds exactly 32. `sep_cell`: all entries of the array are distinct.
All inputs are finite; a program needn't handle non-finite values.
Results may differ from the reference program's by a relative error of at most 0.0014.
Values may be sent and summed in bfloat16 or wider, within the bound.
No kernel may reach another device: no remote copies, remote signals or barrier semaphores. Data moves between devices by JAX's collectives and lax.ppermute only.
A program may use at most 192 MiB of HBM per device.

```python
import math
import jax
import jax.numpy as jnp
import numpy as np
from jax import lax

NSRC = 2
BLK = 128
W1 = 16384
WM = 8192
WL = 8192
CX = 8
CY = 48
CZ = 384
NX = 64
NY = 192
NZ = 384
SEP = 65536
NBLK = 512
MOSTB = 32
N_WIDE = 8
N_NARROW = 4


def draw_sep_cell(key, part):
    total_cells = 3 * CX * CY * CZ
    entry_count = NBLK * BLK
    first_key, second_key = jax.random.split(jax.random.fold_in(key, 17))
    middle = jax.random.permutation(first_key, total_cells - 2)[:entry_count - 2].astype(jnp.int32) + 1
    ends = jnp.array([0, total_cells - 1], jnp.int32)
    entries = jnp.concatenate([ends, middle])
    order = jax.random.permutation(second_key, entry_count)
    return entries[order].reshape(NBLK, BLK).astype(jnp.int32)


def steps_of(rng, shape, cuts, least, top_value):
    def one(axis_at, blocks):
        steps = jax.random.uniform(jax.random.fold_in(jax.random.fold_in(rng, 6), axis_at), (blocks,), jnp.float32, least / len(cuts), top_value / len(cuts))
        return jnp.repeat(jnp.exp(steps), shape[axis_at] // blocks).reshape((-1,) + (1,) * (len(shape) - axis_at - 1))

    level = one(*cuts[0])
    for cut in cuts[1:]:
        level = level * one(*cut)
    return level


def assign_block(own_key, own, number, rows, number_of, top, reach, skew):
    order = jax.random.permutation(own_key, number_of)
    heavy_load, ordinary = portions_of(number_of, rows * top, reach, skew, True), portions_of(number_of, rows * top, reach, skew, False)
    places = jnp.arange(number_of)

    def named(tallies, turn):
        used = int((tallies > 0).sum())
        fixed = max(1, used // 4)
        moved = fixed + (places - fixed + turn * (used - fixed)) % max(1, number_of - fixed)
        return jnp.zeros((number_of,), jnp.int32).at[order[jnp.where(places < fixed, places, moved)]].set(jnp.asarray(tallies, jnp.int32))

    tallies = jnp.where(number % 4 == 0, named(heavy_load, number // 4), named(ordinary, number - number // 4 - 1))
    mixed = jax.random.permutation(jax.random.fold_in(own, 3), number_of)
    source_of, receiver = mixed[0:number_of // 2 * 2:2], mixed[1:number_of // 2 * 2:2]
    margin = jnp.minimum(tallies[source_of] - 1, reach - tallies[receiver]) // 2
    margin = jnp.where((source_of == order[0]) | (receiver == order[0]) | (tallies[receiver] == 0), 0, jnp.maximum(margin, 0))
    moved = jax.random.randint(jax.random.fold_in(own, 4), (number_of // 2,), 0, 1 << 20) % (margin + 1)
    tallies = tallies.at[source_of].add(-moved).at[receiver].add(moved)
    labels = jnp.searchsorted(jnp.cumsum(tallies), jnp.arange(rows * top), side="right").astype(jnp.int32)
    listing = labels.reshape(top, rows).T
    listing = listing[jax.random.permutation(jax.random.fold_in(own, 1), rows)]
    turn = jax.random.randint(jax.random.fold_in(own, 2), (rows, 1), 0, top)
    return jnp.take_along_axis(listing, (jnp.arange(top)[None, :] + turn) % top, axis=1)


def portions_of(number_of, total, most, skew, full):
    portions = [(1 << 20) // math.isqrt(standing ** skew) + 1 for standing in range(1, number_of + 1)]
    largest = most if full else min(most, max(-(-total // number_of), total * portions[0] // sum(portions)))
    least = 1 if total - largest >= number_of - 1 else 0
    counts, spare = [largest] + [least] * (number_of - 1), total - largest - least * (number_of - 1)
    while spare > 0:
        candidates = [i for i in range(1, number_of) if counts[i] < largest] or [i for i in range(1, number_of) if counts[i] < most]
        whole, left = sum([portions[i] for i in candidates]), spare
        for i in candidates:
            extra = min(most - counts[i], max(1, left * portions[i] // whole), spare)
            counts[i] = counts[i] + extra
            spare = spare - extra
    return np.array(counts)


def normal_values(rng, dims, width, reach, shards=(), kind=jnp.bfloat16):
    values = width * jax.random.normal(rng, dims, jnp.float32)
    if shards:
        values = values * steps_of(rng, dims, shards, -0.22, 0.18)
    return jnp.clip(values, -reach, reach).astype(kind)


def setup_inputs(seed: int = 0) -> dict:
    splits = jax.random.split(jax.random.key(seed), 9)
    solution = normal_values(splits[0], (NSRC, 3, NX, NY, NZ), 0.3, 4.0, ((2, 8), (3, 4)), jnp.float32)
    source_term = normal_values(splits[1], (NSRC, 3, NX, NY, NZ), 1.0, 6.0, ((2, 8), (3, 4)), jnp.float32)
    permittivity = jnp.clip(jnp.exp(math.log(12.0) - 2.4849066 * jax.random.uniform(splits[2], (NX, NY, NZ), jnp.float32) ** steps_of(splits[2], (NX, NY, NZ), ((0, 8), (1, 4)), -0.2, 0.2)), 1.0, 12.0).astype(jnp.bfloat16)
    inv_top = normal_values(splits[3], (W1, W1), (8 * W1) ** -0.5, 0.015625, ((0, 8), (1, 4)))
    inv_mid = normal_values(splits[4], (2, WM, WM), (8 * WM) ** -0.5, 0.0234375, ((1, 8), (2, 4)))
    inv_low = normal_values(splits[5], (4, WL, WL), (8 * WL) ** -0.5, 0.0234375, ((1, 8), (2, 4)))
    sep_tile_keys = jax.random.split(jax.random.fold_in(splits[6], 1), NBLK // NBLK)
    sep_tile_turns = jax.random.permutation(jax.random.fold_in(splits[6], 3), NBLK // NBLK)
    sep_tile = jax.vmap(lambda own, number: assign_block(jax.random.fold_in(splits[6], 2), own, number, NBLK, N_WIDE * N_NARROW, 1, MOSTB, 2))(sep_tile_keys, sep_tile_turns).reshape((NBLK, 1))
    sep_cell = draw_sep_cell(jax.random.fold_in(splits[8], 71), 0)
    return dict(solution=solution, source_term=source_term, permittivity=permittivity, inv_top=inv_top, inv_mid=inv_mid, inv_low=inv_low, sep_tile=sep_tile, sep_cell=sep_cell)


OMEGA_SQ = 0.5


def window(grid_field, starts):
    extent = grid_field.shape
    return grid_field[..., starts[0]:extent[-3] - 1 + starts[0], starts[1]:extent[-2] - 1 + starts[1], starts[2]:extent[-1] - 1 + starts[2]]


def forward(grid_field, along):
    starts = [0, 0, 0]
    starts[along] = 1
    return window(grid_field, starts) - window(grid_field, [0, 0, 0])


def backward(grid_field, along):
    starts = [1, 1, 1]
    starts[along] = 0
    return window(grid_field, [1, 1, 1]) - window(grid_field, starts)


def curl_curl(padded, dielectric):
    elec_x = padded[..., 0, :, :, :]
    elec_y = padded[..., 1, :, :, :]
    elec_z = padded[..., 2, :, :, :]
    magnet_x = forward(elec_z, 1) - forward(elec_y, 2)
    magnet_y = forward(elec_x, 2) - forward(elec_z, 0)
    magnet_z = forward(elec_y, 0) - forward(elec_x, 1)
    curl_x = backward(magnet_z, 1) - backward(magnet_y, 2)
    curl_y = backward(magnet_x, 2) - backward(magnet_z, 0)
    curl_z = backward(magnet_y, 0) - backward(magnet_x, 1)
    curls = jnp.stack([curl_x, curl_y, curl_z], axis=-4)
    interior = padded[..., 1:-1, 1:-1, 1:-1]
    return curls - OMEGA_SQ * dielectric * interior


def front_apply(rhs_piece, inverse):
    return lax.dot_general(rhs_piece, inverse, (((1,), (1,)), ((), ())), preferred_element_type=jnp.float32)


def reference(solution, source_term, permittivity, inv_top, inv_mid, inv_low, sep_tile, sep_cell):
    dielectric = permittivity.astype(jnp.float32)

    def apply_source(one_source):
        padded = jnp.pad(one_source, ((0, 0), (1, 1), (1, 1), (1, 1)))
        return curl_curl(padded, dielectric)

    def residual_of(field_now):
        return source_term - lax.map(apply_source, field_now)

    residual = residual_of(solution)
    block_tile = sep_tile[:, 0][:, None]
    tile_wide = block_tile // N_NARROW
    tile_narrow = block_tile % N_NARROW
    cell_count = CX * CY * CZ
    component = sep_cell // cell_count
    remainder = sep_cell % cell_count
    pos_i = remainder // (CY * CZ)
    pos_j = (remainder // CZ) % CY
    pos_k = remainder % CZ
    glob_x = tile_wide * CX + pos_i
    glob_y = tile_narrow * CY + pos_j
    picked = residual[:, component, glob_x, glob_y, pos_k]
    rhs_all = picked.reshape(NSRC, SEP).astype(jnp.bfloat16)
    pieces = [front_apply(rhs_all[:, :W1], inv_top)]
    for front_idx in range(2):
        start_at = W1 + front_idx * WM
        pieces.append(front_apply(rhs_all[:, start_at:start_at + WM], inv_mid[front_idx]))
    for front_idx in range(4):
        start_at = W1 + 2 * WM + front_idx * WL
        pieces.append(front_apply(rhs_all[:, start_at:start_at + WL], inv_low[front_idx]))
    update = jnp.concatenate(pieces, axis=1).reshape(NSRC, NBLK, BLK)
    new_solution = solution.at[:, component, glob_x, glob_y, pos_k].add(update)
    new_residual = residual_of(new_solution)
    return new_solution, new_residual
```

```python
import functools

import jax
import jax.numpy as jnp
import numpy as np
from jax import lax
from jax.experimental import pallas as pl
from jax.experimental.pallas import tpu as pltpu
from jax.sharding import PartitionSpec as P

OMEGA_SQ = 0.5
MIB = 1 << 20

NEAR = ((0, 0), (1, 0), (-1, 0), (0, 1), (0, -1), (-1, 1), (1, -1))


def iota(shape, dim):
    return lax.broadcasted_iota(jnp.int32, shape, dim)


def ahead(x, axis, edge=0.0):
    n = x.shape[axis]
    return jnp.where(iota(x.shape, axis) == n - 1, edge, pltpu.roll(x, n - 1, axis))


def behind(x, axis, edge):
    return jnp.where(iota(x.shape, axis) == 0, edge, pltpu.roll(x, 1, axis))


def faces_kernel(first_ref, last_ref, low_ref, high_ref, xp_ref, xm_ref, yp_ref, ym_ref, d1_ref, d2_ref):
    ex, ey, ez = last_ref[0, 0, 0], last_ref[0, 1, 0], last_ref[0, 2, 0]
    xp_ref[0, 0] = (ey + (ahead(ex, 0) - ex)).astype(xp_ref.dtype)
    xp_ref[0, 1] = (ez + (ahead(ex, 1) - ex)).astype(xp_ref.dtype)
    xm_ref[0, 0] = first_ref[0, 1, 0].astype(xm_ref.dtype)
    xm_ref[0, 1] = first_ref[0, 2, 0].astype(xm_ref.dtype)
    rows = high_ref.shape[3]
    hx, hy, hz = (high_ref[0, c, :, rows - 1, :] for c in range(3))
    yp_ref[0, 0] = (hx + (ahead(hy, 0) - hy)).astype(yp_ref.dtype)
    yp_ref[0, 1] = (hz + (ahead(hy, 1) - hy)).astype(yp_ref.dtype)
    lx, lz = low_ref[0, 0, :, 0, :], low_ref[0, 2, :, 0, :]
    ym_ref[0, 0] = lx.astype(ym_ref.dtype)
    ym_ref[0, 1] = lz.astype(ym_ref.dtype)
    d1_ref[0] = lx[lx.shape[0] - 1 :].astype(d1_ref.dtype)
    d2_ref[0] = hy[:1].astype(d2_ref.dtype)


def faces(field):
    ns, _, cx, cy, cz = field.shape
    half = jnp.bfloat16
    plane, slab = (1, 3, 1, cy, cz), (1, 3, cx, 8, cz)
    wide, narrow, line = (ns, 2, cy, cz), (ns, 2, cx, cz), (ns, 1, cz)
    return pl.pallas_call(
        faces_kernel,
        grid=(ns,),
        in_specs=[
            pl.BlockSpec(plane, lambda s: (s, 0, 0, 0, 0)),
            pl.BlockSpec(plane, lambda s: (s, 0, cx - 1, 0, 0)),
            pl.BlockSpec(slab, lambda s: (s, 0, 0, 0, 0)),
            pl.BlockSpec(slab, lambda s: (s, 0, 0, cy // 8 - 1, 0)),
        ],
        out_specs=[
            pl.BlockSpec((1, 2, cy, cz), lambda s: (s, 0, 0, 0)),
            pl.BlockSpec((1, 2, cy, cz), lambda s: (s, 0, 0, 0)),
            pl.BlockSpec((1, 2, cx, cz), lambda s: (s, 0, 0, 0)),
            pl.BlockSpec((1, 2, cx, cz), lambda s: (s, 0, 0, 0)),
            pl.BlockSpec((1, 1, cz), lambda s: (s, 0, 0)),
            pl.BlockSpec((1, 1, cz), lambda s: (s, 0, 0)),
        ],
        out_shape=[jax.ShapeDtypeStruct(shape, half) for shape in (wide, wide, narrow, narrow, line, line)],
        name="faces",
    )(field, field, field, field)


def curl_plane(own, beyond, back_z, back_y, y_row_x, y_row_z, y_edge_z, y_edge_x):
    ex, ey, ez = own
    hx = (ahead(ez, 0, y_row_z) - ez) - (ahead(ey, 1) - ey)
    hy = (ahead(ex, 1) - ex) - (beyond[1] - ez)
    hz = (beyond[0] - ey) - (ahead(ex, 0, y_row_x) - ex)
    cx = (hz - behind(hz, 0, y_edge_z)) - (hy - behind(hy, 1, ex))
    cy = (hx - behind(hx, 1, -ey)) - (hz - back_z)
    cz = (hy - back_y) - (hx - behind(hx, 0, y_edge_x))
    return cx, cy, cz, hz, hy


def gather_kernel(
    count_ref, sol_ref, next_ref, src_ref, perm_ref, xm_ref, xp_ref, ym_ref, yp_ref, d1_ref, d2_ref, line_ref, depth_ref,
    res_ref, out_ref, lines, turned, back_z, back_y,
):
    i = pl.program_id(0)
    planes = pl.num_programs(0)
    last = i == planes - 1
    ns, _, _, cy, cz = sol_ref.shape
    scaled = OMEGA_SQ * perm_ref[0].astype(jnp.float32)
    f32 = jnp.float32
    row = iota((cy, cz), 0)
    for s in range(ns):
        own = [sol_ref[s, c, 0] for c in range(3)]

        @pl.when(i == 0)
        def _():
            corner = jnp.where(row == cy - 1, d1_ref[s].astype(f32), 0.0)
            back_z[s] = own[1] - (xm_ref[s, 0].astype(f32) + corner)
            back_y[s] = xm_ref[s, 1].astype(f32) - own[2]

        beyond = [jnp.where(last, xp_ref[s, c].astype(f32), next_ref[s, c + 1, 0]) for c in range(2)]
        y_row_x = yp_ref[s, 0, pl.ds(i, 1), :]
        y_row_z = yp_ref[s, 1, pl.ds(i, 1), :]
        edge = ym_ref[s, 0, pl.ds(i, 1), :] + jnp.where(last, d2_ref[s].astype(f32), 0.0)
        curls = curl_plane(
            own, beyond, back_z[s], back_y[s], y_row_x, y_row_z, edge - own[0], own[2] - ym_ref[s, 1, pl.ds(i, 1), :]
        )
        for c in range(3):
            value = src_ref[s, c, 0] - (curls[c] - scaled * own[c])
            res_ref[s, c, 0] = value
            first = pl.multiple_of(c * planes * cy + i * cy, 16)
            lines[pl.ds(first, cy), s * cz : (s + 1) * cz] = value.astype(jnp.bfloat16)
        back_z[s], back_y[s] = curls[3], curls[4]

    @pl.when(last)
    def _():
        out_ref[...] = jnp.zeros_like(out_ref)
        total = lines.shape[0]
        for a in range(total // 128):
            for b in range(ns * cz // 128):
                turned[b * 128 : (b + 1) * 128, a * 128 : (a + 1) * 128] = lines[
                    a * 128 : (a + 1) * 128, b * 128 : (b + 1) * 128
                ].T

        @pl.loop(0, (count_ref[0] + 1) // 2)
        def _(p):
            hot = (iota((total, 256), 0) == line_ref[pl.ds(p, 1), :]).astype(f32).astype(jnp.bfloat16)
            got = jnp.dot(turned[...], hot, preferred_element_type=f32)
            at = iota((cz, 256), 0) == depth_ref[pl.ds(p, 1), :]
            sums = [
                jnp.sum(jnp.where(at, got[s * cz : (s + 1) * cz], 0.0), axis=0, keepdims=True) for s in range(ns)
            ]
            for h in range(2):
                for s in range(ns):
                    out_ref[p, h : h + 1, s * 128 : (s + 1) * 128] = sums[s][:, h * 128 : (h + 1) * 128]


def residual_and_gather(field, source, permittivity, halos, counts, line, depth):
    ns, _, cx, cy, cz = field.shape
    total = 3 * cx * cy
    pairs = line.shape[0]
    plane = (ns, 3, 1, cy, cz)
    whole = lambda x: pl.BlockSpec(x.shape, lambda i, *_: (0,) * x.ndim)
    halos = [h if n in (0, 1) else h.astype(jnp.float32) for n, h in enumerate(halos)]
    grid_spec = pltpu.PrefetchScalarGridSpec(
        num_scalar_prefetch=1,
        grid=(cx,),
        in_specs=[
            pl.BlockSpec(plane, lambda i, *_: (0, 0, i, 0, 0)),
            pl.BlockSpec(plane, lambda i, *_: (0, 0, jnp.minimum(i + 1, cx - 1), 0, 0)),
            pl.BlockSpec(plane, lambda i, *_: (0, 0, i, 0, 0)),
            pl.BlockSpec((1, cy, cz), lambda i, *_: (i, 0, 0)),
            *[whole(h) for h in halos],
            whole(line),
            whole(depth),
        ],
        out_specs=[
            pl.BlockSpec(plane, lambda i, *_: (0, 0, i, 0, 0)),
            pl.BlockSpec((pairs, 2, ns * 128), lambda i, *_: (0, 0, 0)),
        ],
        scratch_shapes=[
            pltpu.VMEM((total, ns * cz), jnp.bfloat16),
            pltpu.VMEM((ns * cz, total), jnp.bfloat16),
            pltpu.VMEM((ns, cy, cz), jnp.float32),
            pltpu.VMEM((ns, cy, cz), jnp.float32),
        ],
    )
    return pl.pallas_call(
        gather_kernel,
        grid_spec=grid_spec,
        out_shape=[
            jax.ShapeDtypeStruct(field.shape, jnp.float32),
            jax.ShapeDtypeStruct((pairs, 2, ns * 128), jnp.float32),
        ],
        compiler_params=pltpu.CompilerParams(vmem_limit_bytes=40 * MIB),
        name="residual_gather",
    )(counts, field, field, source, permittivity, *halos, line, depth)


def fronts_kernel(steps, x_top, x_mid, x_low, top_ref, mid_ref, low_ref, y_ref):
    g = pl.program_id(0)
    starts = (0, steps[0], steps[0] + steps[1])
    base = 0
    for start, count, x_ref, w_ref in zip(starts, steps, (x_top, x_mid, x_low), (top_ref, mid_ref, low_ref), strict=True):
        rows = w_ref.shape[1]

        @pl.when(jnp.logical_and(g >= start, g < start + count))
        def _(start=start, rows=rows, base=base, x_ref=x_ref, w_ref=w_ref):
            at = pl.multiple_of(base + (g - start) * rows, 128)
            y_ref[:, pl.ds(at, rows)] = lax.dot_general(
                x_ref[0], w_ref[0], (((1,), (1,)), ((), ())), preferred_element_type=jnp.float32
            )

        base += count * rows


def fronts(parts, inverses):
    sources = parts[0].shape[1]
    rows = []
    for inv in inverses:
        step = inv.shape[1]
        while step > 256 and step * inv.shape[2] * 2 > 2 * MIB:
            step //= 2
        rows.append(step)
    per = [inv.shape[1] // step for inv, step in zip(inverses, rows, strict=True)]
    steps = [inv.shape[0] * p for inv, p in zip(inverses, per, strict=True)]
    starts = [0, steps[0], steps[0] + steps[1]]
    height = sum(inv.shape[0] * inv.shape[1] for inv in inverses)

    def local(n, g):
        return jnp.clip(g - starts[n], 0, steps[n] - 1)

    x_specs = [
        pl.BlockSpec((1,) + x.shape[1:], functools.partial(lambda g, n: (local(n, g) // per[n], 0, 0), n=n))
        for n, x in enumerate(parts)
    ]
    w_specs = [
        pl.BlockSpec(
            (1, rows[n], inv.shape[2]),
            functools.partial(lambda g, n: (local(n, g) // per[n], local(n, g) % per[n], 0), n=n),
        )
        for n, inv in enumerate(inverses)
    ]
    entries = sum(inv.size for inv in inverses)
    return pl.pallas_call(
        functools.partial(fronts_kernel, tuple(steps)),
        grid=(sum(steps),),
        in_specs=[*x_specs, *w_specs],
        out_specs=pl.BlockSpec((sources, height), lambda g: (0, 0)),
        out_shape=jax.ShapeDtypeStruct((sources, height), jnp.float32),
        compiler_params=pltpu.CompilerParams(vmem_limit_bytes=40 * MIB),
        cost_estimate=pl.CostEstimate(flops=4 * entries, bytes_accessed=2 * entries, transcendentals=0),
        name="fronts",
    )(*parts, *inverses)


def correct_kernel(
    count_ref, sol_ref, res_ref, perm_ref, line_ref, depth_ref, value_ref,
    out_ref, new_ref, delta, x_halo, y_halo, back_z, back_y,
):
    i = pl.program_id(0)
    planes = pl.num_programs(0)
    last = i == planes - 1
    ns, _, _, cy, cz = sol_ref.shape
    pairs = line_ref.shape[0] // len(NEAR)
    f32 = jnp.float32

    @pl.when(i == 0)
    def _():
        delta[...] = jnp.zeros_like(delta)
        x_halo[...] = jnp.zeros_like(x_halo)
        y_halo[...] = jnp.zeros_like(y_halo)
        place = (
            (delta, 0, delta.shape[0]),
            (x_halo, 0, 2 * cy),
            (x_halo, 2 * cy, 3 * cy),
            *[(y_halo, 0, y_halo.shape[0])] * 4,
        )
        for q, (target, first, height) in enumerate(place):

            @pl.loop(0, (count_ref[q] + 1) // 2)
            def _(p, q=q, target=target, first=first, height=height):
                slot = q * pairs + p
                hot = (iota((height, 256), 0) == line_ref[pl.ds(slot, 1), :]).astype(f32).astype(jnp.bfloat16)
                at = iota((cz, 256), 0) == depth_ref[pl.ds(slot, 1), :]
                pair = [value_ref[pl.ds(2 * slot + h, 1), :] for h in range(2)]
                spread = jnp.concatenate(
                    [
                        jnp.where(
                            at, jnp.concatenate([v[:, s * 128 : (s + 1) * 128] for v in pair], axis=1), 0.0
                        ).astype(jnp.bfloat16)
                        for s in range(ns)
                    ],
                    axis=0,
                )
                target[first : first + height, :] += lax.dot_general(
                    hot, spread, (((1,), (1,)), ((), ())), preferred_element_type=f32
                )

    scaled = OMEGA_SQ * perm_ref[0].astype(f32)
    for s in range(ns):
        lanes = slice(s * cz, (s + 1) * cz)

        def plane(c, at, lanes=lanes):
            return delta[pl.ds(pl.multiple_of(c * planes * cy + at * cy, 8), cy), lanes]

        own = [plane(c, i) for c in range(3)]

        @pl.when(i == 0)
        def _(own=own, lanes=lanes, s=s):
            ex, ey, ez = (x_halo[(2 + c) * cy : (3 + c) * cy, lanes] for c in range(3))
            corner = y_halo[5 * planes : 5 * planes + 1, lanes]
            back_z[s] = own[1] - (ey + (ahead(ex, 0, corner) - ex))
            back_y[s] = (ez + (ahead(ex, 1) - ex)) - own[2]

        after = jnp.minimum(i + 1, planes - 1)
        beyond = [jnp.where(last, x_halo[c * cy : (c + 1) * cy, lanes], plane(c + 1, after)) for c in range(2)]
        y_row_x = y_halo[pl.ds(i, 1), lanes]
        y_row_z = y_halo[pl.ds(planes + i, 1), lanes]
        hx, hy, hz = (y_halo[pl.ds((2 + c) * planes + i, 1), lanes] for c in range(3))
        hy_after = jnp.where(
            last, y_halo[5 * planes + 1 : 5 * planes + 2, lanes], y_halo[pl.ds(3 * planes + after, 1), lanes]
        )
        curls = curl_plane(
            own,
            beyond,
            back_z[s],
            back_y[s],
            y_row_x,
            y_row_z,
            (hx + (hy_after - hy)) - own[0],
            own[2] - (hz + (ahead(hy, 1) - hy)),
        )
        for c in range(3):
            out_ref[s, c, 0] = sol_ref[s, c, 0] + own[c]
            new_ref[s, c, 0] = res_ref[s, c, 0] - (curls[c] - scaled * own[c])
        back_z[s], back_y[s] = curls[3], curls[4]


def correct(field, residual, permittivity, counts, line, depth, values):
    ns, _, cx, cy, cz = field.shape
    plane = pl.BlockSpec((ns, 3, 1, cy, cz), lambda i, *_: (0, 0, i, 0, 0))
    whole = lambda x: pl.BlockSpec(x.shape, lambda i, *_: (0,) * x.ndim)
    y_lines = -(-(5 * cx + 2) // 16) * 16
    grid_spec = pltpu.PrefetchScalarGridSpec(
        num_scalar_prefetch=1,
        grid=(cx,),
        in_specs=[
            plane,
            plane,
            pl.BlockSpec((1, cy, cz), lambda i, *_: (i, 0, 0)),
            whole(line),
            whole(depth),
            whole(values),
        ],
        out_specs=[plane, plane],
        scratch_shapes=[
            pltpu.VMEM((3 * cx * cy, ns * cz), jnp.float32),
            pltpu.VMEM((5 * cy, ns * cz), jnp.float32),
            pltpu.VMEM((y_lines, ns * cz), jnp.float32),
            pltpu.VMEM((ns, cy, cz), jnp.float32),
            pltpu.VMEM((ns, cy, cz), jnp.float32),
        ],
    )
    return pl.pallas_call(
        correct_kernel,
        grid_spec=grid_spec,
        out_shape=[jax.ShapeDtypeStruct(field.shape, jnp.float32)] * 2,
        compiler_params=pltpu.CompilerParams(vmem_limit_bytes=40 * MIB),
        name="correct",
    )(counts, field, residual, permittivity, line, depth, values)


def block_rows_of(inverses, wide_count, block_rows):
    per_device = sum(inv.shape[0] * inv.shape[1] for inv in inverses) // block_rows
    table, base = [], 0
    for inv in inverses:
        per = inv.shape[1] // block_rows
        for f in range(inv.shape[0]):
            b = np.arange(per * wide_count)
            table.append(b // per * per_device + base + f * per + b % per)
        base += inv.shape[0] * per
    return np.concatenate(table).astype(np.int32)


def block_columns_of(inverses, narrow_count, block_rows):
    table, base = [], 0
    for inv in inverses:
        per = inv.shape[2] // block_rows
        for _ in range(inv.shape[0]):
            table.append(base + np.arange(per * narrow_count).reshape(narrow_count, per))
            base += per * narrow_count
    return np.concatenate(table, axis=1).astype(np.int32)


def to_all_wide(block, wide_count):
    spread = jnp.broadcast_to(block[None], (wide_count, *block.shape)).reshape(-1, *block.shape[1:])
    return lax.all_to_all(spread, "wide", 0, 0, tiled=True)


def on_device(solution, source_term, permittivity, inv_top, inv_mid, inv_low, sep_tile, sep_cell):
    wide_count, narrow_count = lax.axis_size("wide"), lax.axis_size("narrow")
    my_wide, my_narrow = lax.axis_index("wide"), lax.axis_index("narrow")
    ns, _, cx, cy, cz = solution.shape
    block_count, block_rows = sep_cell.shape
    capacity = max(2, 2 * block_count // (wide_count * narrow_count))
    inverses = (inv_top[None], inv_mid, inv_low)

    xp, xm, yp, ym, d1, d2 = faces(solution)
    up_wide = [(w, w + 1) for w in range(wide_count - 1)]
    up_narrow = [(n, n + 1) for n in range(narrow_count - 1)]
    diagonal = [
        (w * narrow_count + n, (w + 1) * narrow_count + n - 1)
        for w in range(wide_count - 1)
        for n in range(1, narrow_count)
    ]
    flip = lambda pairs: [(b, a) for a, b in pairs]
    halos = (
        lax.ppermute(xp, "wide", up_wide),
        lax.ppermute(xm, "wide", flip(up_wide)),
        lax.ppermute(yp, "narrow", up_narrow),
        lax.ppermute(ym, "narrow", flip(up_narrow)),
        lax.ppermute(d1, ("wide", "narrow"), diagonal),
        lax.ppermute(d2, ("wide", "narrow"), flip(diagonal)),
    )

    block_tile = sep_tile[:, 0]
    block_ids = jnp.arange(block_count, dtype=jnp.int32)
    slot_rank = jnp.sum(
        jnp.logical_and(
            block_tile[:, None] == block_tile[None, :], block_ids[None, :] < block_ids[:, None]
        ).astype(jnp.int32),
        axis=1,
    )
    offsets = np.array(NEAR, np.int32)
    near_wide, near_narrow = my_wide + offsets[:, 0], my_narrow + offsets[:, 1]
    inside = (near_wide >= 0) & (near_wide < wide_count) & (near_narrow >= 0) & (near_narrow < narrow_count)
    near_tile = jnp.where(inside, near_wide * narrow_count + near_narrow, -1)
    named = block_tile[None, :] == near_tile[:, None]
    counts = jnp.sum(named.astype(jnp.int32), axis=1)
    slots = jnp.arange(capacity, dtype=jnp.int32)
    match = jnp.logical_and(named[:, None, :], slot_rank[None, None, :] == slots[None, :, None])
    near_ids = jnp.sum(jnp.where(match, block_ids[None, None, :], 0), axis=2)
    found = slots[None, :] < counts[:, None]
    cells = jnp.take(sep_cell, near_ids.reshape(-1), axis=0).reshape(len(NEAR), capacity, block_rows)
    depth = cells % cz
    row = cells // cz
    part, at_i, at_j = row // (cx * cy), row // cy % cx, row % cy
    rule = (
        (row, row >= 0),
        ((part - 1) * cy + at_j, (part >= 1) & (at_i == 0)),
        (part * cy + at_j, at_i == cx - 1),
        (part // 2 * cx + at_i, (part != 1) & (at_j == 0)),
        ((2 + part) * cx + at_i, at_j == cy - 1),
        (jnp.full_like(row, 5 * cx), (part == 0) & (at_i == cx - 1) & (at_j == 0)),
        (jnp.full_like(row, 5 * cx + 1), (part == 1) & (at_i == 0) & (at_j == cy - 1)),
    )
    line = jnp.stack(
        [jnp.where(found[q, :, None] & keep[q], at[q], -1) for q, (at, keep) in enumerate(rule)]
    )
    line = line.reshape(-1, 2 * block_rows)
    depth = depth.reshape(-1, 2 * block_rows)
    own_pairs = capacity // 2

    residual, picked = residual_and_gather(
        solution, source_term, permittivity, halos, counts, line[:own_pairs], depth[:own_pairs]
    )
    picked = picked.reshape(capacity, ns * block_rows).astype(jnp.bfloat16)
    row_tiles = lax.all_gather(picked, "narrow", axis=0, tiled=True)
    everyone = to_all_wide(row_tiles, wide_count)

    wanted = jnp.asarray(block_columns_of(inverses, narrow_count, block_rows))[my_narrow]
    columns = jnp.take(everyone, block_tile[wanted] * capacity + slot_rank[wanted], axis=0)
    columns = columns.reshape(-1, ns, block_rows).transpose(1, 0, 2).reshape(ns, -1)
    parts, base = [], 0
    for inv in inverses:
        width = inv.shape[0] * inv.shape[2]
        parts.append(columns[:, base : base + width].reshape(ns, inv.shape[0], -1).transpose(1, 0, 2))
        base += width
    partial = fronts(parts, inverses).astype(jnp.bfloat16)
    rows = partial.shape[1] // block_rows
    shares = lax.all_gather(partial.reshape(ns, rows, block_rows), "narrow", axis=0, tiled=False)
    summed = jnp.sum(shares.astype(jnp.float32), axis=0).astype(jnp.bfloat16)
    summed = summed.transpose(1, 0, 2).reshape(rows, ns * block_rows)
    updates = to_all_wide(summed, wide_count)

    place = jnp.asarray(block_rows_of(inverses, wide_count, block_rows))
    values = jnp.take(updates, place[near_ids.reshape(-1)], axis=0).astype(jnp.float32)
    return tuple(correct(solution, residual, permittivity, counts, line, depth, values))


def solution(mesh):
    return jax.shard_map(
        on_device,
        mesh=mesh,
        in_specs=(
            P(None, None, "wide", "narrow", None),
            P(None, None, "wide", "narrow", None),
            P("wide", "narrow", None),
            P("wide", "narrow"),
            P(None, "wide", "narrow"),
            P(None, "wide", "narrow"),
            P(),
            P(),
        ),
        out_specs=(P(None, None, "wide", "narrow", None), P(None, None, "wide", "narrow", None)),
        check_vma=False,
    )
```

```python
import functools

import jax
import jax.numpy as jnp
import numpy as np
from jax import lax
from jax.experimental import pallas as pl
from jax.experimental.pallas import tpu as pltpu
from jax.sharding import PartitionSpec as P

OMEGA_SQ = 0.5
MIB = 1 << 20

NEAR = ((0, 0), (1, 0), (-1, 0), (0, 1), (0, -1), (-1, 1), (1, -1))


def iota(shape, dim):
    return lax.broadcasted_iota(jnp.int32, shape, dim)


def ahead(x, axis, edge=0.0):
    n = x.shape[axis]
    return jnp.where(iota(x.shape, axis) == n - 1, edge, pltpu.roll(x, n - 1, axis))


def behind(x, axis, edge):
    return jnp.where(iota(x.shape, axis) == 0, edge, pltpu.roll(x, 1, axis))


def faces_kernel(first_ref, last_ref, low_ref, high_ref, xp_ref, xm_ref, yp_ref, ym_ref, d1_ref, d2_ref):
    ex, ey, ez = last_ref[0, 0, 0], last_ref[0, 1, 0], last_ref[0, 2, 0]
    xp_ref[0, 0] = (ey + (ahead(ex, 0) - ex)).astype(xp_ref.dtype)
    xp_ref[0, 1] = (ez + (ahead(ex, 1) - ex)).astype(xp_ref.dtype)
    xm_ref[0, 0] = first_ref[0, 1, 0].astype(xm_ref.dtype)
    xm_ref[0, 1] = first_ref[0, 2, 0].astype(xm_ref.dtype)
    rows = high_ref.shape[3]
    hx, hy, hz = (high_ref[0, c, :, rows - 1, :] for c in range(3))
    yp_ref[0, 0] = (hx + (ahead(hy, 0) - hy)).astype(yp_ref.dtype)
    yp_ref[0, 1] = (hz + (ahead(hy, 1) - hy)).astype(yp_ref.dtype)
    lx, lz = low_ref[0, 0, :, 0, :], low_ref[0, 2, :, 0, :]
    ym_ref[0, 0] = lx.astype(ym_ref.dtype)
    ym_ref[0, 1] = lz.astype(ym_ref.dtype)
    d1_ref[0] = lx[lx.shape[0] - 1 :].astype(d1_ref.dtype)
    d2_ref[0] = hy[:1].astype(d2_ref.dtype)


def faces(field):
    ns, _, cx, cy, cz = field.shape
    half = jnp.bfloat16
    plane, slab = (1, 3, 1, cy, cz), (1, 3, cx, 8, cz)
    wide, narrow, line = (ns, 2, cy, cz), (ns, 2, cx, cz), (ns, 1, cz)
    return pl.pallas_call(
        faces_kernel,
        grid=(ns,),
        in_specs=[
            pl.BlockSpec(plane, lambda s: (s, 0, 0, 0, 0)),
            pl.BlockSpec(plane, lambda s: (s, 0, cx - 1, 0, 0)),
            pl.BlockSpec(slab, lambda s: (s, 0, 0, 0, 0)),
            pl.BlockSpec(slab, lambda s: (s, 0, 0, cy // 8 - 1, 0)),
        ],
        out_specs=[
            pl.BlockSpec((1, 2, cy, cz), lambda s: (s, 0, 0, 0)),
            pl.BlockSpec((1, 2, cy, cz), lambda s: (s, 0, 0, 0)),
            pl.BlockSpec((1, 2, cx, cz), lambda s: (s, 0, 0, 0)),
            pl.BlockSpec((1, 2, cx, cz), lambda s: (s, 0, 0, 0)),
            pl.BlockSpec((1, 1, cz), lambda s: (s, 0, 0)),
            pl.BlockSpec((1, 1, cz), lambda s: (s, 0, 0)),
        ],
        out_shape=[jax.ShapeDtypeStruct(shape, half) for shape in (wide, wide, narrow, narrow, line, line)],
        compiler_params=pltpu.CompilerParams(vmem_limit_bytes=60 * MIB),
        name="faces",
    )(field, field, field, field)


def curl_plane(own, beyond, back_z, back_y, y_row_x, y_row_z, y_edge_z, y_edge_x):
    ex, ey, ez = own
    hx = (ahead(ez, 0, y_row_z) - ez) - (ahead(ey, 1) - ey)
    hy = (ahead(ex, 1) - ex) - (beyond[1] - ez)
    hz = (beyond[0] - ey) - (ahead(ex, 0, y_row_x) - ex)
    cx = (hz - behind(hz, 0, y_edge_z)) - (hy - behind(hy, 1, ex))
    cy = (hx - behind(hx, 1, -ey)) - (hz - back_z)
    cz = (hy - back_y) - (hx - behind(hx, 0, y_edge_x))
    return cx, cy, cz, hz, hy


def gather_kernel(
    count_ref, sol_ref, next_ref, src_ref, perm_ref, xm_ref, xp_ref, ym_ref, yp_ref, d1_ref, d2_ref, line_ref, depth_ref,
    res_ref, out_ref, lines, turned, back_z, back_y, y_rows,
):
    i = pl.program_id(0)
    planes = pl.num_programs(0)
    last = i == planes - 1
    ns, _, _, cy, cz = sol_ref.shape

    @pl.when(i == 0)
    def _():
        for n, ref in enumerate((yp_ref, ym_ref)):
            for s in range(ns):
                for c in range(2):
                    y_rows[n, s, c] = ref[s, c].astype(jnp.float32)

    scaled = OMEGA_SQ * perm_ref[0].astype(jnp.float32)
    f32 = jnp.float32
    row = iota((cy, cz), 0)
    for s in range(ns):
        own = [sol_ref[s, c, 0] for c in range(3)]

        @pl.when(i == 0)
        def _():
            corner = jnp.where(row == cy - 1, d1_ref[s].astype(f32), 0.0)
            back_z[s] = own[1] - (xm_ref[s, 0].astype(f32) + corner)
            back_y[s] = xm_ref[s, 1].astype(f32) - own[2]

        beyond = [jnp.where(last, xp_ref[s, c].astype(f32), next_ref[s, c + 1, 0]) for c in range(2)]
        y_row_x, y_row_z = (y_rows[0, s, c, pl.ds(i, 1), :] for c in range(2))
        edge = y_rows[1, s, 0, pl.ds(i, 1), :] + jnp.where(last, d2_ref[s].astype(f32), 0.0)
        curls = curl_plane(
            own, beyond, back_z[s], back_y[s], y_row_x, y_row_z, edge - own[0], own[2] - y_rows[1, s, 1, pl.ds(i, 1), :]
        )
        for c in range(3):
            value = src_ref[s, c, 0] - (curls[c] - scaled * own[c])
            res_ref[s, c, 0] = value
            first = pl.multiple_of(c * planes * cy + i * cy, 16)
            lines[pl.ds(first, cy), s * cz : (s + 1) * cz] = value.astype(jnp.bfloat16)
        back_z[s], back_y[s] = curls[3], curls[4]

    @pl.when(last)
    def _():
        out_ref[...] = jnp.zeros_like(out_ref)
        total = lines.shape[0]
        for a in range(total // 128):
            for b in range(ns * cz // 128):
                turned[b * 128 : (b + 1) * 128, a * 128 : (a + 1) * 128] = lines[
                    a * 128 : (a + 1) * 128, b * 128 : (b + 1) * 128
                ].T

        group, width = out_ref.shape[1], line_ref.shape[1]

        @pl.loop(0, pl.cdiv(count_ref[0], group))
        def _(p):
            hot = (iota((total, width), 0) == line_ref[pl.ds(p, 1), :]).astype(f32).astype(jnp.bfloat16)
            got = jnp.dot(turned[...], hot, preferred_element_type=f32)
            at = iota((cz, width), 0) == depth_ref[pl.ds(p, 1), :]
            for s in range(ns):
                sums = jnp.sum(jnp.where(at, got[s * cz : (s + 1) * cz], 0.0), axis=0, keepdims=True)
                for h in range(group):
                    out_ref[p, h : h + 1, s * 128 : (s + 1) * 128] = sums[:, h * 128 : (h + 1) * 128]


def residual_and_gather(field, source, permittivity, halos, counts, line, depth):
    ns, _, cx, cy, cz = field.shape
    total = 3 * cx * cy
    groups, group = line.shape[0], line.shape[1] // 128
    plane = (ns, 3, 1, cy, cz)
    whole = lambda x: pl.BlockSpec(x.shape, lambda i, *_: (0,) * x.ndim)
    grid_spec = pltpu.PrefetchScalarGridSpec(
        num_scalar_prefetch=1,
        grid=(cx,),
        in_specs=[
            pl.BlockSpec(plane, lambda i, *_: (0, 0, i, 0, 0)),
            pl.BlockSpec(plane, lambda i, *_: (0, 0, jnp.minimum(i + 1, cx - 1), 0, 0)),
            pl.BlockSpec(plane, lambda i, *_: (0, 0, i, 0, 0)),
            pl.BlockSpec((1, cy, cz), lambda i, *_: (i, 0, 0)),
            *[whole(h) for h in halos],
            whole(line),
            whole(depth),
        ],
        out_specs=[
            pl.BlockSpec(plane, lambda i, *_: (0, 0, i, 0, 0)),
            pl.BlockSpec((groups, group, ns * 128), lambda i, *_: (0, 0, 0)),
        ],
        scratch_shapes=[
            pltpu.VMEM((total, ns * cz), jnp.bfloat16),
            pltpu.VMEM((ns * cz, total), jnp.bfloat16),
            pltpu.VMEM((ns, cy, cz), jnp.float32),
            pltpu.VMEM((ns, cy, cz), jnp.float32),
            pltpu.VMEM((2, ns, 2, cx, cz), jnp.float32),
        ],
    )
    return pl.pallas_call(
        gather_kernel,
        grid_spec=grid_spec,
        out_shape=[
            jax.ShapeDtypeStruct(field.shape, jnp.float32),
            jax.ShapeDtypeStruct((groups, group, ns * 128), jnp.float32),
        ],
        compiler_params=pltpu.CompilerParams(vmem_limit_bytes=60 * MIB),
        name="residual_gather",
    )(counts, field, field, source, permittivity, *halos, line, depth)


def fronts_kernel(x_top, x_mid, x_low, top_ref, mid_ref, low_ref, y_ref, top_buf, mid_buf, low_buf, sem):
    jobs, base = [], 0
    for x_ref, w_ref, buf in ((x_top, top_ref, top_buf), (x_mid, mid_ref, mid_buf), (x_low, low_ref, low_buf)):
        count, height, width = w_ref.shape
        rows = height
        while rows > 256 and rows * width * 2 > 4 * MIB:
            rows //= 2
        for f in range(count):
            for r in range(0, height, rows):
                at = pl.ds(r, rows)
                copy = pltpu.make_async_copy(w_ref.at[f, at], buf.at[f, at], sem.at[len(jobs)])
                jobs.append((copy, x_ref, buf, f, at, pl.ds(base + r, rows)))
            base += height
    for job in jobs:
        job[0].start()
    for copy, x_ref, buf, f, at, out in jobs:
        copy.wait()
        y_ref[:, out] = lax.dot_general(
            x_ref[f], buf[f, at], (((1,), (1,)), ((), ())), preferred_element_type=jnp.float32
        )


def fronts(parts, inverses):
    sources = parts[0].shape[1]
    height = sum(inv.shape[0] * inv.shape[1] for inv in inverses)
    entries = sum(inv.size for inv in inverses)
    here, there = pl.BlockSpec(memory_space=pltpu.VMEM), pl.BlockSpec(memory_space=pl.ANY)
    return pl.pallas_call(
        fronts_kernel,
        in_specs=[here] * 3 + [there] * 3,
        out_specs=here,
        out_shape=jax.ShapeDtypeStruct((sources, height), jnp.float32),
        scratch_shapes=[pltpu.VMEM(inv.shape, inv.dtype) for inv in inverses] + [pltpu.SemaphoreType.DMA((64,))],
        compiler_params=pltpu.CompilerParams(vmem_limit_bytes=60 * MIB),
        cost_estimate=pl.CostEstimate(flops=4 * entries, bytes_accessed=2 * entries, transcendentals=0),
        name="fronts",
    )(*parts, *inverses)


def correct_kernel(
    count_ref, sol_ref, res_ref, perm_ref, own_line_ref, own_depth_ref, line_ref, depth_ref, value_ref,
    out_ref, new_ref, delta, x_halo, y_halo, back_z, back_y,
):
    i = pl.program_id(0)
    planes = pl.num_programs(0)
    last = i == planes - 1
    ns, _, _, cy, cz = sol_ref.shape
    f32, half = jnp.float32, jnp.bfloat16
    capacity = value_ref.shape[0] // len(NEAR)

    def values_of(first, count):
        rows = [value_ref[pl.ds(first + h, 1), :] for h in range(count)]
        return [jnp.concatenate([v[:, s * 128 : (s + 1) * 128] for v in rows], axis=1) for s in range(ns)]

    def times(a, b):
        return lax.dot_general(a, b, (((1,), (1,)), ((), ())), preferred_element_type=f32)

    @pl.when(i == 0)
    def _():
        delta[...] = jnp.zeros_like(delta)
        x_halo[...] = jnp.zeros_like(x_halo)
        y_halo[...] = jnp.zeros_like(y_halo)
        own_width = own_line_ref.shape[1]
        own_group = own_width // 128

        @pl.loop(0, pl.cdiv(count_ref[0], own_group))
        def _(p):
            values = values_of(p * own_group, own_group)
            hot = (iota((delta.shape[0], own_width), 0) == own_line_ref[pl.ds(p, 1), :]).astype(f32).astype(half)
            at = iota((cz, own_width), 0) == own_depth_ref[pl.ds(p, 1), :]
            delta[...] += times(hot, jnp.concatenate([jnp.where(at, v, 0.0).astype(half) for v in values], axis=0))

        width = line_ref.shape[1]
        group = width // 128
        y_lines = y_halo.shape[1]
        place = ((x_halo, 0, 2 * cy), (x_halo, 2 * cy, 3 * cy), *[(y_halo, 0, y_lines)] * 4)
        for q, (target, first, height) in enumerate(place):

            @pl.loop(0, pl.cdiv(count_ref[q + 1], group))
            def _(p, q=q, target=target, first=first, height=height):
                row = q * (capacity // group) + p
                values = values_of((q + 1) * capacity + p * group, group)
                at = iota((height, width), 0) == line_ref[pl.ds(row, 1), :]
                hot = (iota((cz, width), 0) == depth_ref[pl.ds(row, 1), :]).astype(f32).astype(half)
                got = times(jnp.concatenate([jnp.where(at, v, 0.0).astype(half) for v in values], axis=0), hot)
                for s in range(ns):
                    target[s, first : first + height] += got[s * height : (s + 1) * height]

    scaled = OMEGA_SQ * perm_ref[0].astype(f32)
    for s in range(ns):
        lanes = slice(s * cz, (s + 1) * cz)

        def plane(c, at, lanes=lanes):
            return delta[pl.ds(pl.multiple_of(c * planes * cy + at * cy, 8), cy), lanes]

        own = [plane(c, i) for c in range(3)]

        @pl.when(i == 0)
        def _(own=own, s=s):
            ex, ey, ez = (x_halo[s, (2 + c) * cy : (3 + c) * cy] for c in range(3))
            corner = y_halo[s, 5 * planes : 5 * planes + 1]
            back_z[s] = own[1] - (ey + (ahead(ex, 0, corner) - ex))
            back_y[s] = (ez + (ahead(ex, 1) - ex)) - own[2]

        after = jnp.minimum(i + 1, planes - 1)
        beyond = [jnp.where(last, x_halo[s, c * cy : (c + 1) * cy], plane(c + 1, after)) for c in range(2)]
        y_row_x = y_halo[s, pl.ds(i, 1), :]
        y_row_z = y_halo[s, pl.ds(planes + i, 1), :]
        hx, hy, hz = (y_halo[s, pl.ds((2 + c) * planes + i, 1), :] for c in range(3))
        hy_after = jnp.where(
            last, y_halo[s, 5 * planes + 1 : 5 * planes + 2], y_halo[s, pl.ds(3 * planes + after, 1), :]
        )
        curls = curl_plane(
            own,
            beyond,
            back_z[s],
            back_y[s],
            y_row_x,
            y_row_z,
            (hx + (hy_after - hy)) - own[0],
            own[2] - (hz + (ahead(hy, 1) - hy)),
        )
        for c in range(3):
            out_ref[s, c, 0] = sol_ref[s, c, 0] + own[c]
            new_ref[s, c, 0] = res_ref[s, c, 0] - (curls[c] - scaled * own[c])
        back_z[s], back_y[s] = curls[3], curls[4]


def correct(field, residual, permittivity, counts, own_line, own_depth, line, depth, values):
    ns, _, cx, cy, cz = field.shape
    plane = pl.BlockSpec((ns, 3, 1, cy, cz), lambda i, *_: (0, 0, i, 0, 0))
    whole = lambda x: pl.BlockSpec(x.shape, lambda i, *_: (0,) * x.ndim)
    y_lines = -(-(5 * cx + 2) // 16) * 16
    grid_spec = pltpu.PrefetchScalarGridSpec(
        num_scalar_prefetch=1,
        grid=(cx,),
        in_specs=[
            plane,
            plane,
            pl.BlockSpec((1, cy, cz), lambda i, *_: (i, 0, 0)),
            *[whole(x) for x in (own_line, own_depth, line, depth, values)],
        ],
        out_specs=[plane, plane],
        scratch_shapes=[
            pltpu.VMEM((3 * cx * cy, ns * cz), jnp.float32),
            pltpu.VMEM((ns, 5 * cy, cz), jnp.float32),
            pltpu.VMEM((ns, y_lines, cz), jnp.float32),
            pltpu.VMEM((ns, cy, cz), jnp.float32),
            pltpu.VMEM((ns, cy, cz), jnp.float32),
        ],
    )
    return pl.pallas_call(
        correct_kernel,
        grid_spec=grid_spec,
        out_shape=[jax.ShapeDtypeStruct(field.shape, jnp.float32)] * 2,
        compiler_params=pltpu.CompilerParams(vmem_limit_bytes=60 * MIB),
        name="correct",
    )(counts, field, residual, permittivity, own_line, own_depth, line, depth, values)


def block_rows_of(inverses, wide_count, block_rows):
    per_device = sum(inv.shape[0] * inv.shape[1] for inv in inverses) // block_rows
    table, base = [], 0
    for inv in inverses:
        per = inv.shape[1] // block_rows
        for f in range(inv.shape[0]):
            b = np.arange(per * wide_count)
            table.append(b // per * per_device + base + f * per + b % per)
        base += inv.shape[0] * per
    return np.concatenate(table).astype(np.int32)


def block_columns_of(inverses, narrow_count, block_rows):
    table, base = [], 0
    for inv in inverses:
        per = inv.shape[2] // block_rows
        for _ in range(inv.shape[0]):
            table.append(base + np.arange(per * narrow_count).reshape(narrow_count, per))
            base += per * narrow_count
    return np.concatenate(table, axis=1).astype(np.int32)


def to_all_wide(block, wide_count):
    spread = jnp.broadcast_to(block[None], (wide_count, *block.shape)).reshape(-1, *block.shape[1:])
    return lax.all_to_all(spread, "wide", 0, 0, tiled=True)


def on_device(solution, source_term, permittivity, inv_top, inv_mid, inv_low, sep_tile, sep_cell):
    wide_count, narrow_count = lax.axis_size("wide"), lax.axis_size("narrow")
    my_wide, my_narrow = lax.axis_index("wide"), lax.axis_index("narrow")
    ns, _, cx, cy, cz = solution.shape
    block_count, block_rows = sep_cell.shape
    capacity = max(2, 2 * block_count // (wide_count * narrow_count))
    inverses = (inv_top[None], inv_mid, inv_low)

    xp, xm, yp, ym, d1, d2 = faces(solution)
    up_wide = [(w, w + 1) for w in range(wide_count - 1)]
    up_narrow = [(n, n + 1) for n in range(narrow_count - 1)]
    diagonal = [
        (w * narrow_count + n, (w + 1) * narrow_count + n - 1)
        for w in range(wide_count - 1)
        for n in range(1, narrow_count)
    ]
    flip = lambda pairs: [(b, a) for a, b in pairs]
    from_xm, from_xp = lax.ppermute(xp, "wide", up_wide), lax.ppermute(xm, "wide", flip(up_wide))
    from_ym = lax.ppermute(yp, "narrow", up_narrow)
    from_d1 = lax.ppermute(d1, ("wide", "narrow"), diagonal)
    from_d2 = lax.ppermute(d2, ("wide", "narrow"), flip(diagonal))
    ym, from_d1 = lax.optimization_barrier((ym, from_d1))
    halos = (from_xm, from_xp, from_ym, lax.ppermute(ym, "narrow", flip(up_narrow)), from_d1, from_d2)

    block_tile = sep_tile[:, 0]
    block_ids = jnp.arange(block_count, dtype=jnp.int32)
    slot_rank = jnp.sum(
        jnp.logical_and(
            block_tile[:, None] == block_tile[None, :], block_ids[None, :] < block_ids[:, None]
        ).astype(jnp.int32),
        axis=1,
    )
    offsets = np.array(NEAR, np.int32)
    near_wide, near_narrow = my_wide + offsets[:, 0], my_narrow + offsets[:, 1]
    inside = (near_wide >= 0) & (near_wide < wide_count) & (near_narrow >= 0) & (near_narrow < narrow_count)
    near_tile = jnp.where(inside, near_wide * narrow_count + near_narrow, -1)
    named = block_tile[None, :] == near_tile[:, None]
    counts = jnp.sum(named.astype(jnp.int32), axis=1)
    slots = jnp.arange(capacity, dtype=jnp.int32)
    match = jnp.logical_and(named[:, None, :], slot_rank[None, None, :] == slots[None, :, None])
    near_ids = jnp.sum(jnp.where(match, block_ids[None, None, :], 0), axis=2)
    near_rows = jnp.sum(
        jnp.where(match, block_rows_of(inverses, wide_count, block_rows)[None, None, :], 0), axis=2
    )
    found = slots[None, :] < counts[:, None]
    cells = jnp.take(sep_cell, near_ids.reshape(-1), axis=0).reshape(len(NEAR), capacity, block_rows)
    depth = cells % cz
    row = cells // cz
    part, at_i, at_j = row // (cx * cy), row // cy % cx, row % cy
    rule = (
        (row, row >= 0),
        ((part - 1) * cy + at_j, (part >= 1) & (at_i == 0)),
        (part * cy + at_j, at_i == cx - 1),
        (part // 2 * cx + at_i, (part != 1) & (at_j == 0)),
        ((2 + part) * cx + at_i, at_j == cy - 1),
        (jnp.full_like(row, 5 * cx), (part == 0) & (at_i == cx - 1) & (at_j == 0)),
        (jnp.full_like(row, 5 * cx + 1), (part == 1) & (at_i == 0) & (at_j == cy - 1)),
    )
    line = jnp.stack(
        [jnp.where(found[q, :, None] & keep[q], at[q], -1) for q, (at, keep) in enumerate(rule)]
    )
    arrives = (block_tile % narrow_count * wide_count + block_tile // narrow_count) * capacity + slot_rank
    table = block_columns_of(inverses, narrow_count, block_rows)
    held_at = jnp.sum(
        jnp.where(
            (table[:, :, None] == block_ids) & (np.arange(narrow_count)[:, None, None] == my_narrow), arrives, 0
        ),
        axis=(0, 2),
    )
    own_width, width = min(8, capacity) * block_rows, min(4, capacity) * block_rows
    own_line, own_depth = line[0].reshape(-1, own_width), depth[0].reshape(-1, own_width)
    line, depth = line[1:].reshape(-1, width), depth[1:].reshape(-1, width)

    residual, picked = residual_and_gather(
        solution, source_term, permittivity, halos, counts, own_line, own_depth
    )
    picked = picked.reshape(capacity, ns * block_rows).astype(jnp.bfloat16)
    everyone = lax.all_gather(to_all_wide(picked, wide_count), "narrow", axis=0, tiled=True)

    columns = jnp.take(everyone, held_at, axis=0)
    columns = columns.reshape(-1, ns, block_rows).transpose(1, 0, 2).reshape(ns, -1)
    parts, base = [], 0
    for inv in inverses:
        width = inv.shape[0] * inv.shape[2]
        parts.append(columns[:, base : base + width].reshape(ns, inv.shape[0], -1).transpose(1, 0, 2))
        base += width
    partial = fronts(parts, inverses).astype(jnp.bfloat16)
    rows = partial.shape[1] // block_rows
    shares = lax.all_gather(partial.reshape(ns, rows, block_rows), "narrow", axis=0, tiled=False)
    summed = jnp.sum(shares.astype(jnp.float32), axis=0).astype(jnp.bfloat16)
    summed = summed.transpose(1, 0, 2).reshape(rows, ns * block_rows)
    updates = to_all_wide(summed, wide_count)

    values = jnp.take(updates, near_rows.reshape(-1), axis=0).astype(jnp.float32)
    return tuple(correct(solution, residual, permittivity, counts, own_line, own_depth, line, depth, values))


def solution(mesh):
    return jax.shard_map(
        on_device,
        mesh=mesh,
        in_specs=(
            P(None, None, "wide", "narrow", None),
            P(None, None, "wide", "narrow", None),
            P("wide", "narrow", None),
            P("wide", "narrow"),
            P(None, "wide", "narrow"),
            P(None, "wide", "narrow"),
            P(),
            P(),
        ),
        out_specs=(P(None, None, "wide", "narrow", None), P(None, None, "wide", "narrow", None)),
        check_vma=False,
    )
```

```python
import jax
import jax.numpy as jnp
import numpy as np
from jax import lax
from jax.experimental import pallas as pl
from jax.experimental.pallas import tpu as pltpu
from jax.sharding import PartitionSpec as P

OMEGA_SQ = 0.5
MIB = 1 << 20

NEAR = ((0, 0), (1, 0), (-1, 0), (0, 1), (0, -1), (-1, 1), (1, -1))


def iota(shape, dim):
    return lax.broadcasted_iota(jnp.int32, shape, dim)


def lane_blocks(x):
    return [x[:, at : at + 128] for at in range(0, x.shape[1], 128)]


def shifted(x, axis, step, edge):
    if axis == 1:
        size, blocks = 128, lane_blocks(x)
        fill = lane_blocks(jnp.broadcast_to(edge, x.shape))
        turned = [pltpu.roll(b, step % size, 1) for b in blocks]
        mask = iota((1, size), 1)
    else:
        size, tiles = 8, x.shape[0] // 8
        turned = pltpu.roll(x.reshape(tiles, size, x.shape[1]), step % size, 1)
        turned = [turned[t] for t in range(tiles)]
        filled = jnp.broadcast_to(edge, (size, x.shape[1])) if jnp.ndim(edge) == 0 or edge.shape[0] == 1 else edge
        fill = [filled[:size]] * tiles
        mask = iota((size, 1), 0)
    if step < 0:
        others = [*turned[1:], fill[-1]]
        mask = mask == size - 1
    else:
        others = [fill[0], *turned[:-1]]
        mask = mask == 0
    return jnp.concatenate([jnp.where(mask, o, t) for o, t in zip(others, turned, strict=True)], axis=axis)


def ahead(x, axis, edge=0.0):
    return shifted(x, axis, -1, edge)


def behind(x, axis, edge):
    return shifted(x, axis, 1, edge)


def rows_kernel(low_ref, high_ref, out_ref):
    top = high_ref.shape[3] - 1
    rows = [low_ref[0, 0, :, 0, :], low_ref[0, 2, :, 0, :], *(high_ref[0, c, :, top, :] for c in range(3))]
    for n, row in enumerate(rows):
        out_ref[0, n] = row.astype(out_ref.dtype)


def outer_rows(field):
    ns, _, cx, cy, cz = field.shape
    slab = (1, 3, cx, 8, cz)
    return pl.pallas_call(
        rows_kernel,
        grid=(ns,),
        in_specs=[
            pl.BlockSpec(slab, lambda s: (s, 0, 0, 0, 0)),
            pl.BlockSpec(slab, lambda s: (s, 0, 0, cy // 8 - 1, 0)),
        ],
        out_specs=pl.BlockSpec((1, 5, cx, cz), lambda s: (s, 0, 0, 0)),
        out_shape=jax.ShapeDtypeStruct((ns, 5, cx, cz), jnp.bfloat16),
        compiler_params=pltpu.CompilerParams(vmem_limit_bytes=60 * MIB),
        name="outer_rows",
    )(field, field)


def near_row(near_ref, side, ref, n, i):
    row = ref[n].astype(jnp.float32)
    return jnp.where(near_ref[2 + side] > 0, row[i : i + 1], 0.0)


def planes_kernel(near_ref, first_ref, last_ref, prev_ref, next_ref, up_ref, down_ref):
    planes = prev_ref.shape[3]
    cy = first_ref.shape[3]
    dtype = up_ref.dtype
    ex, ey, ez = last_ref[0, 0, 0], last_ref[0, 1, 0], last_ref[0, 2, 0]
    past = near_row(near_ref, 1, next_ref.at[0, 0], 0, planes - 1)
    up_ref[0, :cy] = (ey + (ahead(ex, 0, past) - ex)).astype(dtype)
    up_ref[0, cy:] = (ez + (ahead(ex, 1) - ex)).astype(dtype)
    down_ref[0, :cy] = first_ref[0, 1, 0].astype(dtype)
    down_ref[0, cy : 2 * cy] = first_ref[0, 2, 0].astype(dtype)
    before = near_row(near_ref, 0, prev_ref.at[0, 0], 3, 0)
    down_ref[0, 2 * cy :] = jnp.broadcast_to(before, (down_ref.shape[1] - 2 * cy, before.shape[1])).astype(dtype)


def outer_planes(field, near, rows):
    ns, _, cx, cy, cz = field.shape
    plane = (1, 3, 1, cy, cz)
    grid_spec = pltpu.PrefetchScalarGridSpec(
        num_scalar_prefetch=1,
        grid=(ns,),
        in_specs=[
            pl.BlockSpec(plane, lambda s, _: (s, 0, 0, 0, 0)),
            pl.BlockSpec(plane, lambda s, _: (s, 0, cx - 1, 0, 0)),
            pl.BlockSpec((1, 1, 5, cx, cz), lambda s, near: (near[0], s, 0, 0, 0)),
            pl.BlockSpec((1, 1, 5, cx, cz), lambda s, near: (near[1], s, 0, 0, 0)),
        ],
        out_specs=[
            pl.BlockSpec((1, 2 * cy, cz), lambda s, _: (s, 0, 0)),
            pl.BlockSpec((1, 2 * cy + 16, cz), lambda s, _: (s, 0, 0)),
        ],
    )
    return pl.pallas_call(
        planes_kernel,
        grid_spec=grid_spec,
        out_shape=[
            jax.ShapeDtypeStruct((ns, 2 * cy, cz), jnp.bfloat16),
            jax.ShapeDtypeStruct((ns, 2 * cy + 16, cz), jnp.bfloat16),
        ],
        compiler_params=pltpu.CompilerParams(vmem_limit_bytes=60 * MIB),
        name="outer_planes",
    )(near, field, field, rows, rows)


def curl_plane(own, beyond, back_z, back_y, y_row_x, y_row_z, y_edge_z, y_edge_x):
    ex, ey, ez = own
    hx = (ahead(ez, 0, y_row_z) - ez) - (ahead(ey, 1) - ey)
    hy = (ahead(ex, 1) - ex) - (beyond[1] - ez)
    hz = (beyond[0] - ey) - (ahead(ex, 0, y_row_x) - ex)
    cx = (hz - behind(hz, 0, y_edge_z)) - (hy - behind(hy, 1, ex))
    cy = (hx - behind(hx, 1, -ey)) - (hz - back_z)
    cz = (hy - back_y) - (hx - behind(hx, 0, y_edge_x))
    return cx, cy, cz, hz, hy


def magnetic(own, beyond, row_x):
    ex, ey, ez = own
    return (beyond[0] - ey) - (ahead(ex, 0, row_x) - ex), (ahead(ex, 1) - ex) - (beyond[1] - ez)


def spread_rows(near_ref, prev_ref, next_ref, scratch):
    for s in range(scratch.shape[0]):
        for n in range(5):
            side, ref = (1, next_ref) if n < 2 else (0, prev_ref)
            scratch[s, n] = jnp.where(near_ref[2 + side] > 0, ref[0, s, n].astype(jnp.float32), 0.0)


def residual_plane(s, i, own, beyond, back, rows, after, planes, at, scaled, lines):
    cy, cz = own[0].shape
    cx = rows.shape[2]
    row_x, row_z, ex, ey, ez = (rows[s, n, pl.ds(i, 1), :] for n in range(5))
    curls = curl_plane(
        own, beyond, back[0], back[1], row_x, row_z, (ex + (after - ey)) - own[0], own[2] - (ez + (ahead(ey, 1) - ey))
    )
    for c in range(3):
        value = planes[s, c, at] - (curls[c] - scaled * own[c])
        planes[s, c, at] = value
        first = pl.multiple_of((c * cx + i) * cy, 16)
        lines[pl.ds(first, cy), s * cz : (s + 1) * cz] = value.astype(jnp.bfloat16)
    return curls[3], curls[4]


def inner_kernel(
    near_ref, sol_ref, src_ref, perm_ref, prev_ref, over_ref, res_ref, out_ref,
    field, planes, lines, back_z, back_y, rows, field_sem, plane_sem, res_sem, line_sem,
):
    ns, _, cx, cy, _ = field.shape

    def field_copy(i):
        return pltpu.make_async_copy(sol_ref.at[:, :, i], field.at[:, :, i], field_sem.at[i])

    def plane_copy(i):
        return pltpu.make_async_copy(src_ref.at[:, :, i], planes.at[:, :, i], plane_sem.at[i])

    def res_copy(i):
        return pltpu.make_async_copy(planes.at[:, :, i], res_ref.at[:, :, i], res_sem.at[i])

    def line_copy(i, c):
        at = pl.ds(pl.multiple_of((c * cx + i) * cy, 16), cy)
        return pltpu.make_async_copy(lines.at[at], out_ref.at[at], line_sem.at[c, i])

    for i in range(cx):
        field_copy(i).start()
        if 0 < i < cx - 1:
            plane_copy(i).start()
    spread_rows(near_ref, prev_ref, over_ref, rows)
    field_copy(0).wait()
    field_copy(1).wait()
    for s in range(ns):
        first, second = ([field[s, c, i] for c in range(3)] for i in range(2))
        back_z[s], back_y[s] = magnetic(first, second[1:], rows[s, 0, :1])

    @pl.loop(1, cx - 1)
    def _(i):
        field_copy(i + 1).wait()
        plane_copy(i).wait()
        scaled = OMEGA_SQ * perm_ref[i].astype(jnp.float32)
        for s in range(ns):
            own = [field[s, c, i] for c in range(3)]
            beyond = [field[s, c + 1, i + 1] for c in range(2)]
            back_z[s], back_y[s] = residual_plane(
                s, i, own, beyond, (back_z[s], back_y[s]), rows, rows[s, 3, pl.ds(i + 1, 1), :], planes, i, scaled, lines
            )
        res_copy(i).start()
        for c in range(3):
            line_copy(i, c).start()

    @pl.loop(1, cx - 1)
    def _(i):
        res_copy(i).wait()
        for c in range(3):
            line_copy(i, c).wait()


def inner_residual(field, source, permittivity, near, y_rows):
    ns, _, cx, cy, cz = field.shape
    tile_rows = (1, ns, 5, cx, cz)
    anywhere = pl.BlockSpec(memory_space=pl.ANY)
    dma = pltpu.SemaphoreType.DMA
    grid_spec = pltpu.PrefetchScalarGridSpec(
        num_scalar_prefetch=1,
        grid=(1,),
        in_specs=[
            anywhere,
            anywhere,
            pl.BlockSpec((cx, cy, cz), lambda g, _: (0, 0, 0)),
            pl.BlockSpec(tile_rows, lambda g, near: (near[0], 0, 0, 0, 0)),
            pl.BlockSpec(tile_rows, lambda g, near: (near[1], 0, 0, 0, 0)),
        ],
        out_specs=[anywhere, anywhere],
        scratch_shapes=[
            pltpu.VMEM(field.shape, jnp.float32),
            pltpu.VMEM(field.shape, jnp.float32),
            pltpu.VMEM((3 * cx * cy, ns * cz), jnp.bfloat16),
            pltpu.VMEM((ns, cy, cz), jnp.float32),
            pltpu.VMEM((ns, cy, cz), jnp.float32),
            pltpu.VMEM((ns, 5, cx, cz), jnp.float32),
            dma((cx,)),
            dma((cx,)),
            dma((cx,)),
            dma((3, cx)),
        ],
    )
    return pl.pallas_call(
        inner_kernel,
        grid_spec=grid_spec,
        out_shape=[
            jax.ShapeDtypeStruct(field.shape, jnp.float32),
            jax.ShapeDtypeStruct((3 * cx * cy, ns * cz), jnp.bfloat16),
        ],
        compiler_params=pltpu.CompilerParams(vmem_limit_bytes=60 * MIB),
        cost_estimate=pl.CostEstimate(flops=60 * field.size, bytes_accessed=14 * field.size, transcendentals=0),
        name="inner_residual",
    )(near, field, source, permittivity, y_rows, y_rows)


def gather_kernel(
    count_ref, near_ref, sol_ref, src_ref, perm_ref, prev_ref, over_ref, up_ref, down_ref, inner_ref, line_ref, depth_ref, _,
    res_ref, out_ref, field, planes, lines, turned, rows, field_sem, plane_sem, line_sem,
):
    ns, _, cx, cy, cz = sol_ref.shape
    total = lines.shape[0]
    f32 = jnp.float32
    ends = (0, cx - 1)
    field_copies = [
        pltpu.make_async_copy(sol_ref.at[:, :, i], field.at[:, :, n], field_sem.at[n])
        for n, i in enumerate((0, 1, cx - 2, cx - 1))
    ]
    plane_copies = [
        pltpu.make_async_copy(src_ref.at[:, :, i], planes.at[:, :, n], plane_sem.at[n]) for n, i in enumerate(ends)
    ]
    line_copies = []
    for c in range(3):
        at = pl.ds((c * cx + 1) * cy, (cx - 2) * cy)
        line_copies.append(pltpu.make_async_copy(inner_ref.at[at], lines.at[at], line_sem.at[c]))
    res_copies = [
        pltpu.make_async_copy(planes.at[:, :, n], res_ref.at[:, :, i], plane_sem.at[n]) for n, i in enumerate(ends)
    ]
    for copy in field_copies[:2] + plane_copies[:1] + field_copies[2:] + plane_copies[1:] + line_copies:
        copy.start()
    spread_rows(near_ref, prev_ref, over_ref, rows)
    out_ref[...] = jnp.zeros_like(out_ref)

    for copy in field_copies[:2] + plane_copies[:1]:
        copy.wait()
    scaled = OMEGA_SQ * perm_ref[0].astype(f32)
    for s in range(ns):
        own = [field[s, c, 0] for c in range(3)]
        back = own[1] - up_ref[s, :cy].astype(f32), up_ref[s, cy:].astype(f32) - own[2]
        beyond = [field[s, c + 1, 1] for c in range(2)]
        residual_plane(s, 0, own, beyond, back, rows, rows[s, 3, 1:2], planes, 0, scaled, lines)
    res_copies[0].start()

    for copy in field_copies[2:] + plane_copies[1:]:
        copy.wait()
    scaled = OMEGA_SQ * perm_ref[cx - 1].astype(f32)
    for s in range(ns):
        own = [field[s, c, 3] for c in range(3)]
        back = magnetic([field[s, c, 2] for c in range(3)], own[1:], rows[s, 0, cx - 2 : cx - 1])
        beyond = [down_ref[s, c * cy : (c + 1) * cy].astype(f32) for c in range(2)]
        after = down_ref[s, 2 * cy :].astype(f32)[:1]
        residual_plane(s, cx - 1, own, beyond, back, rows, after, planes, 1, scaled, lines)
    res_copies[1].start()

    for copy in line_copies:
        copy.wait()
    for a in range(total // 128):
        for b in range(ns * cz // 128):
            turned[b * 128 : (b + 1) * 128, a * 128 : (a + 1) * 128] = lines[
                a * 128 : (a + 1) * 128, b * 128 : (b + 1) * 128
            ].T
    group, width = out_ref.shape[1], line_ref.shape[1]

    @pl.loop(0, pl.cdiv(count_ref[0], group))
    def _(p):
        hot = (iota((total, width), 0) == line_ref[pl.ds(p, 1), :]).astype(f32).astype(jnp.bfloat16)
        got = jnp.dot(turned[...], hot, preferred_element_type=f32)
        at = iota((cz, width), 0) == depth_ref[pl.ds(p, 1), :]
        for s in range(ns):
            sums = jnp.sum(jnp.where(at, got[s * cz : (s + 1) * cz], 0.0), axis=0, keepdims=True)
            for h in range(group):
                out_ref[p, h : h + 1, s * 128 : (s + 1) * 128] = sums[:, h * 128 : (h + 1) * 128]

    for copy in res_copies:
        copy.wait()


def outer_residual_and_gather(field, source, permittivity, counts, near, y_rows, up, down, residual, inner, line, depth):
    ns, _, cx, cy, cz = field.shape
    total = 3 * cx * cy
    groups, group = line.shape[0], line.shape[1] // 128
    whole = lambda x: pl.BlockSpec(x.shape, lambda g, *_: (0,) * x.ndim)
    tile_rows = (1, ns, 5, cx, cz)
    anywhere = pl.BlockSpec(memory_space=pl.ANY)
    dma = pltpu.SemaphoreType.DMA
    grid_spec = pltpu.PrefetchScalarGridSpec(
        num_scalar_prefetch=2,
        grid=(1,),
        in_specs=[
            anywhere,
            anywhere,
            whole(permittivity),
            pl.BlockSpec(tile_rows, lambda g, _, near: (near[0], 0, 0, 0, 0)),
            pl.BlockSpec(tile_rows, lambda g, _, near: (near[1], 0, 0, 0, 0)),
            whole(up),
            whole(down),
            anywhere,
            whole(line),
            whole(depth),
            anywhere,
        ],
        out_specs=[anywhere, pl.BlockSpec((groups, group, ns * 128), lambda g, *_: (0, 0, 0))],
        scratch_shapes=[
            pltpu.VMEM((ns, 3, 4, cy, cz), jnp.float32),
            pltpu.VMEM((ns, 3, 2, cy, cz), jnp.float32),
            pltpu.VMEM((total, ns * cz), jnp.bfloat16),
            pltpu.VMEM((ns * cz, total), jnp.bfloat16),
            pltpu.VMEM((ns, 5, cx, cz), jnp.float32),
            dma((4,)),
            dma((2,)),
            dma((3,)),
        ],
    )
    return pl.pallas_call(
        gather_kernel,
        grid_spec=grid_spec,
        out_shape=[
            jax.ShapeDtypeStruct(field.shape, jnp.float32),
            jax.ShapeDtypeStruct((groups, group, ns * 128), jnp.float32),
        ],
        input_output_aliases={12: 0},
        compiler_params=pltpu.CompilerParams(vmem_limit_bytes=60 * MIB),
        name="outer_residual_gather",
    )(counts, near, field, source, permittivity, y_rows, y_rows, up, down, inner, line, depth, residual)


def fronts_kernel(x_top, x_mid, x_low, top_ref, mid_ref, low_ref, y_ref, top_buf, mid_buf, low_buf, sem):
    jobs, base = [], 0
    for x_ref, w_ref, buf in ((x_top, top_ref, top_buf), (x_mid, mid_ref, mid_buf), (x_low, low_ref, low_buf)):
        count, height, width = w_ref.shape
        rows = height
        while rows > 256 and rows * width * 2 > 4 * MIB:
            rows //= 2
        for f in range(count):
            for r in range(0, height, rows):
                at = pl.ds(r, rows)
                copy = pltpu.make_async_copy(w_ref.at[f, at], buf.at[f, at], sem.at[len(jobs)])
                jobs.append((copy, x_ref, buf, f, at, pl.ds(base + r, rows)))
            base += height
    for job in jobs:
        job[0].start()
    for copy, x_ref, buf, f, at, out in jobs:
        copy.wait()
        y_ref[:, out] = lax.dot_general(
            x_ref[f], buf[f, at], (((1,), (1,)), ((), ())), preferred_element_type=jnp.float32
        )


def fronts(parts, inverses):
    sources = parts[0].shape[1]
    height = sum(inv.shape[0] * inv.shape[1] for inv in inverses)
    entries = sum(inv.size for inv in inverses)
    here, there = pl.BlockSpec(memory_space=pltpu.VMEM), pl.BlockSpec(memory_space=pl.ANY)
    return pl.pallas_call(
        fronts_kernel,
        in_specs=[here] * 3 + [there] * 3,
        out_specs=here,
        out_shape=jax.ShapeDtypeStruct((sources, height), jnp.float32),
        scratch_shapes=[pltpu.VMEM(inv.shape, inv.dtype) for inv in inverses] + [pltpu.SemaphoreType.DMA((64,))],
        compiler_params=pltpu.CompilerParams(vmem_limit_bytes=60 * MIB),
        cost_estimate=pl.CostEstimate(flops=4 * entries, bytes_accessed=2 * entries, transcendentals=0),
        name="fronts",
    )(*parts, *inverses)


def correct_kernel(
    count_ref, sol_ref, res_ref, perm_ref, own_line_ref, own_depth_ref, line_ref, depth_ref, value_ref,
    out_ref, new_ref, field, residual, delta, x_halo, y_halo, back_z, back_y, in_sem, out_sem,
):
    ns, _, planes, cy, cz = sol_ref.shape
    f32, half = jnp.float32, jnp.bfloat16

    def copies_in(i):
        return [
            pltpu.make_async_copy(ref.at[:, :, i], buf.at[:, :, i], in_sem.at[n, i])
            for n, (ref, buf) in enumerate(((sol_ref, field), (res_ref, residual)))
        ]

    def copies_out(i):
        return [
            pltpu.make_async_copy(buf.at[:, :, i], ref.at[:, :, i], out_sem.at[n, i])
            for n, (ref, buf) in enumerate(((out_ref, field), (new_ref, residual)))
        ]

    for i in range(planes):
        for copy in copies_in(i):
            copy.start()
    capacity = value_ref.shape[0] // len(NEAR)

    def values_of(first, count):
        rows = [value_ref[pl.ds(first + h, 1), :] for h in range(count)]
        return [jnp.concatenate([v[:, s * 128 : (s + 1) * 128] for v in rows], axis=1) for s in range(ns)]

    def times(a, b):
        return lax.dot_general(a, b, (((1,), (1,)), ((), ())), preferred_element_type=f32)

    x_halo[...] = jnp.zeros_like(x_halo)
    y_halo[...] = jnp.zeros_like(y_halo)
    own_width = own_line_ref.shape[1]
    own_group = own_width // 128

    def own_part(p):
        values = values_of(p * own_group, own_group)
        hot = (iota((delta.shape[0], own_width), 0) == own_line_ref[pl.ds(p, 1), :]).astype(f32).astype(half)
        at = iota((cz, own_width), 0) == own_depth_ref[pl.ds(p, 1), :]
        return times(hot, jnp.concatenate([jnp.where(at, v, 0.0).astype(half) for v in values], axis=0))

    delta[...] = own_part(0)

    @pl.loop(1, pl.cdiv(count_ref[0], own_group))
    def _(p):
        delta[...] += own_part(p)

    width = line_ref.shape[1]
    group = width // 128
    place = (
        (x_halo, 0, 2 * cy),
        (x_halo, 2 * cy, 3 * cy),
        (y_halo, 0, 2 * planes),
        (y_halo, 2 * planes, 3 * planes),
        (y_halo, 5 * planes, 8),
        (y_halo, 5 * planes, 8),
    )
    for q, (target, first, height) in enumerate(place):

        @pl.loop(0, pl.cdiv(count_ref[q + 1], group))
        def _(p, q=q, target=target, first=first, height=height):
            row = q * (capacity // group) + p

            @pl.when(count_ref[len(NEAR) + row] > 0)
            def _():
                values = values_of((q + 1) * capacity + p * group, group)
                at = iota((height, width), 0) == line_ref[pl.ds(row, 1), :]
                hot = (iota((cz, width), 0) == depth_ref[pl.ds(row, 1), :]).astype(f32).astype(half)
                got = times(jnp.concatenate([jnp.where(at, v, 0.0) for v in values], axis=0).astype(half), hot)
                for s in range(ns):
                    target[s, first : first + height] += got[s * height : (s + 1) * height]

    def plane(s, c, i):
        return delta[pl.ds(pl.multiple_of((c * planes + i) * cy, 8), cy), s * cz : (s + 1) * cz]

    for s in range(ns):
        ex, ey, ez = (x_halo[s, (2 + c) * cy : (3 + c) * cy] for c in range(3))
        corner = y_halo[s, 5 * planes : 5 * planes + 1]
        back_z[s] = plane(s, 1, 0) - (ey + (ahead(ex, 0, corner) - ex))
        back_y[s] = (ez + (ahead(ex, 1) - ex)) - plane(s, 2, 0)

    @pl.loop(0, planes)
    def _(i):
        last = i == planes - 1
        after = jnp.minimum(i + 1, planes - 1)
        scaled = OMEGA_SQ * perm_ref[i].astype(f32)
        for copy in copies_in(i):
            copy.wait()
        for s in range(ns):
            own = [plane(s, c, i) for c in range(3)]
            beyond = [jnp.where(last, x_halo[s, c * cy : (c + 1) * cy], plane(s, c + 1, after)) for c in range(2)]
            y_row_x = y_halo[s, pl.ds(i, 1), :]
            y_row_z = y_halo[s, pl.ds(planes + i, 1), :]
            hx, hy, hz = (y_halo[s, pl.ds((2 + c) * planes + i, 1), :] for c in range(3))
            hy_after = jnp.where(
                last, y_halo[s, 5 * planes + 1 : 5 * planes + 2], y_halo[s, pl.ds(3 * planes + after, 1), :]
            )
            curls = curl_plane(
                own,
                beyond,
                back_z[s],
                back_y[s],
                y_row_x,
                y_row_z,
                (hx + (hy_after - hy)) - own[0],
                own[2] - (hz + (ahead(hy, 1) - hy)),
            )
            for c in range(3):
                field[s, c, i] += own[c]
                residual[s, c, i] -= curls[c] - scaled * own[c]
            back_z[s], back_y[s] = curls[3], curls[4]
        for copy in copies_out(i):
            copy.start()

    @pl.loop(0, planes)
    def _(i):
        for copy in copies_out(i):
            copy.wait()


def correct(field, residual, permittivity, counts, own_line, own_depth, line, depth, values):
    ns, _, cx, cy, cz = field.shape
    anywhere = pl.BlockSpec(memory_space=pl.ANY)
    whole = lambda x: pl.BlockSpec(x.shape, lambda g, *_: (0,) * x.ndim)
    y_lines = 5 * cx + 8
    grid_spec = pltpu.PrefetchScalarGridSpec(
        num_scalar_prefetch=1,
        grid=(1,),
        in_specs=[
            anywhere,
            anywhere,
            *[whole(x) for x in (permittivity, own_line, own_depth, line, depth, values)],
        ],
        out_specs=[anywhere, anywhere],
        scratch_shapes=[
            pltpu.VMEM(field.shape, jnp.float32),
            pltpu.VMEM(field.shape, jnp.float32),
            pltpu.VMEM((3 * cx * cy, ns * cz), jnp.float32),
            pltpu.VMEM((ns, 5 * cy, cz), jnp.float32),
            pltpu.VMEM((ns, y_lines, cz), jnp.float32),
            pltpu.VMEM((ns, cy, cz), jnp.float32),
            pltpu.VMEM((ns, cy, cz), jnp.float32),
            pltpu.SemaphoreType.DMA((2, cx)),
            pltpu.SemaphoreType.DMA((2, cx)),
        ],
    )
    return pl.pallas_call(
        correct_kernel,
        grid_spec=grid_spec,
        out_shape=[jax.ShapeDtypeStruct(field.shape, jnp.float32)] * 2,
        compiler_params=pltpu.CompilerParams(vmem_limit_bytes=60 * MIB),
        name="correct",
    )(counts, field, residual, permittivity, own_line, own_depth, line, depth, values)


def block_rows_of(inverses, wide_count, block_rows):
    per_device = sum(inv.shape[0] * inv.shape[1] for inv in inverses) // block_rows
    table, base = [], 0
    for inv in inverses:
        per = inv.shape[1] // block_rows
        for f in range(inv.shape[0]):
            b = np.arange(per * wide_count)
            table.append(b // per * per_device + base + f * per + b % per)
        base += inv.shape[0] * per
    return np.concatenate(table).astype(np.int32)


def block_columns_of(inverses, narrow_count, block_rows):
    table, base = [], 0
    for inv in inverses:
        per = inv.shape[2] // block_rows
        for _ in range(inv.shape[0]):
            table.append(base + np.arange(per * narrow_count).reshape(narrow_count, per))
            base += per * narrow_count
    return np.concatenate(table, axis=1).astype(np.int32)


def to_all_wide(block, wide_count):
    spread = jnp.broadcast_to(block[None], (wide_count, *block.shape)).reshape(-1, *block.shape[1:])
    return lax.all_to_all(spread, "wide", 0, 0, tiled=True)


def on_device(solution, source_term, permittivity, inv_top, inv_mid, inv_low, sep_tile, sep_cell):
    wide_count, narrow_count = lax.axis_size("wide"), lax.axis_size("narrow")
    my_wide, my_narrow = lax.axis_index("wide"), lax.axis_index("narrow")
    ns, _, cx, cy, cz = solution.shape
    block_count, block_rows = sep_cell.shape
    capacity = max(2, 2 * block_count // (wide_count * narrow_count))
    inverses = (inv_top[None], inv_mid, inv_low)

    near = jnp.stack(
        [
            jnp.maximum(my_narrow - 1, 0),
            jnp.minimum(my_narrow + 1, narrow_count - 1),
            (my_narrow > 0).astype(jnp.int32),
            (my_narrow < narrow_count - 1).astype(jnp.int32),
        ]
    )
    y_rows = lax.all_gather(outer_rows(solution), "narrow", axis=0, tiled=False)
    to_up, to_down = outer_planes(solution, near, y_rows)
    steps = [(w, w + 1) for w in range(wide_count - 1)]
    up = lax.ppermute(to_up, "wide", steps)
    down = lax.ppermute(to_down, "wide", [(b, a) for a, b in steps])
    inner, inner_lines = inner_residual(solution, source_term, permittivity, near, y_rows)

    block_tile = sep_tile[:, 0]
    block_ids = jnp.arange(block_count, dtype=jnp.int32)
    slot_rank = jnp.sum(
        jnp.logical_and(
            block_tile[:, None] == block_tile[None, :], block_ids[None, :] < block_ids[:, None]
        ).astype(jnp.int32),
        axis=1,
    )
    offsets = np.array(NEAR, np.int32)
    near_wide, near_narrow = my_wide + offsets[:, 0], my_narrow + offsets[:, 1]
    inside = (near_wide >= 0) & (near_wide < wide_count) & (near_narrow >= 0) & (near_narrow < narrow_count)
    near_tile = jnp.where(inside, near_wide * narrow_count + near_narrow, -1)
    named = block_tile[None, :] == near_tile[:, None]
    counts = jnp.sum(named.astype(jnp.int32), axis=1)
    slots = jnp.arange(capacity, dtype=jnp.int32)
    match = jnp.logical_and(named[:, None, :], slot_rank[None, None, :] == slots[None, :, None])
    near_ids = jnp.sum(jnp.where(match, block_ids[None, None, :], 0), axis=2)
    near_rows = jnp.sum(
        jnp.where(match, block_rows_of(inverses, wide_count, block_rows)[None, None, :], 0), axis=2
    )
    found = slots[None, :] < counts[:, None]
    cells = jnp.take(sep_cell, near_ids.reshape(-1), axis=0).reshape(len(NEAR), capacity, block_rows)
    depth = cells % cz
    row = cells // cz
    part, at_i, at_j = row // (cx * cy), row // cy % cx, row % cy
    rule = (
        (row, row >= 0),
        ((part - 1) * cy + at_j, (part >= 1) & (at_i == 0)),
        (part * cy + at_j, at_i == cx - 1),
        (part // 2 * cx + at_i, (part != 1) & (at_j == 0)),
        (part * cx + at_i, at_j == cy - 1),
        (jnp.zeros_like(row), (part == 0) & (at_i == cx - 1) & (at_j == 0)),
        (jnp.ones_like(row), (part == 1) & (at_i == 0) & (at_j == cy - 1)),
    )
    line = jnp.stack(
        [jnp.where(found[q, :, None] & keep[q], at[q], -1) for q, (at, keep) in enumerate(rule)]
    )
    arrives = (block_tile % narrow_count * wide_count + block_tile // narrow_count) * capacity + slot_rank
    table = block_columns_of(inverses, narrow_count, block_rows)
    held_at = jnp.sum(
        jnp.where(
            (table[:, :, None] == block_ids) & (np.arange(narrow_count)[:, None, None] == my_narrow), arrives, 0
        ),
        axis=(0, 2),
    )
    own_width, width = min(8, capacity) * block_rows, min(4, capacity) * block_rows
    own_line, own_depth = line[0].reshape(-1, own_width), depth[0].reshape(-1, own_width)
    line, depth = line[1:].reshape(-1, width), depth[1:].reshape(-1, width)
    loads = jnp.concatenate([counts, jnp.max(line, axis=1) + 1])

    residual, picked = outer_residual_and_gather(
        solution, source_term, permittivity, counts, near, y_rows, up, down, inner, inner_lines, own_line, own_depth
    )
    picked = picked.reshape(capacity, ns * block_rows).astype(jnp.bfloat16)
    everyone = lax.all_gather(to_all_wide(picked, wide_count), "narrow", axis=0, tiled=True)

    columns = jnp.take(everyone, held_at, axis=0)
    columns = columns.reshape(-1, ns, block_rows).transpose(1, 0, 2).reshape(ns, -1)
    parts, base = [], 0
    for inv in inverses:
        width = inv.shape[0] * inv.shape[2]
        parts.append(columns[:, base : base + width].reshape(ns, inv.shape[0], -1).transpose(1, 0, 2))
        base += width
    partial = fronts(parts, inverses).astype(jnp.bfloat16)
    rows = partial.shape[1] // block_rows
    shares = lax.all_gather(partial.reshape(ns, rows, block_rows), "narrow", axis=0, tiled=False)
    summed = jnp.sum(shares.astype(jnp.float32), axis=0).astype(jnp.bfloat16)
    summed = summed.transpose(1, 0, 2).reshape(rows, ns * block_rows)
    updates = to_all_wide(summed, wide_count)

    values = jnp.take(updates, near_rows.reshape(-1), axis=0).astype(jnp.float32)
    return tuple(correct(solution, residual, permittivity, loads, own_line, own_depth, line, depth, values))


def solution(mesh):
    return jax.shard_map(
        on_device,
        mesh=mesh,
        in_specs=(
            P(None, None, "wide", "narrow", None),
            P(None, None, "wide", "narrow", None),
            P("wide", "narrow", None),
            P("wide", "narrow"),
            P(None, "wide", "narrow"),
            P(None, "wide", "narrow"),
            P(),
            P(),
        ),
        out_specs=(P(None, None, "wide", "narrow", None), P(None, None, "wide", "narrow", None)),
        check_vma=False,
    )
```

```python
import jax
import jax.numpy as jnp
import numpy as np
from jax import lax
from jax.experimental import pallas as pl
from jax.experimental.pallas import tpu as pltpu
from jax.sharding import PartitionSpec as P

OMEGA_SQ = 0.5
MIB = 1 << 20

NEAR = ((0, 0), (1, 0), (-1, 0), (0, 1), (0, -1), (-1, 1), (1, -1))


def iota(shape, dim):
    return lax.broadcasted_iota(jnp.int32, shape, dim)


def lane_blocks(x):
    return [x[:, at : at + 128] for at in range(0, x.shape[1], 128)]


def shifted(x, axis, step, edge):
    if axis == 1:
        size, blocks = 128, lane_blocks(x)
        fill = lane_blocks(jnp.broadcast_to(edge, x.shape))
        turned = [pltpu.roll(b, step % size, 1) for b in blocks]
        mask = iota((1, size), 1)
    else:
        size, tiles = 8, x.shape[0] // 8
        turned = pltpu.roll(x.reshape(tiles, size, x.shape[1]), step % size, 1)
        turned = [turned[t] for t in range(tiles)]
        filled = jnp.broadcast_to(edge, (size, x.shape[1])) if jnp.ndim(edge) == 0 or edge.shape[0] == 1 else edge
        fill = [filled[:size]] * tiles
        mask = iota((size, 1), 0)
    if step < 0:
        others = [*turned[1:], fill[-1]]
        mask = mask == size - 1
    else:
        others = [fill[0], *turned[:-1]]
        mask = mask == 0
    return jnp.concatenate([jnp.where(mask, o, t) for o, t in zip(others, turned, strict=True)], axis=axis)


def ahead(x, axis, edge=0.0):
    return shifted(x, axis, -1, edge)


def behind(x, axis, edge):
    return shifted(x, axis, 1, edge)


def rows_kernel(low_ref, high_ref, out_ref):
    top = high_ref.shape[3] - 1
    for s in range(out_ref.shape[0]):
        rows = [low_ref[s, 0, :, 0, :], low_ref[s, 2, :, 0, :], *(high_ref[s, c, :, top, :] for c in range(3))]
        for n, row in enumerate(rows):
            out_ref[s, n] = row.astype(out_ref.dtype)


def outer_rows(field):
    ns, _, cx, cy, cz = field.shape
    slab = (ns, 3, cx, 8, cz)
    return pl.pallas_call(
        rows_kernel,
        grid=(1,),
        in_specs=[
            pl.BlockSpec(slab, lambda g: (0, 0, 0, 0, 0)),
            pl.BlockSpec(slab, lambda g: (0, 0, 0, cy // 8 - 1, 0)),
        ],
        out_specs=pl.BlockSpec((ns, 5, cx, cz), lambda g: (0, 0, 0, 0)),
        out_shape=jax.ShapeDtypeStruct((ns, 5, cx, cz), jnp.bfloat16),
        compiler_params=pltpu.CompilerParams(vmem_limit_bytes=60 * MIB),
        name="outer_rows",
    )(field, field)


def beside(rows_ref):
    me, last = lax.axis_index("narrow"), rows_ref.shape[0] - 1
    return (jnp.maximum(me - 1, 0), me > 0), (jnp.minimum(me + 1, last), me < last)


def planes_kernel(first_ref, last_ref, rows_ref, up_ref, down_ref):
    planes, cy, dtype = rows_ref.shape[3], first_ref.shape[3], up_ref.dtype
    (before, has_before), (after, has_after) = beside(rows_ref)
    for s in range(up_ref.shape[0]):
        ex, ey, ez = (last_ref[s, c, 0] for c in range(3))
        past = jnp.where(has_after, rows_ref[after, s, 0].astype(jnp.float32)[planes - 1 :], 0.0)
        up_ref[s, :cy] = (ey + (ahead(ex, 0, past) - ex)).astype(dtype)
        up_ref[s, cy:] = (ez + (ahead(ex, 1) - ex)).astype(dtype)
        down_ref[s, :cy] = first_ref[s, 1, 0].astype(dtype)
        down_ref[s, cy : 2 * cy] = first_ref[s, 2, 0].astype(dtype)
        edge = jnp.where(has_before, rows_ref[before, s, 3].astype(jnp.float32)[:1], 0.0)
        down_ref[s, 2 * cy :] = jnp.broadcast_to(edge, (down_ref.shape[1] - 2 * cy, edge.shape[1])).astype(dtype)


def outer_planes(field, rows):
    ns, _, cx, cy, cz = field.shape
    plane = (ns, 3, 1, cy, cz)
    heights = (2 * cy, 2 * cy + 16)
    return pl.pallas_call(
        planes_kernel,
        grid=(1,),
        in_specs=[
            pl.BlockSpec(plane, lambda g: (0, 0, 0, 0, 0)),
            pl.BlockSpec(plane, lambda g: (0, 0, cx - 1, 0, 0)),
            pl.BlockSpec(rows.shape, lambda g: (0,) * 5),
        ],
        out_specs=[pl.BlockSpec((ns, h, cz), lambda g: (0, 0, 0)) for h in heights],
        out_shape=[jax.ShapeDtypeStruct((ns, h, cz), jnp.bfloat16) for h in heights],
        compiler_params=pltpu.CompilerParams(vmem_limit_bytes=60 * MIB),
        name="outer_planes",
    )(field, field, rows)


def curl_plane(own, beyond, back_z, back_y, y_row_x, y_row_z, y_edge_z, y_edge_x):
    ex, ey, ez = own
    hx = (ahead(ez, 0, y_row_z) - ez) - (ahead(ey, 1) - ey)
    hy = (ahead(ex, 1) - ex) - (beyond[1] - ez)
    hz = (beyond[0] - ey) - (ahead(ex, 0, y_row_x) - ex)
    cx = (hz - behind(hz, 0, y_edge_z)) - (hy - behind(hy, 1, ex))
    cy = (hx - behind(hx, 1, -ey)) - (hz - back_z)
    cz = (hy - back_y) - (hx - behind(hx, 0, y_edge_x))
    return cx, cy, cz, hz, hy


def magnetic(own, beyond, row_x):
    ex, ey, ez = own
    return (beyond[0] - ey) - (ahead(ex, 0, row_x) - ex), (ahead(ex, 1) - ex) - (beyond[1] - ez)


def spread_rows(rows_ref, scratch):
    before, after = beside(rows_ref)
    for s in range(scratch.shape[0]):
        for n in range(5):
            tile, there = after if n < 2 else before
            scratch[s, n] = jnp.where(there, rows_ref[tile, s, n].astype(jnp.float32), 0.0)


def residual_plane(s, i, own, beyond, back, rows, after, planes, at, scaled, lines):
    cy, cz = own[0].shape
    cx = rows.shape[2]
    row_x, row_z, ex, ey, ez = (rows[s, n, pl.ds(i, 1), :] for n in range(5))
    curls = curl_plane(
        own, beyond, back[0], back[1], row_x, row_z, (ex + (after - ey)) - own[0], own[2] - (ez + (ahead(ey, 1) - ey))
    )
    for c in range(3):
        value = planes[s, c, at] - (curls[c] - scaled * own[c])
        planes[s, c, at] = value
        first = pl.multiple_of((c * cx + i) * cy, 16)
        lines[pl.ds(first, cy), s * cz : (s + 1) * cz] = value.astype(jnp.bfloat16)
    return curls[3], curls[4]


def inner_kernel(
    sol_ref, src_ref, perm_ref, rows_ref, res_ref, out_ref,
    field, planes, lines, back_z, back_y, rows, field_sem, plane_sem, res_sem, line_sem,
):
    ns, _, cx, cy, _ = field.shape

    def field_copy(i):
        return pltpu.make_async_copy(sol_ref.at[:, :, i], field.at[:, :, i], field_sem.at[i])

    def plane_copy(i):
        return pltpu.make_async_copy(src_ref.at[:, :, i], planes.at[:, :, i], plane_sem.at[i])

    def res_copy(i):
        return pltpu.make_async_copy(planes.at[:, :, i], res_ref.at[:, :, i], res_sem.at[i])

    def line_copy(i, c):
        at = pl.ds(pl.multiple_of((c * cx + i) * cy, 16), cy)
        return pltpu.make_async_copy(lines.at[at], out_ref.at[at], line_sem.at[c, i])

    for i in range(cx):
        field_copy(i).start()
        if 0 < i < cx - 1:
            plane_copy(i).start()
    spread_rows(rows_ref, rows)
    field_copy(0).wait()
    field_copy(1).wait()
    for s in range(ns):
        first, second = ([field[s, c, i] for c in range(3)] for i in range(2))
        back_z[s], back_y[s] = magnetic(first, second[1:], rows[s, 0, :1])

    @pl.loop(1, cx - 1)
    def _(i):
        field_copy(i + 1).wait()
        plane_copy(i).wait()
        scaled = OMEGA_SQ * perm_ref[i].astype(jnp.float32)
        for s in range(ns):
            own = [field[s, c, i] for c in range(3)]
            beyond = [field[s, c + 1, i + 1] for c in range(2)]
            back_z[s], back_y[s] = residual_plane(
                s, i, own, beyond, (back_z[s], back_y[s]), rows, rows[s, 3, pl.ds(i + 1, 1), :], planes, i, scaled, lines
            )
        res_copy(i).start()
        for c in range(3):
            line_copy(i, c).start()

    @pl.loop(1, cx - 1)
    def _(i):
        res_copy(i).wait()
        for c in range(3):
            line_copy(i, c).wait()


def inner_residual(field, source, permittivity, y_rows):
    ns, _, cx, cy, cz = field.shape
    anywhere = pl.BlockSpec(memory_space=pl.ANY)
    dma = pltpu.SemaphoreType.DMA
    grid_spec = pl.GridSpec(
        grid=(1,),
        in_specs=[
            anywhere,
            anywhere,
            pl.BlockSpec((cx, cy, cz), lambda g: (0, 0, 0)),
            pl.BlockSpec(y_rows.shape, lambda g: (0,) * 5),
        ],
        out_specs=[anywhere, anywhere],
        scratch_shapes=[
            pltpu.VMEM(field.shape, jnp.float32),
            pltpu.VMEM(field.shape, jnp.float32),
            pltpu.VMEM((3 * cx * cy, ns * cz), jnp.bfloat16),
            pltpu.VMEM((ns, cy, cz), jnp.float32),
            pltpu.VMEM((ns, cy, cz), jnp.float32),
            pltpu.VMEM((ns, 5, cx, cz), jnp.float32),
            dma((cx,)),
            dma((cx,)),
            dma((cx,)),
            dma((3, cx)),
        ],
    )
    return pl.pallas_call(
        inner_kernel,
        grid_spec=grid_spec,
        out_shape=[
            jax.ShapeDtypeStruct(field.shape, jnp.float32),
            jax.ShapeDtypeStruct((3 * cx * cy, ns * cz), jnp.bfloat16),
        ],
        compiler_params=pltpu.CompilerParams(vmem_limit_bytes=60 * MIB),
        cost_estimate=pl.CostEstimate(flops=60 * field.size, bytes_accessed=14 * field.size, transcendentals=0),
        name="inner_residual",
    )(field, source, permittivity, y_rows)


def gather_kernel(
    count_ref, sol_ref, src_ref, perm_ref, rows_ref, up_ref, down_ref, inner_ref, line_ref, depth_ref, _,
    res_ref, out_ref, field, planes, lines, turned, rows, got_ref, field_sem, plane_sem, line_sem,
):
    ns, _, cx, cy, cz = sol_ref.shape
    total = lines.shape[0]
    f32 = jnp.float32
    ends = (0, cx - 1)
    field_copies = [
        pltpu.make_async_copy(sol_ref.at[:, :, i], field.at[:, :, n], field_sem.at[n])
        for n, i in enumerate((0, 1, cx - 2, cx - 1))
    ]
    plane_copies = [
        pltpu.make_async_copy(src_ref.at[:, :, i], planes.at[:, :, n], plane_sem.at[n]) for n, i in enumerate(ends)
    ]
    line_copies = []
    for c in range(3):
        at = pl.ds((c * cx + 1) * cy, (cx - 2) * cy)
        line_copies.append(pltpu.make_async_copy(inner_ref.at[at], lines.at[at], line_sem.at[c]))
    res_copies = [
        pltpu.make_async_copy(planes.at[:, :, n], res_ref.at[:, :, i], plane_sem.at[n]) for n, i in enumerate(ends)
    ]
    for copy in field_copies[:2] + plane_copies[:1] + field_copies[2:] + plane_copies[1:] + line_copies:
        copy.start()
    spread_rows(rows_ref, rows)
    got_ref[...] = jnp.zeros_like(got_ref)

    for copy in field_copies[:2] + plane_copies[:1]:
        copy.wait()
    scaled = OMEGA_SQ * perm_ref[0].astype(f32)
    for s in range(ns):
        own = [field[s, c, 0] for c in range(3)]
        back = own[1] - up_ref[s, :cy].astype(f32), up_ref[s, cy:].astype(f32) - own[2]
        beyond = [field[s, c + 1, 1] for c in range(2)]
        residual_plane(s, 0, own, beyond, back, rows, rows[s, 3, 1:2], planes, 0, scaled, lines)
    res_copies[0].start()

    for copy in field_copies[2:] + plane_copies[1:]:
        copy.wait()
    scaled = OMEGA_SQ * perm_ref[cx - 1].astype(f32)
    for s in range(ns):
        own = [field[s, c, 3] for c in range(3)]
        back = magnetic([field[s, c, 2] for c in range(3)], own[1:], rows[s, 0, cx - 2 : cx - 1])
        beyond = [down_ref[s, c * cy : (c + 1) * cy].astype(f32) for c in range(2)]
        after = down_ref[s, 2 * cy :].astype(f32)[:1]
        residual_plane(s, cx - 1, own, beyond, back, rows, after, planes, 1, scaled, lines)
    res_copies[1].start()

    for copy in line_copies:
        copy.wait()
    for a in range(total // 128):
        for b in range(ns * cz // 128):
            turned[b * 128 : (b + 1) * 128, a * 128 : (a + 1) * 128] = lines[
                a * 128 : (a + 1) * 128, b * 128 : (b + 1) * 128
            ].T
    group, width = got_ref.shape[1], line_ref.shape[1]

    @pl.loop(0, pl.cdiv(count_ref[0], group))
    def _(p):
        hot = (iota((total, width), 0) == line_ref[pl.ds(p, 1), :]).astype(f32).astype(jnp.bfloat16)
        got = jnp.dot(turned[...], hot, preferred_element_type=f32)
        at = iota((cz, width), 0) == depth_ref[pl.ds(p, 1), :]
        for s in range(ns):
            sums = jnp.sum(jnp.where(at, got[s * cz : (s + 1) * cz], 0.0), axis=0, keepdims=True)
            for h in range(group):
                got_ref[p, h : h + 1, s * 128 : (s + 1) * 128] = sums[:, h * 128 : (h + 1) * 128]

    picked = got_ref[...].reshape(out_ref.shape[1:]).astype(out_ref.dtype)
    for w in range(out_ref.shape[0]):
        out_ref[w] = picked
    for copy in res_copies:
        copy.wait()


def outer_residual_and_gather(copies, field, source, permittivity, counts, y_rows, up, down, residual, inner, line, depth):
    ns, _, cx, cy, cz = field.shape
    total = 3 * cx * cy
    groups, group = line.shape[0], line.shape[1] // 128
    whole = lambda x: pl.BlockSpec(x.shape, lambda g, *_: (0,) * x.ndim)
    anywhere = pl.BlockSpec(memory_space=pl.ANY)
    dma = pltpu.SemaphoreType.DMA
    grid_spec = pltpu.PrefetchScalarGridSpec(
        num_scalar_prefetch=1,
        grid=(1,),
        in_specs=[
            anywhere,
            anywhere,
            whole(permittivity),
            whole(y_rows),
            whole(up),
            whole(down),
            anywhere,
            whole(line),
            whole(depth),
            anywhere,
        ],
        out_specs=[anywhere, pl.BlockSpec((copies, groups * group, ns * 128), lambda g, *_: (0, 0, 0))],
        scratch_shapes=[
            pltpu.VMEM((ns, 3, 4, cy, cz), jnp.float32),
            pltpu.VMEM((ns, 3, 2, cy, cz), jnp.float32),
            pltpu.VMEM((total, ns * cz), jnp.bfloat16),
            pltpu.VMEM((ns * cz, total), jnp.bfloat16),
            pltpu.VMEM((ns, 5, cx, cz), jnp.float32),
            pltpu.VMEM((groups, group, ns * 128), jnp.float32),
            dma((4,)),
            dma((2,)),
            dma((3,)),
        ],
    )
    return pl.pallas_call(
        gather_kernel,
        grid_spec=grid_spec,
        out_shape=[
            jax.ShapeDtypeStruct(field.shape, jnp.float32),
            jax.ShapeDtypeStruct((copies, groups * group, ns * 128), jnp.bfloat16),
        ],
        input_output_aliases={10: 0},
        compiler_params=pltpu.CompilerParams(vmem_limit_bytes=60 * MIB),
        name="outer_residual_gather",
    )(counts, field, source, permittivity, y_rows, up, down, inner, line, depth, residual)


def fronts_kernel(columns_ref, top_ref, mid_ref, low_ref, y_ref, top_buf, mid_buf, low_buf, x_buf, y_buf, sem):
    ns = y_buf.shape[0]
    jobs, base, column = [], 0, 0
    for w_ref, buf in ((top_ref, top_buf), (mid_ref, mid_buf), (low_ref, low_buf)):
        count, height, width = w_ref.shape
        rows = height
        while rows > 256 and rows * width * 2 > 4 * MIB:
            rows //= 2
        for f in range(count):
            for r in range(0, height, rows):
                at = pl.ds(r, rows)
                copy = pltpu.make_async_copy(w_ref.at[f, at], buf.at[f, at], sem.at[len(jobs)])
                jobs.append((copy, buf, f, at, slice(column, column + width), (base + r) // 128))
            base += height
            column += width
    for job in jobs:
        job[0].start()
    columns = columns_ref[...].astype(jnp.float32)
    for b in range(columns.shape[0]):
        for s in range(ns):
            x_buf[s : s + 1, b * 128 : (b + 1) * 128] = columns[b : b + 1, s * 128 : (s + 1) * 128]
    for copy, buf, f, at, lanes, first in jobs:
        copy.wait()
        got = lax.dot_general(
            x_buf[:, lanes].astype(jnp.bfloat16),
            buf[f, at],
            (((1,), (1,)), ((), ())),
            preferred_element_type=jnp.float32,
        )
        for b in range(got.shape[1] // 128):
            for s in range(ns):
                y_buf[s, first + b : first + b + 1] = got[s : s + 1, b * 128 : (b + 1) * 128]
    y_ref[...] = y_buf[...].astype(y_ref.dtype)


def fronts(columns, inverses):
    ns = columns.shape[1] // 128
    blocks = sum(inv.shape[0] * inv.shape[1] for inv in inverses) // 128
    entries = sum(inv.size for inv in inverses)
    here, there = pl.BlockSpec(memory_space=pltpu.VMEM), pl.BlockSpec(memory_space=pl.ANY)
    return pl.pallas_call(
        fronts_kernel,
        in_specs=[here] + [there] * 3,
        out_specs=here,
        out_shape=jax.ShapeDtypeStruct((ns, blocks, 128), jnp.bfloat16),
        scratch_shapes=[
            *[pltpu.VMEM(inv.shape, inv.dtype) for inv in inverses],
            pltpu.VMEM((ns, columns.shape[0] * 128), jnp.float32),
            pltpu.VMEM((ns, blocks, 128), jnp.float32),
            pltpu.SemaphoreType.DMA((64,)),
        ],
        compiler_params=pltpu.CompilerParams(vmem_limit_bytes=60 * MIB),
        cost_estimate=pl.CostEstimate(flops=4 * entries, bytes_accessed=2 * entries, transcendentals=0),
        name="fronts",
    )(columns, *inverses)


def correct_kernel(
    count_ref, sol_ref, res_ref, perm_ref, own_line_ref, own_depth_ref, line_ref, depth_ref, given_ref,
    out_ref, new_ref, value_ref, field, residual, delta, x_halo, y_halo, back_z, back_y, in_sem, out_sem,
):
    ns, _, planes, cy, cz = sol_ref.shape
    f32, half = jnp.float32, jnp.bfloat16

    def copies_in(i):
        return [
            pltpu.make_async_copy(ref.at[:, :, i], buf.at[:, :, i], in_sem.at[n, i])
            for n, (ref, buf) in enumerate(((sol_ref, field), (res_ref, residual)))
        ]

    def copies_out(i):
        return [
            pltpu.make_async_copy(buf.at[:, :, i], ref.at[:, :, i], out_sem.at[n, i])
            for n, (ref, buf) in enumerate(((out_ref, field), (new_ref, residual)))
        ]

    for i in range(planes):
        for copy in copies_in(i):
            copy.start()
    capacity = value_ref.shape[0] // len(NEAR)

    def values_of(first, count):
        rows = [value_ref[pl.ds(first + h, 1), :] for h in range(count)]
        return [jnp.concatenate([v[:, s * 128 : (s + 1) * 128] for v in rows], axis=1) for s in range(ns)]

    def times(a, b):
        return lax.dot_general(a, b, (((1,), (1,)), ((), ())), preferred_element_type=f32)

    value_ref[...] = given_ref[...].astype(f32)
    x_halo[...] = jnp.zeros_like(x_halo)
    y_halo[...] = jnp.zeros_like(y_halo)
    own_width = own_line_ref.shape[1]
    own_group = own_width // 128

    def own_part(p):
        values = values_of(p * own_group, own_group)
        hot = (iota((delta.shape[0], own_width), 0) == own_line_ref[pl.ds(p, 1), :]).astype(f32).astype(half)
        at = iota((cz, own_width), 0) == own_depth_ref[pl.ds(p, 1), :]
        return times(hot, jnp.concatenate([jnp.where(at, v, 0.0).astype(half) for v in values], axis=0))

    delta[...] = own_part(0)

    @pl.loop(1, pl.cdiv(count_ref[0], own_group))
    def _(p):
        delta[...] += own_part(p)

    width = line_ref.shape[1]
    group = width // 128
    place = (
        (x_halo, 0, 2 * cy),
        (x_halo, 2 * cy, 3 * cy),
        (y_halo, 0, 2 * planes),
        (y_halo, 2 * planes, 3 * planes),
        (y_halo, 5 * planes, 8),
        (y_halo, 5 * planes, 8),
    )
    for q, (target, first, height) in enumerate(place):

        @pl.loop(0, pl.cdiv(count_ref[q + 1], group))
        def _(p, q=q, target=target, first=first, height=height):
            row = q * (capacity // group) + p

            @pl.when(count_ref[len(NEAR) + row] > 0)
            def _():
                values = values_of((q + 1) * capacity + p * group, group)
                at = iota((height, width), 0) == line_ref[pl.ds(row, 1), :]
                hot = (iota((cz, width), 0) == depth_ref[pl.ds(row, 1), :]).astype(f32).astype(half)
                got = times(jnp.concatenate([jnp.where(at, v, 0.0) for v in values], axis=0).astype(half), hot)
                for s in range(ns):
                    target[s, first : first + height] += got[s * height : (s + 1) * height]

    def plane(s, c, i):
        return delta[pl.ds(pl.multiple_of((c * planes + i) * cy, 8), cy), s * cz : (s + 1) * cz]

    for s in range(ns):
        ex, ey, ez = (x_halo[s, (2 + c) * cy : (3 + c) * cy] for c in range(3))
        corner = y_halo[s, 5 * planes : 5 * planes + 1]
        back_z[s] = plane(s, 1, 0) - (ey + (ahead(ex, 0, corner) - ex))
        back_y[s] = (ez + (ahead(ex, 1) - ex)) - plane(s, 2, 0)

    @pl.loop(0, planes)
    def _(i):
        last = i == planes - 1
        after = jnp.minimum(i + 1, planes - 1)
        scaled = OMEGA_SQ * perm_ref[i].astype(f32)
        for copy in copies_in(i):
            copy.wait()
        for s in range(ns):
            own = [plane(s, c, i) for c in range(3)]
            beyond = [jnp.where(last, x_halo[s, c * cy : (c + 1) * cy], plane(s, c + 1, after)) for c in range(2)]
            y_row_x = y_halo[s, pl.ds(i, 1), :]
            y_row_z = y_halo[s, pl.ds(planes + i, 1), :]
            hx, hy, hz = (y_halo[s, pl.ds((2 + c) * planes + i, 1), :] for c in range(3))
            hy_after = jnp.where(
                last, y_halo[s, 5 * planes + 1 : 5 * planes + 2], y_halo[s, pl.ds(3 * planes + after, 1), :]
            )
            curls = curl_plane(
                own,
                beyond,
                back_z[s],
                back_y[s],
                y_row_x,
                y_row_z,
                (hx + (hy_after - hy)) - own[0],
                own[2] - (hz + (ahead(hy, 1) - hy)),
            )
            for c in range(3):
                field[s, c, i] += own[c]
                residual[s, c, i] -= curls[c] - scaled * own[c]
            back_z[s], back_y[s] = curls[3], curls[4]
        for copy in copies_out(i):
            copy.start()

    @pl.loop(0, planes)
    def _(i):
        for copy in copies_out(i):
            copy.wait()


def correct(field, residual, permittivity, counts, own_line, own_depth, line, depth, values):
    ns, _, cx, cy, cz = field.shape
    anywhere = pl.BlockSpec(memory_space=pl.ANY)
    whole = lambda x: pl.BlockSpec(x.shape, lambda g, *_: (0,) * x.ndim)
    y_lines = 5 * cx + 8
    grid_spec = pltpu.PrefetchScalarGridSpec(
        num_scalar_prefetch=1,
        grid=(1,),
        in_specs=[
            anywhere,
            anywhere,
            *[whole(x) for x in (permittivity, own_line, own_depth, line, depth, values)],
        ],
        out_specs=[anywhere, anywhere],
        scratch_shapes=[
            pltpu.VMEM(values.shape, jnp.float32),
            pltpu.VMEM(field.shape, jnp.float32),
            pltpu.VMEM(field.shape, jnp.float32),
            pltpu.VMEM((3 * cx * cy, ns * cz), jnp.float32),
            pltpu.VMEM((ns, 5 * cy, cz), jnp.float32),
            pltpu.VMEM((ns, y_lines, cz), jnp.float32),
            pltpu.VMEM((ns, cy, cz), jnp.float32),
            pltpu.VMEM((ns, cy, cz), jnp.float32),
            pltpu.SemaphoreType.DMA((2, cx)),
            pltpu.SemaphoreType.DMA((2, cx)),
        ],
    )
    return pl.pallas_call(
        correct_kernel,
        grid_spec=grid_spec,
        out_shape=[jax.ShapeDtypeStruct(field.shape, jnp.float32)] * 2,
        compiler_params=pltpu.CompilerParams(vmem_limit_bytes=60 * MIB),
        name="correct",
    )(counts, field, residual, permittivity, own_line, own_depth, line, depth, values)


def block_rows_of(inverses, wide_count, block_rows):
    per_device = sum(inv.shape[0] * inv.shape[1] for inv in inverses) // block_rows
    table, base = [], 0
    for inv in inverses:
        per = inv.shape[1] // block_rows
        for f in range(inv.shape[0]):
            b = np.arange(per * wide_count)
            table.append(b // per * per_device + base + f * per + b % per)
        base += inv.shape[0] * per
    return np.concatenate(table).astype(np.int32)


def block_columns_of(inverses, narrow_count, block_rows):
    table, base = [], 0
    for inv in inverses:
        per = inv.shape[2] // block_rows
        for _ in range(inv.shape[0]):
            table.append(base + np.arange(per * narrow_count).reshape(narrow_count, per))
            base += per * narrow_count
    return np.concatenate(table, axis=1).astype(np.int32)


def to_all_wide(block, wide_count):
    spread = jnp.broadcast_to(block[None], (wide_count, *block.shape)).reshape(-1, *block.shape[1:])
    return lax.all_to_all(spread, "wide", 0, 0, tiled=True)


def on_device(solution, source_term, permittivity, inv_top, inv_mid, inv_low, sep_tile, sep_cell):
    wide_count, narrow_count = lax.axis_size("wide"), lax.axis_size("narrow")
    my_wide, my_narrow = lax.axis_index("wide"), lax.axis_index("narrow")
    ns, _, cx, cy, cz = solution.shape
    block_count, block_rows = sep_cell.shape
    capacity = max(2, 2 * block_count // (wide_count * narrow_count))
    inverses = (inv_top[None], inv_mid, inv_low)

    y_rows = lax.all_gather(outer_rows(solution), "narrow", axis=0, tiled=False)
    to_up, to_down = outer_planes(solution, y_rows)
    steps = [(w, w + 1) for w in range(wide_count - 1)]
    up = lax.ppermute(to_up, "wide", steps)
    down = lax.ppermute(to_down, "wide", [(b, a) for a, b in steps])
    inner, inner_lines = inner_residual(solution, source_term, permittivity, y_rows)

    block_tile = sep_tile[:, 0]
    block_ids = jnp.arange(block_count, dtype=jnp.int32)
    slot_rank = jnp.sum(
        jnp.logical_and(
            block_tile[:, None] == block_tile[None, :], block_ids[None, :] < block_ids[:, None]
        ).astype(jnp.int32),
        axis=1,
    )
    offsets = np.array(NEAR, np.int32)
    near_wide, near_narrow = my_wide + offsets[:, 0], my_narrow + offsets[:, 1]
    inside = (near_wide >= 0) & (near_wide < wide_count) & (near_narrow >= 0) & (near_narrow < narrow_count)
    near_tile = jnp.where(inside, near_wide * narrow_count + near_narrow, -1)
    named = block_tile[None, :] == near_tile[:, None]
    counts = jnp.sum(named.astype(jnp.int32), axis=1)
    slots = jnp.arange(capacity, dtype=jnp.int32)
    match = jnp.logical_and(named[:, None, :], slot_rank[None, None, :] == slots[None, :, None])
    near_ids = jnp.sum(jnp.where(match, block_ids[None, None, :], 0), axis=2)
    near_rows = jnp.sum(
        jnp.where(match, block_rows_of(inverses, wide_count, block_rows)[None, None, :], 0), axis=2
    )
    found = slots[None, :] < counts[:, None]
    cells = sep_cell.at[near_ids.reshape(-1)].get(mode="promise_in_bounds").reshape(len(NEAR), capacity, block_rows)
    depth = cells % cz
    row = cells // cz
    part, at_i, at_j = row // (cx * cy), row // cy % cx, row % cy
    rule = (
        (row, row >= 0),
        ((part - 1) * cy + at_j, (part >= 1) & (at_i == 0)),
        (part * cy + at_j, at_i == cx - 1),
        (part // 2 * cx + at_i, (part != 1) & (at_j == 0)),
        (part * cx + at_i, at_j == cy - 1),
        (jnp.zeros_like(row), (part == 0) & (at_i == cx - 1) & (at_j == 0)),
        (jnp.ones_like(row), (part == 1) & (at_i == 0) & (at_j == cy - 1)),
    )
    line = jnp.stack(
        [jnp.where(found[q, :, None] & keep[q], at[q], -1) for q, (at, keep) in enumerate(rule)]
    )
    arrives = (block_tile % narrow_count * wide_count + block_tile // narrow_count) * capacity + slot_rank
    table = block_columns_of(inverses, narrow_count, block_rows)
    held_at = jnp.sum(
        jnp.where(
            (table[:, :, None] == block_ids) & (np.arange(narrow_count)[:, None, None] == my_narrow), arrives, 0
        ),
        axis=(0, 2),
    )
    own_width, width = min(8, capacity) * block_rows, min(4, capacity) * block_rows
    own_line, own_depth = line[0].reshape(-1, own_width), depth[0].reshape(-1, own_width)
    line, depth = line[1:].reshape(-1, width), depth[1:].reshape(-1, width)
    loads = jnp.concatenate([counts, jnp.max(line, axis=1) + 1])

    residual, picked = outer_residual_and_gather(
        wide_count, solution, source_term, permittivity, counts, y_rows, up, down, inner, inner_lines, own_line, own_depth
    )
    column = lax.all_to_all(picked.reshape(-1, ns * block_rows), "wide", 0, 0, tiled=True)
    everyone = lax.all_gather(column, "narrow", axis=0, tiled=True)
    columns = everyone.at[held_at].get(mode="promise_in_bounds")
    partial = fronts(columns, inverses)
    rows = partial.shape[1]
    shares = lax.all_gather(partial, "narrow", axis=0, tiled=False)
    summed = jnp.sum(shares.astype(jnp.float32), axis=0).astype(jnp.bfloat16)
    summed = summed.transpose(1, 0, 2).reshape(rows, ns * block_rows)
    updates = to_all_wide(summed, wide_count)

    values = updates.at[near_rows.reshape(-1)].get(mode="promise_in_bounds")
    return tuple(correct(solution, residual, permittivity, loads, own_line, own_depth, line, depth, values))


def solution(mesh):
    return jax.shard_map(
        on_device,
        mesh=mesh,
        in_specs=(
            P(None, None, "wide", "narrow", None),
            P(None, None, "wide", "narrow", None),
            P("wide", "narrow", None),
            P("wide", "narrow"),
            P(None, "wide", "narrow"),
            P(None, "wide", "narrow"),
            P(),
            P(),
        ),
        out_specs=(P(None, None, "wide", "narrow", None), P(None, None, "wide", "narrow", None)),
        check_vma=False,
    )
```

```python
import jax
import jax.numpy as jnp
import numpy as np
from jax import lax
from jax.experimental import pallas as pl
from jax.experimental.pallas import tpu as pltpu
from jax.sharding import PartitionSpec as P

OMEGA_SQ = 0.5
MIB = 1 << 20

NEAR = ((0, 0), (1, 0), (-1, 0), (0, 1), (0, -1), (-1, 1), (1, -1))


def iota(shape, dim):
    return lax.broadcasted_iota(jnp.int32, shape, dim)


def lane_blocks(x):
    return [x[:, at : at + 128] for at in range(0, x.shape[1], 128)]


def shifted(x, axis, step, edge):
    if axis == 1:
        size, blocks = 128, lane_blocks(x)
        fill = lane_blocks(jnp.broadcast_to(edge, x.shape))
        turned = [pltpu.roll(b, step % size, 1) for b in blocks]
        mask = iota((1, size), 1)
    else:
        size, tiles = 8, x.shape[0] // 8
        turned = pltpu.roll(x.reshape(tiles, size, x.shape[1]), step % size, 1)
        turned = [turned[t] for t in range(tiles)]
        filled = jnp.broadcast_to(edge, (size, x.shape[1])) if jnp.ndim(edge) == 0 or edge.shape[0] == 1 else edge
        fill = [filled[:size]] * tiles
        mask = iota((size, 1), 0)
    if step < 0:
        others = [*turned[1:], fill[-1]]
        mask = mask == size - 1
    else:
        others = [fill[0], *turned[:-1]]
        mask = mask == 0
    return jnp.concatenate([jnp.where(mask, o, t) for o, t in zip(others, turned, strict=True)], axis=axis)


def ahead(x, axis, edge=0.0):
    return shifted(x, axis, -1, edge)


def behind(x, axis, edge):
    return shifted(x, axis, 1, edge)


def staged(body, scalars, operands, small):
    def kernel(*refs):
        held, sem = refs[-1 - len(small) : -1], refs[-1]
        refs = list(refs[: -1 - len(small)])
        copies = []
        for k, n in enumerate(small):
            copies.append(pltpu.make_async_copy(refs[scalars + n], held[k], sem.at[k]))
            refs[scalars + n] = held[k]
        for copy in copies:
            copy.start()

        def ready():
            for copy in copies:
                copy.wait()

        body(ready, *refs)

    extra = [pltpu.VMEM(operands[n].shape, operands[n].dtype) for n in small]
    return kernel, [*extra, pltpu.SemaphoreType.DMA((len(small),))]


def rows_kernel(low_ref, high_ref, out_ref):
    top = high_ref.shape[3] - 1
    for s in range(out_ref.shape[0]):
        rows = [low_ref[s, 0, :, 0, :], low_ref[s, 2, :, 0, :], *(high_ref[s, c, :, top, :] for c in range(3))]
        for n, row in enumerate(rows):
            out_ref[s, n] = row.astype(out_ref.dtype)


def outer_rows(field):
    ns, _, cx, cy, cz = field.shape
    slab = (ns, 3, cx, 8, cz)
    return pl.pallas_call(
        rows_kernel,
        grid=(1,),
        in_specs=[
            pl.BlockSpec(slab, lambda g: (0, 0, 0, 0, 0)),
            pl.BlockSpec(slab, lambda g: (0, 0, 0, cy // 8 - 1, 0)),
        ],
        out_specs=pl.BlockSpec((ns, 5, cx, cz), lambda g: (0, 0, 0, 0)),
        out_shape=jax.ShapeDtypeStruct((ns, 5, cx, cz), jnp.bfloat16),
        compiler_params=pltpu.CompilerParams(vmem_limit_bytes=60 * MIB),
        name="outer_rows",
    )(field, field)


def beside(rows_ref):
    me, last = lax.axis_index("narrow"), rows_ref.shape[0] - 1
    return (jnp.maximum(me - 1, 0), me > 0), (jnp.minimum(me + 1, last), me < last)


def planes_kernel(first_ref, last_ref, rows_ref, up_ref, down_ref):
    planes, cy, dtype = rows_ref.shape[3], first_ref.shape[3], up_ref.dtype
    (before, has_before), (after, has_after) = beside(rows_ref)
    for s in range(up_ref.shape[0]):
        ex, ey, ez = (last_ref[s, c, 0] for c in range(3))
        past = jnp.where(has_after, rows_ref[after, s, 0].astype(jnp.float32)[planes - 1 :], 0.0)
        up_ref[s, :cy] = (ey + (ahead(ex, 0, past) - ex)).astype(dtype)
        up_ref[s, cy:] = (ez + (ahead(ex, 1) - ex)).astype(dtype)
        down_ref[s, :cy] = first_ref[s, 1, 0].astype(dtype)
        down_ref[s, cy : 2 * cy] = first_ref[s, 2, 0].astype(dtype)
        edge = jnp.where(has_before, rows_ref[before, s, 3].astype(jnp.float32)[:1], 0.0)
        down_ref[s, 2 * cy :] = jnp.broadcast_to(edge, (down_ref.shape[1] - 2 * cy, edge.shape[1])).astype(dtype)


def outer_planes(field, rows):
    ns, _, cx, cy, cz = field.shape
    plane = (ns, 3, 1, cy, cz)
    heights = (2 * cy, 2 * cy + 16)
    return pl.pallas_call(
        planes_kernel,
        grid=(1,),
        in_specs=[
            pl.BlockSpec(plane, lambda g: (0, 0, 0, 0, 0)),
            pl.BlockSpec(plane, lambda g: (0, 0, cx - 1, 0, 0)),
            pl.BlockSpec(rows.shape, lambda g: (0,) * 5),
        ],
        out_specs=[pl.BlockSpec((ns, h, cz), lambda g: (0, 0, 0)) for h in heights],
        out_shape=[jax.ShapeDtypeStruct((ns, h, cz), jnp.bfloat16) for h in heights],
        compiler_params=pltpu.CompilerParams(vmem_limit_bytes=60 * MIB),
        name="outer_planes",
    )(field, field, rows)


def curl_plane(own, beyond, back_z, back_y, y_row_x, y_row_z, y_edge_z, y_edge_x):
    ex, ey, ez = own
    hx = (ahead(ez, 0, y_row_z) - ez) - (ahead(ey, 1) - ey)
    hy = (ahead(ex, 1) - ex) - (beyond[1] - ez)
    hz = (beyond[0] - ey) - (ahead(ex, 0, y_row_x) - ex)
    cx = (hz - behind(hz, 0, y_edge_z)) - (hy - behind(hy, 1, ex))
    cy = (hx - behind(hx, 1, -ey)) - (hz - back_z)
    cz = (hy - back_y) - (hx - behind(hx, 0, y_edge_x))
    return cx, cy, cz, hz, hy


def magnetic(own, beyond, row_x):
    ex, ey, ez = own
    return (beyond[0] - ey) - (ahead(ex, 0, row_x) - ex), (ahead(ex, 1) - ex) - (beyond[1] - ez)


def spread_rows(rows_ref, scratch):
    before, after = beside(rows_ref)
    for s in range(scratch.shape[0]):
        for n in range(5):
            tile, there = after if n < 2 else before
            scratch[s, n] = jnp.where(there, rows_ref[tile, s, n].astype(jnp.float32), 0.0)


def residual_plane(s, i, own, beyond, back, rows, after, planes, at, scaled, lines):
    cy, cz = own[0].shape
    cx = rows.shape[2]
    row_x, row_z, ex, ey, ez = (rows[s, n, pl.ds(i, 1), :] for n in range(5))
    curls = curl_plane(
        own, beyond, back[0], back[1], row_x, row_z, (ex + (after - ey)) - own[0], own[2] - (ez + (ahead(ey, 1) - ey))
    )
    for c in range(3):
        value = planes[s, c, at] - (curls[c] - scaled * own[c])
        planes[s, c, at] = value
        first = pl.multiple_of((c * cx + i) * cy, 16)
        lines[pl.ds(first, cy), s * cz : (s + 1) * cz] = value.astype(jnp.bfloat16)
    return curls[3], curls[4]


def inner_kernel(
    sol_ref, src_ref, perm_ref, rows_ref, res_ref, out_ref,
    field, planes, lines, back_z, back_y, rows, field_sem, plane_sem, res_sem, line_sem,
):
    ns, _, cx, cy, _ = field.shape

    def field_copy(i):
        return pltpu.make_async_copy(sol_ref.at[:, :, i], field.at[:, :, i], field_sem.at[i])

    def plane_copy(i):
        return pltpu.make_async_copy(src_ref.at[:, :, i], planes.at[:, :, i], plane_sem.at[i])

    def res_copy(i):
        return pltpu.make_async_copy(planes.at[:, :, i], res_ref.at[:, :, i], res_sem.at[i])

    def line_copy(i, c):
        at = pl.ds(pl.multiple_of((c * cx + i) * cy, 16), cy)
        return pltpu.make_async_copy(lines.at[at], out_ref.at[at], line_sem.at[c, i])

    for i in range(cx):
        field_copy(i).start()
        if 0 < i < cx - 1:
            plane_copy(i).start()
    spread_rows(rows_ref, rows)
    field_copy(0).wait()
    field_copy(1).wait()
    for s in range(ns):
        first, second = ([field[s, c, i] for c in range(3)] for i in range(2))
        back_z[s], back_y[s] = magnetic(first, second[1:], rows[s, 0, :1])

    @pl.loop(1, cx - 1)
    def _(i):
        field_copy(i + 1).wait()
        plane_copy(i).wait()
        scaled = OMEGA_SQ * perm_ref[i].astype(jnp.float32)
        for s in range(ns):
            own = [field[s, c, i] for c in range(3)]
            beyond = [field[s, c + 1, i + 1] for c in range(2)]
            back_z[s], back_y[s] = residual_plane(
                s, i, own, beyond, (back_z[s], back_y[s]), rows, rows[s, 3, pl.ds(i + 1, 1), :], planes, i, scaled, lines
            )
        res_copy(i).start()
        for c in range(3):
            line_copy(i, c).start()

    @pl.loop(1, cx - 1)
    def _(i):
        res_copy(i).wait()
        for c in range(3):
            line_copy(i, c).wait()


def inner_residual(field, source, permittivity, y_rows):
    ns, _, cx, cy, cz = field.shape
    anywhere = pl.BlockSpec(memory_space=pl.ANY)
    dma = pltpu.SemaphoreType.DMA
    grid_spec = pl.GridSpec(
        grid=(1,),
        in_specs=[
            anywhere,
            anywhere,
            pl.BlockSpec((cx, cy, cz), lambda g: (0, 0, 0)),
            pl.BlockSpec(y_rows.shape, lambda g: (0,) * 5),
        ],
        out_specs=[anywhere, anywhere],
        scratch_shapes=[
            pltpu.VMEM(field.shape, jnp.float32),
            pltpu.VMEM(field.shape, jnp.float32),
            pltpu.VMEM((3 * cx * cy, ns * cz), jnp.bfloat16),
            pltpu.VMEM((ns, cy, cz), jnp.float32),
            pltpu.VMEM((ns, cy, cz), jnp.float32),
            pltpu.VMEM((ns, 5, cx, cz), jnp.float32),
            dma((cx,)),
            dma((cx,)),
            dma((cx,)),
            dma((3, cx)),
        ],
    )
    return pl.pallas_call(
        inner_kernel,
        grid_spec=grid_spec,
        out_shape=[
            jax.ShapeDtypeStruct(field.shape, jnp.float32),
            jax.ShapeDtypeStruct((3 * cx * cy, ns * cz), jnp.bfloat16),
        ],
        compiler_params=pltpu.CompilerParams(vmem_limit_bytes=60 * MIB),
        cost_estimate=pl.CostEstimate(flops=60 * field.size, bytes_accessed=14 * field.size, transcendentals=0),
        name="inner_residual",
    )(field, source, permittivity, y_rows)


def gather_kernel(
    ready, count_ref, sol_ref, src_ref, perm_ref, rows_ref, up_ref, down_ref, inner_ref, line_ref, depth_ref, _,
    res_ref, out_ref, field, planes, lines, turned, rows, got_ref, field_sem, plane_sem, line_sem,
):
    ns, _, cx, cy, cz = sol_ref.shape
    total = lines.shape[0]
    f32 = jnp.float32
    ends = (0, cx - 1)
    field_copies = [
        pltpu.make_async_copy(sol_ref.at[:, :, i], field.at[:, :, n], field_sem.at[n])
        for n, i in enumerate((0, 1, cx - 2, cx - 1))
    ]
    plane_copies = [
        pltpu.make_async_copy(src_ref.at[:, :, i], planes.at[:, :, n], plane_sem.at[n]) for n, i in enumerate(ends)
    ]
    line_copies = []
    for c in range(3):
        at = pl.ds((c * cx + 1) * cy, (cx - 2) * cy)
        line_copies.append(pltpu.make_async_copy(inner_ref.at[at], lines.at[at], line_sem.at[c]))
    res_copies = [
        pltpu.make_async_copy(planes.at[:, :, n], res_ref.at[:, :, i], plane_sem.at[n]) for n, i in enumerate(ends)
    ]
    for copy in field_copies[:2] + plane_copies[:1] + field_copies[2:] + plane_copies[1:] + line_copies:
        copy.start()
    ready()
    spread_rows(rows_ref, rows)
    got_ref[...] = jnp.zeros_like(got_ref)

    for copy in field_copies[:2] + plane_copies[:1]:
        copy.wait()
    scaled = OMEGA_SQ * perm_ref[0].astype(f32)
    for s in range(ns):
        own = [field[s, c, 0] for c in range(3)]
        back = own[1] - up_ref[s, :cy].astype(f32), up_ref[s, cy:].astype(f32) - own[2]
        beyond = [field[s, c + 1, 1] for c in range(2)]
        residual_plane(s, 0, own, beyond, back, rows, rows[s, 3, 1:2], planes, 0, scaled, lines)
    res_copies[0].start()

    for copy in field_copies[2:] + plane_copies[1:]:
        copy.wait()
    scaled = OMEGA_SQ * perm_ref[cx - 1].astype(f32)
    for s in range(ns):
        own = [field[s, c, 3] for c in range(3)]
        back = magnetic([field[s, c, 2] for c in range(3)], own[1:], rows[s, 0, cx - 2 : cx - 1])
        beyond = [down_ref[s, c * cy : (c + 1) * cy].astype(f32) for c in range(2)]
        after = down_ref[s, 2 * cy :].astype(f32)[:1]
        residual_plane(s, cx - 1, own, beyond, back, rows, after, planes, 1, scaled, lines)
    res_copies[1].start()

    for copy in line_copies:
        copy.wait()
    for a in range(total // 128):
        for b in range(ns * cz // 128):
            turned[b * 128 : (b + 1) * 128, a * 128 : (a + 1) * 128] = lines[
                a * 128 : (a + 1) * 128, b * 128 : (b + 1) * 128
            ].T
    group, width = got_ref.shape[1], line_ref.shape[1]

    @pl.loop(0, pl.cdiv(count_ref[0], group))
    def _(p):
        hot = (iota((total, width), 0) == line_ref[pl.ds(p, 1), :]).astype(f32).astype(jnp.bfloat16)
        got = jnp.dot(turned[...], hot, preferred_element_type=f32)
        at = iota((cz, width), 0) == depth_ref[pl.ds(p, 1), :]
        for s in range(ns):
            sums = jnp.sum(jnp.where(at, got[s * cz : (s + 1) * cz], 0.0), axis=0, keepdims=True)
            for h in range(group):
                got_ref[p, h : h + 1, s * 128 : (s + 1) * 128] = sums[:, h * 128 : (h + 1) * 128]

    picked = got_ref[...].reshape(out_ref.shape[1:]).astype(out_ref.dtype)
    for w in range(out_ref.shape[0]):
        out_ref[w] = picked
    for copy in res_copies:
        copy.wait()


def outer_residual_and_gather(copies, field, source, permittivity, counts, y_rows, up, down, residual, inner, line, depth):
    ns, _, cx, cy, cz = field.shape
    total = 3 * cx * cy
    groups, group = line.shape[0], line.shape[1] // 128
    operands = field, source, permittivity, y_rows, up, down, inner, line, depth, residual
    kernel, extra = staged(gather_kernel, 1, operands, (2, 3, 4, 5, 7, 8))
    anywhere = pl.BlockSpec(memory_space=pl.ANY)
    dma = pltpu.SemaphoreType.DMA
    grid_spec = pltpu.PrefetchScalarGridSpec(
        num_scalar_prefetch=1,
        grid=(1,),
        in_specs=[anywhere] * 10,
        out_specs=[anywhere, pl.BlockSpec((copies, groups * group, ns * 128), lambda g, *_: (0, 0, 0))],
        scratch_shapes=[
            pltpu.VMEM((ns, 3, 4, cy, cz), jnp.float32),
            pltpu.VMEM((ns, 3, 2, cy, cz), jnp.float32),
            pltpu.VMEM((total, ns * cz), jnp.bfloat16),
            pltpu.VMEM((ns * cz, total), jnp.bfloat16),
            pltpu.VMEM((ns, 5, cx, cz), jnp.float32),
            pltpu.VMEM((groups, group, ns * 128), jnp.float32),
            dma((4,)),
            dma((2,)),
            dma((3,)),
            *extra,
        ],
    )
    return pl.pallas_call(
        kernel,
        grid_spec=grid_spec,
        out_shape=[
            jax.ShapeDtypeStruct(field.shape, jnp.float32),
            jax.ShapeDtypeStruct((copies, groups * group, ns * 128), jnp.bfloat16),
        ],
        input_output_aliases={10: 0},
        compiler_params=pltpu.CompilerParams(vmem_limit_bytes=60 * MIB),
        name="outer_residual_gather",
    )(counts, *operands)


def fronts_kernel(at_ref, given_ref, top_ref, mid_ref, low_ref, y_ref, top_buf, mid_buf, low_buf, given, x_buf, y_buf, sem):
    ns = y_buf.shape[0]
    jobs, base, column = [], 0, 0
    for w_ref, buf in ((top_ref, top_buf), (mid_ref, mid_buf), (low_ref, low_buf)):
        count, height, width = w_ref.shape
        rows = height
        while rows > 256 and rows * width * 2 > 4 * MIB:
            rows //= 2
        for f in range(count):
            for r in range(0, height, rows):
                at = pl.ds(r, rows)
                copy = pltpu.make_async_copy(w_ref.at[f, at], buf.at[f, at], sem.at[len(jobs)])
                jobs.append((copy, buf, f, at, slice(column, column + width), (base + r) // 128))
            base += height
            column += width
    for job in jobs:
        job[0].start()
    given[...] = given_ref[...].astype(jnp.float32)
    for b in range(x_buf.shape[1] // 128):
        row = given[pl.ds(at_ref[b], 1), :]
        for s in range(ns):
            x_buf[s : s + 1, b * 128 : (b + 1) * 128] = row[:, s * 128 : (s + 1) * 128]
    for copy, buf, f, at, lanes, first in jobs:
        copy.wait()
        got = lax.dot_general(
            x_buf[:, lanes].astype(jnp.bfloat16),
            buf[f, at],
            (((1,), (1,)), ((), ())),
            preferred_element_type=jnp.float32,
        )
        for b in range(got.shape[1] // 128):
            for s in range(ns):
                y_buf[s, first + b : first + b + 1] = got[s : s + 1, b * 128 : (b + 1) * 128]
    y_ref[...] = y_buf[...].astype(y_ref.dtype)


def fronts(held_at, everyone, inverses):
    ns = everyone.shape[1] // 128
    blocks = sum(inv.shape[0] * inv.shape[1] for inv in inverses) // 128
    entries = sum(inv.size for inv in inverses)
    there = pl.BlockSpec(memory_space=pl.ANY)
    grid_spec = pltpu.PrefetchScalarGridSpec(
        num_scalar_prefetch=1,
        grid=(1,),
        in_specs=[pl.BlockSpec(everyone.shape, lambda g, _: (0, 0))] + [there] * 3,
        out_specs=pl.BlockSpec((ns, blocks, 128), lambda g, _: (0, 0, 0)),
        scratch_shapes=[
            *[pltpu.VMEM(inv.shape, inv.dtype) for inv in inverses],
            pltpu.VMEM(everyone.shape, jnp.float32),
            pltpu.VMEM((ns, held_at.shape[0] * 128), jnp.float32),
            pltpu.VMEM((ns, blocks, 128), jnp.float32),
            pltpu.SemaphoreType.DMA((64,)),
        ],
    )
    return pl.pallas_call(
        fronts_kernel,
        grid_spec=grid_spec,
        out_shape=jax.ShapeDtypeStruct((ns, blocks, 128), jnp.bfloat16),
        compiler_params=pltpu.CompilerParams(vmem_limit_bytes=60 * MIB),
        cost_estimate=pl.CostEstimate(flops=4 * entries, bytes_accessed=2 * entries, transcendentals=0),
        name="fronts",
    )(held_at, everyone, *inverses)


def correct_kernel(
    count_ref, sol_ref, res_ref, perm_ref, own_line_ref, own_depth_ref, line_ref, depth_ref, given_ref,
    out_ref, new_ref, value_ref, field, residual, delta, x_halo, y_halo, back_z, back_y, in_sem, out_sem,
):
    ns, _, planes, cy, cz = sol_ref.shape
    f32, half = jnp.float32, jnp.bfloat16

    def copies_in(i):
        return [
            pltpu.make_async_copy(ref.at[:, :, i], buf.at[:, :, i], in_sem.at[n, i])
            for n, (ref, buf) in enumerate(((sol_ref, field), (res_ref, residual)))
        ]

    def copies_out(i):
        return [
            pltpu.make_async_copy(buf.at[:, :, i], ref.at[:, :, i], out_sem.at[n, i])
            for n, (ref, buf) in enumerate(((out_ref, field), (new_ref, residual)))
        ]

    for i in range(planes):
        for copy in copies_in(i):
            copy.start()
    chunks = line_ref.shape[0]
    capacity = chunks // (len(NEAR) - 1) * (line_ref.shape[1] // 128)

    def values_of(first, count):
        rows = [value_ref[pl.ds(count_ref[len(NEAR) + chunks + first + h], 1), :] for h in range(count)]
        return [jnp.concatenate([v[:, s * 128 : (s + 1) * 128] for v in rows], axis=1) for s in range(ns)]

    def times(a, b):
        return lax.dot_general(a, b, (((1,), (1,)), ((), ())), preferred_element_type=f32)

    value_ref[...] = given_ref[...].astype(f32)
    x_halo[...] = jnp.zeros_like(x_halo)
    y_halo[...] = jnp.zeros_like(y_halo)
    own_width = own_line_ref.shape[1]
    own_group = own_width // 128

    def own_part(p):
        values = values_of(p * own_group, own_group)
        hot = (iota((delta.shape[0], own_width), 0) == own_line_ref[pl.ds(p, 1), :]).astype(f32).astype(half)
        at = iota((cz, own_width), 0) == own_depth_ref[pl.ds(p, 1), :]
        return times(hot, jnp.concatenate([jnp.where(at, v, 0.0).astype(half) for v in values], axis=0))

    delta[...] = own_part(0)

    @pl.loop(1, pl.cdiv(count_ref[0], own_group))
    def _(p):
        delta[...] += own_part(p)

    width = line_ref.shape[1]
    group = width // 128
    place = (
        (x_halo, 0, 2 * cy),
        (x_halo, 2 * cy, 3 * cy),
        (y_halo, 0, 2 * planes),
        (y_halo, 2 * planes, 3 * planes),
        (y_halo, 5 * planes, 8),
        (y_halo, 5 * planes, 8),
    )
    for q, (target, first, height) in enumerate(place):

        @pl.loop(0, pl.cdiv(count_ref[q + 1], group))
        def _(p, q=q, target=target, first=first, height=height):
            row = q * (capacity // group) + p

            @pl.when(count_ref[len(NEAR) + row] > 0)
            def _():
                values = values_of((q + 1) * capacity + p * group, group)
                at = iota((height, width), 0) == line_ref[pl.ds(row, 1), :]
                hot = (iota((cz, width), 0) == depth_ref[pl.ds(row, 1), :]).astype(f32).astype(half)
                got = times(jnp.concatenate([jnp.where(at, v, 0.0) for v in values], axis=0).astype(half), hot)
                for s in range(ns):
                    target[s, first : first + height] += got[s * height : (s + 1) * height]

    def plane(s, c, i):
        return delta[pl.ds(pl.multiple_of((c * planes + i) * cy, 8), cy), s * cz : (s + 1) * cz]

    for s in range(ns):
        ex, ey, ez = (x_halo[s, (2 + c) * cy : (3 + c) * cy] for c in range(3))
        corner = y_halo[s, 5 * planes : 5 * planes + 1]
        back_z[s] = plane(s, 1, 0) - (ey + (ahead(ex, 0, corner) - ex))
        back_y[s] = (ez + (ahead(ex, 1) - ex)) - plane(s, 2, 0)

    @pl.loop(0, planes)
    def _(i):
        last = i == planes - 1
        after = jnp.minimum(i + 1, planes - 1)
        scaled = OMEGA_SQ * perm_ref[i].astype(f32)
        for copy in copies_in(i):
            copy.wait()
        for s in range(ns):
            own = [plane(s, c, i) for c in range(3)]
            beyond = [jnp.where(last, x_halo[s, c * cy : (c + 1) * cy], plane(s, c + 1, after)) for c in range(2)]
            y_row_x = y_halo[s, pl.ds(i, 1), :]
            y_row_z = y_halo[s, pl.ds(planes + i, 1), :]
            hx, hy, hz = (y_halo[s, pl.ds((2 + c) * planes + i, 1), :] for c in range(3))
            hy_after = jnp.where(
                last, y_halo[s, 5 * planes + 1 : 5 * planes + 2], y_halo[s, pl.ds(3 * planes + after, 1), :]
            )
            curls = curl_plane(
                own,
                beyond,
                back_z[s],
                back_y[s],
                y_row_x,
                y_row_z,
                (hx + (hy_after - hy)) - own[0],
                own[2] - (hz + (ahead(hy, 1) - hy)),
            )
            for c in range(3):
                field[s, c, i] += own[c]
                residual[s, c, i] -= curls[c] - scaled * own[c]
            back_z[s], back_y[s] = curls[3], curls[4]
        for copy in copies_out(i):
            copy.start()

    @pl.loop(0, planes)
    def _(i):
        for copy in copies_out(i):
            copy.wait()


def correct(field, residual, permittivity, counts, own_line, own_depth, line, depth, updates):
    ns, _, cx, cy, cz = field.shape
    anywhere = pl.BlockSpec(memory_space=pl.ANY)
    whole = lambda x: pl.BlockSpec(x.shape, lambda g, *_: (0,) * x.ndim)
    y_lines = 5 * cx + 8
    grid_spec = pltpu.PrefetchScalarGridSpec(
        num_scalar_prefetch=1,
        grid=(1,),
        in_specs=[
            anywhere,
            anywhere,
            *[whole(x) for x in (permittivity, own_line, own_depth, line, depth, updates)],
        ],
        out_specs=[anywhere, anywhere],
        scratch_shapes=[
            pltpu.VMEM(updates.shape, jnp.float32),
            pltpu.VMEM(field.shape, jnp.float32),
            pltpu.VMEM(field.shape, jnp.float32),
            pltpu.VMEM((3 * cx * cy, ns * cz), jnp.float32),
            pltpu.VMEM((ns, 5 * cy, cz), jnp.float32),
            pltpu.VMEM((ns, y_lines, cz), jnp.float32),
            pltpu.VMEM((ns, cy, cz), jnp.float32),
            pltpu.VMEM((ns, cy, cz), jnp.float32),
            pltpu.SemaphoreType.DMA((2, cx)),
            pltpu.SemaphoreType.DMA((2, cx)),
        ],
    )
    return pl.pallas_call(
        correct_kernel,
        grid_spec=grid_spec,
        out_shape=[jax.ShapeDtypeStruct(field.shape, jnp.float32)] * 2,
        compiler_params=pltpu.CompilerParams(vmem_limit_bytes=60 * MIB),
        name="correct",
    )(counts, field, residual, permittivity, own_line, own_depth, line, depth, updates)


def block_rows_of(inverses, wide_count, block_rows):
    per_device = sum(inv.shape[0] * inv.shape[1] for inv in inverses) // block_rows
    table, base = [], 0
    for inv in inverses:
        per = inv.shape[1] // block_rows
        for f in range(inv.shape[0]):
            b = np.arange(per * wide_count)
            table.append(b // per * per_device + base + f * per + b % per)
        base += inv.shape[0] * per
    return np.concatenate(table).astype(np.int32)


def block_columns_of(inverses, narrow_count, block_rows):
    table, base = [], 0
    for inv in inverses:
        per = inv.shape[2] // block_rows
        for _ in range(inv.shape[0]):
            table.append(base + np.arange(per * narrow_count).reshape(narrow_count, per))
            base += per * narrow_count
    return np.concatenate(table, axis=1).astype(np.int32)


def to_all_wide(block, wide_count):
    spread = jnp.broadcast_to(block[None], (wide_count, *block.shape)).reshape(-1, *block.shape[1:])
    return lax.all_to_all(spread, "wide", 0, 0, tiled=True)


def on_device(solution, source_term, permittivity, inv_top, inv_mid, inv_low, sep_tile, sep_cell):
    wide_count, narrow_count = lax.axis_size("wide"), lax.axis_size("narrow")
    my_wide, my_narrow = lax.axis_index("wide"), lax.axis_index("narrow")
    ns, _, cx, cy, cz = solution.shape
    block_count, block_rows = sep_cell.shape
    capacity = max(2, 2 * block_count // (wide_count * narrow_count))
    inverses = (inv_top[None], inv_mid, inv_low)

    y_rows = lax.all_gather(outer_rows(solution), "narrow", axis=0, tiled=False)
    to_up, to_down = outer_planes(solution, y_rows)
    steps = [(w, w + 1) for w in range(wide_count - 1)]
    up = lax.ppermute(to_up, "wide", steps)
    down = lax.ppermute(to_down, "wide", [(b, a) for a, b in steps])
    inner, inner_lines = inner_residual(solution, source_term, permittivity, y_rows)

    block_tile = sep_tile[:, 0]
    block_ids = jnp.arange(block_count, dtype=jnp.int32)
    slot_rank = jnp.sum(
        jnp.logical_and(
            block_tile[:, None] == block_tile[None, :], block_ids[None, :] < block_ids[:, None]
        ).astype(jnp.int32),
        axis=1,
    )
    offsets = np.array(NEAR, np.int32)
    near_wide, near_narrow = my_wide + offsets[:, 0], my_narrow + offsets[:, 1]
    inside = (near_wide >= 0) & (near_wide < wide_count) & (near_narrow >= 0) & (near_narrow < narrow_count)
    near_tile = jnp.where(inside, near_wide * narrow_count + near_narrow, -1)
    named = block_tile[None, :] == near_tile[:, None]
    counts = jnp.sum(named.astype(jnp.int32), axis=1)
    slots = jnp.arange(capacity, dtype=jnp.int32)
    match = jnp.logical_and(named[:, None, :], slot_rank[None, None, :] == slots[None, :, None])
    near_ids = jnp.sum(jnp.where(match, block_ids[None, None, :], 0), axis=2)
    near_rows = jnp.sum(
        jnp.where(match, block_rows_of(inverses, wide_count, block_rows)[None, None, :], 0), axis=2
    )
    found = slots[None, :] < counts[:, None]
    cells = sep_cell.at[near_ids.reshape(-1)].get(mode="promise_in_bounds").reshape(len(NEAR), capacity, block_rows)
    depth = cells % cz
    row = cells // cz
    part, at_i, at_j = row // (cx * cy), row // cy % cx, row % cy
    rule = (
        (row, row >= 0),
        ((part - 1) * cy + at_j, (part >= 1) & (at_i == 0)),
        (part * cy + at_j, at_i == cx - 1),
        (part // 2 * cx + at_i, (part != 1) & (at_j == 0)),
        (part * cx + at_i, at_j == cy - 1),
        (jnp.zeros_like(row), (part == 0) & (at_i == cx - 1) & (at_j == 0)),
        (jnp.ones_like(row), (part == 1) & (at_i == 0) & (at_j == cy - 1)),
    )
    line = jnp.stack(
        [jnp.where(found[q, :, None] & keep[q], at[q], -1) for q, (at, keep) in enumerate(rule)]
    )
    arrives = (block_tile % narrow_count * wide_count + block_tile // narrow_count) * capacity + slot_rank
    table = block_columns_of(inverses, narrow_count, block_rows)
    held_at = jnp.sum(
        jnp.where(
            (table[:, :, None] == block_ids) & (np.arange(narrow_count)[:, None, None] == my_narrow), arrives, 0
        ),
        axis=(0, 2),
    )
    own_width, width = min(8, capacity) * block_rows, min(4, capacity) * block_rows
    own_line, own_depth = line[0].reshape(-1, own_width), depth[0].reshape(-1, own_width)
    line, depth = line[1:].reshape(-1, width), depth[1:].reshape(-1, width)
    loads = jnp.concatenate([counts, jnp.max(line, axis=1) + 1, near_rows.reshape(-1)])

    residual, picked = outer_residual_and_gather(
        wide_count, solution, source_term, permittivity, counts, y_rows, up, down, inner, inner_lines, own_line, own_depth
    )
    column = lax.all_to_all(picked.reshape(-1, ns * block_rows), "wide", 0, 0, tiled=True)
    everyone = lax.all_gather(column, "narrow", axis=0, tiled=True)
    partial = fronts(held_at, everyone, inverses)
    rows = partial.shape[1]
    shares = lax.all_gather(partial, "narrow", axis=0, tiled=False)
    summed = jnp.sum(shares.astype(jnp.float32), axis=0).astype(jnp.bfloat16)
    summed = summed.transpose(1, 0, 2).reshape(rows, ns * block_rows)
    updates = to_all_wide(summed, wide_count)

    return tuple(correct(solution, residual, permittivity, loads, own_line, own_depth, line, depth, updates))


def solution(mesh):
    return jax.shard_map(
        on_device,
        mesh=mesh,
        in_specs=(
            P(None, None, "wide", "narrow", None),
            P(None, None, "wide", "narrow", None),
            P("wide", "narrow", None),
            P("wide", "narrow"),
            P(None, "wide", "narrow"),
            P(None, "wide", "narrow"),
            P(),
            P(),
        ),
        out_specs=(P(None, None, "wide", "narrow", None), P(None, None, "wide", "narrow", None)),
        check_vma=False,
    )
```

```python
import jax
import jax.numpy as jnp
import numpy as np
from jax import lax
from jax.experimental import pallas as pl
from jax.experimental.pallas import tpu as pltpu
from jax.sharding import PartitionSpec as P

OMEGA_SQ = 0.5
MIB = 1 << 20
OWN_GROUP, NEAR_GROUP = 8, 4

NEAR = ((0, 0), (1, 0), (-1, 0), (0, 1), (0, -1), (-1, 1), (1, -1))


def iota(shape, dim):
    return lax.broadcasted_iota(jnp.int32, shape, dim)


def lane_blocks(x):
    return [x[:, at : at + 128] for at in range(0, x.shape[1], 128)]


def shifted(x, axis, step, edge):
    if axis == 1:
        size, blocks = 128, lane_blocks(x)
        fill = lane_blocks(jnp.broadcast_to(edge, x.shape))
        turned = [pltpu.roll(b, step % size, 1) for b in blocks]
        mask = iota((1, size), 1)
    else:
        size, tiles = 8, x.shape[0] // 8
        turned = pltpu.roll(x.reshape(tiles, size, x.shape[1]), step % size, 1)
        turned = [turned[t] for t in range(tiles)]
        filled = jnp.broadcast_to(edge, (size, x.shape[1])) if jnp.ndim(edge) == 0 or edge.shape[0] == 1 else edge
        fill = [filled[:size]] * tiles
        mask = iota((size, 1), 0)
    if step < 0:
        others = [*turned[1:], fill[-1]]
        mask = mask == size - 1
    else:
        others = [fill[0], *turned[:-1]]
        mask = mask == 0
    return jnp.concatenate([jnp.where(mask, o, t) for o, t in zip(others, turned, strict=True)], axis=axis)


def ahead(x, axis, edge=0.0):
    return shifted(x, axis, -1, edge)


def behind(x, axis, edge):
    return shifted(x, axis, 1, edge)


def staged(body, scalars, operands, small):
    def kernel(*refs):
        held, sem = refs[-1 - len(small) : -1], refs[-1]
        refs = list(refs[: -1 - len(small)])
        copies = []
        for k, n in enumerate(small):
            copies.append(pltpu.make_async_copy(refs[scalars + n], held[k], sem.at[k]))
            refs[scalars + n] = held[k]
        for copy in copies:
            copy.start()

        def ready():
            for copy in copies:
                copy.wait()

        body(ready, *refs)

    extra = [pltpu.VMEM(operands[n].shape, operands[n].dtype) for n in small]
    return kernel, [*extra, pltpu.SemaphoreType.DMA((len(small),))]


def rows_kernel(low_ref, high_ref, out_ref):
    top = high_ref.shape[3] - 1
    for s in range(out_ref.shape[0]):
        rows = [low_ref[s, 0, :, 0, :], low_ref[s, 2, :, 0, :], *(high_ref[s, c, :, top, :] for c in range(3))]
        for n, row in enumerate(rows):
            out_ref[s, n] = row.astype(out_ref.dtype)


def joined(ref, first, count):
    return jnp.concatenate([ref[pl.ds(first + h, 1), :] for h in range(count)], axis=1)


def outer_rows(field):
    ns, _, cx, cy, cz = field.shape
    slab = (ns, 3, cx, 8, cz)
    return pl.pallas_call(
        rows_kernel,
        grid=(1,),
        in_specs=[
            pl.BlockSpec(slab, lambda g: (0, 0, 0, 0, 0)),
            pl.BlockSpec(slab, lambda g: (0, 0, 0, cy // 8 - 1, 0)),
        ],
        out_specs=pl.BlockSpec((ns, 5, cx, cz), lambda g: (0, 0, 0, 0)),
        out_shape=jax.ShapeDtypeStruct((ns, 5, cx, cz), jnp.bfloat16),
        compiler_params=pltpu.CompilerParams(vmem_limit_bytes=58 * MIB),
        name="outer_rows",
    )(field, field)


def beside(rows_ref):
    me, last = lax.axis_index("narrow"), rows_ref.shape[0] - 1
    return (jnp.maximum(me - 1, 0), me > 0), (jnp.minimum(me + 1, last), me < last)


def planes_kernel(first_ref, last_ref, rows_ref, up_ref, down_ref):
    planes, cy, dtype = rows_ref.shape[3], first_ref.shape[3], up_ref.dtype
    (before, has_before), (after, has_after) = beside(rows_ref)
    for s in range(up_ref.shape[0]):
        ex, ey, ez = (last_ref[s, c, 0] for c in range(3))
        past = jnp.where(has_after, rows_ref[after, s, 0].astype(jnp.float32)[planes - 1 :], 0.0)
        up_ref[s, :cy] = (ey + (ahead(ex, 0, past) - ex)).astype(dtype)
        up_ref[s, cy:] = (ez + (ahead(ex, 1) - ex)).astype(dtype)
        down_ref[s, :cy] = first_ref[s, 1, 0].astype(dtype)
        down_ref[s, cy : 2 * cy] = first_ref[s, 2, 0].astype(dtype)
        edge = jnp.where(has_before, rows_ref[before, s, 3].astype(jnp.float32)[:1], 0.0)
        down_ref[s, 2 * cy :] = jnp.broadcast_to(edge, (down_ref.shape[1] - 2 * cy, edge.shape[1])).astype(dtype)


def outer_planes(field, rows):
    ns, _, cx, cy, cz = field.shape
    plane = (ns, 3, 1, cy, cz)
    heights = (2 * cy, 2 * cy + 16)
    return pl.pallas_call(
        planes_kernel,
        grid=(1,),
        in_specs=[
            pl.BlockSpec(plane, lambda g: (0, 0, 0, 0, 0)),
            pl.BlockSpec(plane, lambda g: (0, 0, cx - 1, 0, 0)),
            pl.BlockSpec(rows.shape, lambda g: (0,) * 5),
        ],
        out_specs=[pl.BlockSpec((ns, h, cz), lambda g: (0, 0, 0)) for h in heights],
        out_shape=[jax.ShapeDtypeStruct((ns, h, cz), jnp.bfloat16) for h in heights],
        compiler_params=pltpu.CompilerParams(vmem_limit_bytes=58 * MIB),
        name="outer_planes",
    )(field, field, rows)


def curl_plane(own, beyond, back_z, back_y, y_row_x, y_row_z, y_edge_z, y_edge_x):
    ex, ey, ez = own
    hx = (ahead(ez, 0, y_row_z) - ez) - (ahead(ey, 1) - ey)
    hy = (ahead(ex, 1) - ex) - (beyond[1] - ez)
    hz = (beyond[0] - ey) - (ahead(ex, 0, y_row_x) - ex)
    cx = (hz - behind(hz, 0, y_edge_z)) - (hy - behind(hy, 1, ex))
    cy = (hx - behind(hx, 1, -ey)) - (hz - back_z)
    cz = (hy - back_y) - (hx - behind(hx, 0, y_edge_x))
    return cx, cy, cz, hz, hy


def magnetic(own, beyond, row_x):
    ex, ey, ez = own
    return (beyond[0] - ey) - (ahead(ex, 0, row_x) - ex), (ahead(ex, 1) - ex) - (beyond[1] - ez)


def spread_rows(rows_ref, scratch):
    before, after = beside(rows_ref)
    for s in range(scratch.shape[0]):
        for n in range(5):
            tile, there = after if n < 2 else before
            scratch[s, n] = jnp.where(there, rows_ref[tile, s, n].astype(jnp.float32), 0.0)


def residual_plane(s, i, own, beyond, back, rows, after, planes, at, scaled, lines):
    cy, cz = own[0].shape
    cx = rows.shape[2]
    row_x, row_z, ex, ey, ez = (rows[s, n, pl.ds(i, 1), :] for n in range(5))
    curls = curl_plane(
        own, beyond, back[0], back[1], row_x, row_z, (ex + (after - ey)) - own[0], own[2] - (ez + (ahead(ey, 1) - ey))
    )
    for c in range(3):
        value = planes[s, c, at] - (curls[c] - scaled * own[c])
        planes[s, c, at] = value
        first = pl.multiple_of((c * cx + i) * cy, 16)
        lines[pl.ds(first, cy), s * cz : (s + 1) * cz] = value.astype(jnp.bfloat16)
    return curls[3], curls[4]


def inner_kernel(
    sol_ref, src_ref, perm_ref, rows_ref, res_ref, out_ref,
    field, planes, lines, back_z, back_y, rows, field_sem, plane_sem, res_sem, line_sem,
):
    ns, _, cx, cy, _ = field.shape

    def field_copy(i):
        return pltpu.make_async_copy(sol_ref.at[:, :, i], field.at[:, :, i], field_sem.at[i])

    def plane_copy(i):
        return pltpu.make_async_copy(src_ref.at[:, :, i], planes.at[:, :, i], plane_sem.at[i])

    def res_copy(i):
        return pltpu.make_async_copy(planes.at[:, :, i], res_ref.at[:, :, i], res_sem.at[i])

    def line_copy(i, c):
        at = pl.ds(pl.multiple_of((c * cx + i) * cy, 16), cy)
        return pltpu.make_async_copy(lines.at[at], out_ref.at[at], line_sem.at[c, i])

    for i in range(cx):
        field_copy(i).start()
        if 0 < i < cx - 1:
            plane_copy(i).start()
    spread_rows(rows_ref, rows)
    field_copy(0).wait()
    field_copy(1).wait()
    for s in range(ns):
        first, second = ([field[s, c, i] for c in range(3)] for i in range(2))
        back_z[s], back_y[s] = magnetic(first, second[1:], rows[s, 0, :1])

    @pl.loop(1, cx - 1)
    def _(i):
        field_copy(i + 1).wait()
        plane_copy(i).wait()
        scaled = OMEGA_SQ * perm_ref[i].astype(jnp.float32)
        for s in range(ns):
            own = [field[s, c, i] for c in range(3)]
            beyond = [field[s, c + 1, i + 1] for c in range(2)]
            back_z[s], back_y[s] = residual_plane(
                s, i, own, beyond, (back_z[s], back_y[s]), rows, rows[s, 3, pl.ds(i + 1, 1), :], planes, i, scaled, lines
            )
        res_copy(i).start()
        for c in range(3):
            line_copy(i, c).start()

    @pl.loop(1, cx - 1)
    def _(i):
        res_copy(i).wait()
        for c in range(3):
            line_copy(i, c).wait()


def inner_residual(field, source, permittivity, y_rows):
    ns, _, cx, cy, cz = field.shape
    anywhere = pl.BlockSpec(memory_space=pl.ANY)
    dma = pltpu.SemaphoreType.DMA
    grid_spec = pl.GridSpec(
        grid=(1,),
        in_specs=[
            anywhere,
            anywhere,
            pl.BlockSpec((cx, cy, cz), lambda g: (0, 0, 0)),
            pl.BlockSpec(y_rows.shape, lambda g: (0,) * 5),
        ],
        out_specs=[anywhere, anywhere],
        scratch_shapes=[
            pltpu.VMEM(field.shape, jnp.float32),
            pltpu.VMEM(field.shape, jnp.float32),
            pltpu.VMEM((3 * cx * cy, ns * cz), jnp.bfloat16),
            pltpu.VMEM((ns, cy, cz), jnp.float32),
            pltpu.VMEM((ns, cy, cz), jnp.float32),
            pltpu.VMEM((ns, 5, cx, cz), jnp.float32),
            dma((cx,)),
            dma((cx,)),
            dma((cx,)),
            dma((3, cx)),
        ],
    )
    return pl.pallas_call(
        inner_kernel,
        grid_spec=grid_spec,
        out_shape=[
            jax.ShapeDtypeStruct(field.shape, jnp.float32),
            jax.ShapeDtypeStruct((3 * cx * cy, ns * cz), jnp.bfloat16),
        ],
        compiler_params=pltpu.CompilerParams(vmem_limit_bytes=58 * MIB),
        cost_estimate=pl.CostEstimate(flops=60 * field.size, bytes_accessed=14 * field.size, transcendentals=0),
        name="inner_residual",
    )(field, source, permittivity, y_rows)


def gather_kernel(
    ready, count_ref, sol_ref, src_ref, perm_ref, rows_ref, up_ref, down_ref, inner_ref, line_ref, depth_ref, _,
    res_ref, out_ref, field, planes, lines, turned, rows, got_ref, field_sem, plane_sem, line_sem,
):
    ns, _, cx, cy, cz = sol_ref.shape
    total = lines.shape[0]
    f32 = jnp.float32
    ends = (0, cx - 1)
    field_copies = [
        pltpu.make_async_copy(sol_ref.at[:, :, i], field.at[:, :, n], field_sem.at[n])
        for n, i in enumerate((0, 1, cx - 2, cx - 1))
    ]
    plane_copies = [
        pltpu.make_async_copy(src_ref.at[:, :, i], planes.at[:, :, n], plane_sem.at[n]) for n, i in enumerate(ends)
    ]
    line_copies = []
    for c in range(3):
        at = pl.ds((c * cx + 1) * cy, (cx - 2) * cy)
        line_copies.append(pltpu.make_async_copy(inner_ref.at[at], lines.at[at], line_sem.at[c]))
    res_copies = [
        pltpu.make_async_copy(planes.at[:, :, n], res_ref.at[:, :, i], plane_sem.at[n]) for n, i in enumerate(ends)
    ]
    for copy in field_copies[:2] + plane_copies[:1] + field_copies[2:] + plane_copies[1:] + line_copies:
        copy.start()
    ready()
    spread_rows(rows_ref, rows)
    got_ref[...] = jnp.zeros_like(got_ref)

    for copy in field_copies[:2] + plane_copies[:1]:
        copy.wait()
    scaled = OMEGA_SQ * perm_ref[0].astype(f32)
    for s in range(ns):
        own = [field[s, c, 0] for c in range(3)]
        back = own[1] - up_ref[s, :cy].astype(f32), up_ref[s, cy:].astype(f32) - own[2]
        beyond = [field[s, c + 1, 1] for c in range(2)]
        residual_plane(s, 0, own, beyond, back, rows, rows[s, 3, 1:2], planes, 0, scaled, lines)
    res_copies[0].start()

    for copy in field_copies[2:] + plane_copies[1:]:
        copy.wait()
    scaled = OMEGA_SQ * perm_ref[cx - 1].astype(f32)
    for s in range(ns):
        own = [field[s, c, 3] for c in range(3)]
        back = magnetic([field[s, c, 2] for c in range(3)], own[1:], rows[s, 0, cx - 2 : cx - 1])
        beyond = [down_ref[s, c * cy : (c + 1) * cy].astype(f32) for c in range(2)]
        after = down_ref[s, 2 * cy :].astype(f32)[:1]
        residual_plane(s, cx - 1, own, beyond, back, rows, after, planes, 1, scaled, lines)
    res_copies[1].start()

    for copy in line_copies:
        copy.wait()
    for a in range(total // 128):
        for b in range(ns * cz // 128):
            turned[b * 128 : (b + 1) * 128, a * 128 : (a + 1) * 128] = lines[
                a * 128 : (a + 1) * 128, b * 128 : (b + 1) * 128
            ].T
    group = got_ref.shape[1]
    width = group * 128

    @pl.loop(0, pl.cdiv(count_ref[0], group))
    def _(p):
        hot = (iota((total, width), 0) == joined(line_ref, p * group, group)).astype(f32).astype(jnp.bfloat16)
        got = jnp.dot(turned[...], hot, preferred_element_type=f32)
        at = iota((cz, width), 0) == joined(depth_ref, p * group, group)
        for s in range(ns):
            sums = jnp.sum(jnp.where(at, got[s * cz : (s + 1) * cz], 0.0), axis=0, keepdims=True)
            for h in range(group):
                got_ref[p, h : h + 1, s * 128 : (s + 1) * 128] = sums[:, h * 128 : (h + 1) * 128]

    picked = got_ref[...].reshape(out_ref.shape[1:]).astype(out_ref.dtype)
    for w in range(out_ref.shape[0]):
        out_ref[w] = picked
    for copy in res_copies:
        copy.wait()


def outer_residual_and_gather(copies, field, source, permittivity, counts, y_rows, up, down, residual, inner, line, depth):
    ns, _, cx, cy, cz = field.shape
    total = 3 * cx * cy
    group = min(OWN_GROUP, line.shape[0])
    groups = line.shape[0] // group
    operands = field, source, permittivity, y_rows, up, down, inner, line, depth, residual
    kernel, extra = staged(gather_kernel, 1, operands, (2, 3, 4, 5, 7, 8))
    anywhere = pl.BlockSpec(memory_space=pl.ANY)
    dma = pltpu.SemaphoreType.DMA
    grid_spec = pltpu.PrefetchScalarGridSpec(
        num_scalar_prefetch=1,
        grid=(1,),
        in_specs=[anywhere] * 10,
        out_specs=[anywhere, pl.BlockSpec((copies, groups * group, ns * 128), lambda g, *_: (0, 0, 0))],
        scratch_shapes=[
            pltpu.VMEM((ns, 3, 4, cy, cz), jnp.float32),
            pltpu.VMEM((ns, 3, 2, cy, cz), jnp.float32),
            pltpu.VMEM((total, ns * cz), jnp.bfloat16),
            pltpu.VMEM((ns * cz, total), jnp.bfloat16),
            pltpu.VMEM((ns, 5, cx, cz), jnp.float32),
            pltpu.VMEM((groups, group, ns * 128), jnp.float32),
            dma((4,)),
            dma((2,)),
            dma((3,)),
            *extra,
        ],
    )
    return pl.pallas_call(
        kernel,
        grid_spec=grid_spec,
        out_shape=[
            jax.ShapeDtypeStruct(field.shape, jnp.float32),
            jax.ShapeDtypeStruct((copies, groups * group, ns * 128), jnp.bfloat16),
        ],
        input_output_aliases={10: 0},
        compiler_params=pltpu.CompilerParams(vmem_limit_bytes=58 * MIB),
        name="outer_residual_gather",
    )(counts, *operands)


def fronts_kernel(at_ref, given_ref, top_ref, mid_ref, low_ref, y_ref, top_buf, mid_buf, low_buf, given, x_buf, y_buf, sem):
    ns = y_buf.shape[0]
    jobs, base, column = [], 0, 0
    for w_ref, buf in ((top_ref, top_buf), (mid_ref, mid_buf), (low_ref, low_buf)):
        count, height, width = w_ref.shape
        rows = height
        while rows > 256 and rows * width * 2 > 4 * MIB:
            rows //= 2
        for f in range(count):
            for r in range(0, height, rows):
                at = pl.ds(r, rows)
                copy = pltpu.make_async_copy(w_ref.at[f, at], buf.at[f, at], sem.at[len(jobs)])
                jobs.append((copy, buf, f, at, slice(column, column + width), (base + r) // 128))
            base += height
            column += width
    for job in jobs:
        job[0].start()
    given[...] = given_ref[...].astype(jnp.float32)
    for b in range(x_buf.shape[1] // 128):
        row = given[pl.ds(at_ref[b], 1), :]
        for s in range(ns):
            x_buf[s : s + 1, b * 128 : (b + 1) * 128] = row[:, s * 128 : (s + 1) * 128]
    for copy, buf, f, at, lanes, first in jobs:
        copy.wait()
        got = lax.dot_general(
            x_buf[:, lanes].astype(jnp.bfloat16),
            buf[f, at],
            (((1,), (1,)), ((), ())),
            preferred_element_type=jnp.float32,
        )
        for b in range(got.shape[1] // 128):
            for s in range(ns):
                y_buf[s, first + b : first + b + 1] = got[s : s + 1, b * 128 : (b + 1) * 128]
    y_ref[...] = y_buf[...].astype(y_ref.dtype)


def fronts(held_at, everyone, inverses):
    ns = everyone.shape[1] // 128
    blocks = sum(inv.shape[0] * inv.shape[1] for inv in inverses) // 128
    entries = sum(inv.size for inv in inverses)
    there = pl.BlockSpec(memory_space=pl.ANY)
    grid_spec = pltpu.PrefetchScalarGridSpec(
        num_scalar_prefetch=1,
        grid=(1,),
        in_specs=[pl.BlockSpec(everyone.shape, lambda g, _: (0, 0))] + [there] * 3,
        out_specs=pl.BlockSpec((ns, blocks, 128), lambda g, _: (0, 0, 0)),
        scratch_shapes=[
            *[pltpu.VMEM(inv.shape, inv.dtype) for inv in inverses],
            pltpu.VMEM(everyone.shape, jnp.float32),
            pltpu.VMEM((ns, held_at.shape[0] * 128), jnp.float32),
            pltpu.VMEM((ns, blocks, 128), jnp.float32),
            pltpu.SemaphoreType.DMA((64,)),
        ],
    )
    return pl.pallas_call(
        fronts_kernel,
        grid_spec=grid_spec,
        out_shape=jax.ShapeDtypeStruct((ns, blocks, 128), jnp.bfloat16),
        compiler_params=pltpu.CompilerParams(vmem_limit_bytes=58 * MIB),
        cost_estimate=pl.CostEstimate(flops=4 * entries, bytes_accessed=2 * entries, transcendentals=0),
        name="fronts",
    )(held_at, everyone, *inverses)


def correct_kernel(
    count_ref, sol_ref, res_ref, perm_ref, own_line_ref, own_depth_ref, line_ref, depth_ref, given_ref,
    out_ref, new_ref, value_ref, field, residual, delta, x_halo, y_halo, back_z, back_y, in_sem, out_sem,
):
    ns, _, planes, cy, cz = sol_ref.shape
    f32, half = jnp.float32, jnp.bfloat16

    def copies_in(i):
        return [
            pltpu.make_async_copy(ref.at[:, :, i], buf.at[:, :, i], in_sem.at[n, i])
            for n, (ref, buf) in enumerate(((sol_ref, field), (res_ref, residual)))
        ]

    def copies_out(i):
        return [
            pltpu.make_async_copy(buf.at[:, :, i], ref.at[:, :, i], out_sem.at[n, i])
            for n, (ref, buf) in enumerate(((out_ref, field), (new_ref, residual)))
        ]

    for i in range(planes):
        for copy in copies_in(i):
            copy.start()
    capacity = own_line_ref.shape[0]
    own_group, group = min(OWN_GROUP, capacity), min(NEAR_GROUP, capacity)
    own_width, width = own_group * 128, group * 128
    chunks = line_ref.shape[0] // group

    def values_of(first, count):
        rows = [value_ref[pl.ds(count_ref[len(NEAR) + chunks + first + h], 1), :] for h in range(count)]
        return [jnp.concatenate([v[:, s * 128 : (s + 1) * 128] for v in rows], axis=1) for s in range(ns)]

    def times(a, b):
        return lax.dot_general(a, b, (((1,), (1,)), ((), ())), preferred_element_type=f32)

    value_ref[...] = given_ref[...].astype(f32)
    x_halo[...] = jnp.zeros_like(x_halo)
    y_halo[...] = jnp.zeros_like(y_halo)

    def own_part(p):
        values = values_of(p * own_group, own_group)
        hot = (iota((delta.shape[0], own_width), 0) == joined(own_line_ref, p * own_group, own_group)).astype(f32).astype(half)
        at = iota((cz, own_width), 0) == joined(own_depth_ref, p * own_group, own_group)
        return times(hot, jnp.concatenate([jnp.where(at, v, 0.0).astype(half) for v in values], axis=0))

    delta[...] = own_part(0)

    @pl.loop(1, pl.cdiv(count_ref[0], own_group))
    def _(p):
        delta[...] += own_part(p)

    place = (
        (x_halo, 0, 2 * cy),
        (x_halo, 2 * cy, 3 * cy),
        (y_halo, 0, 2 * planes),
        (y_halo, 2 * planes, 3 * planes),
        (y_halo, 5 * planes, 8),
        (y_halo, 5 * planes, 8),
    )
    for q, (target, first, height) in enumerate(place):

        @pl.loop(0, pl.cdiv(count_ref[q + 1], group))
        def _(p, q=q, target=target, first=first, height=height):
            row = q * (capacity // group) + p

            @pl.when(count_ref[len(NEAR) + row] > 0)
            def _():
                values = values_of((q + 1) * capacity + p * group, group)
                at = iota((height, width), 0) == joined(line_ref, row * group, group)
                hot = (iota((cz, width), 0) == joined(depth_ref, row * group, group)).astype(f32).astype(half)
                got = times(jnp.concatenate([jnp.where(at, v, 0.0) for v in values], axis=0).astype(half), hot)
                for s in range(ns):
                    target[s, first : first + height] += got[s * height : (s + 1) * height]

    def plane(s, c, i):
        return delta[pl.ds(pl.multiple_of((c * planes + i) * cy, 8), cy), s * cz : (s + 1) * cz]

    for s in range(ns):
        ex, ey, ez = (x_halo[s, (2 + c) * cy : (3 + c) * cy] for c in range(3))
        corner = y_halo[s, 5 * planes : 5 * planes + 1]
        back_z[s] = plane(s, 1, 0) - (ey + (ahead(ex, 0, corner) - ex))
        back_y[s] = (ez + (ahead(ex, 1) - ex)) - plane(s, 2, 0)

    @pl.loop(0, planes)
    def _(i):
        last = i == planes - 1
        after = jnp.minimum(i + 1, planes - 1)
        scaled = OMEGA_SQ * perm_ref[i].astype(f32)
        for copy in copies_in(i):
            copy.wait()
        for s in range(ns):
            own = [plane(s, c, i) for c in range(3)]
            beyond = [jnp.where(last, x_halo[s, c * cy : (c + 1) * cy], plane(s, c + 1, after)) for c in range(2)]
            y_row_x = y_halo[s, pl.ds(i, 1), :]
            y_row_z = y_halo[s, pl.ds(planes + i, 1), :]
            hx, hy, hz = (y_halo[s, pl.ds((2 + c) * planes + i, 1), :] for c in range(3))
            hy_after = jnp.where(
                last, y_halo[s, 5 * planes + 1 : 5 * planes + 2], y_halo[s, pl.ds(3 * planes + after, 1), :]
            )
            curls = curl_plane(
                own,
                beyond,
                back_z[s],
                back_y[s],
                y_row_x,
                y_row_z,
                (hx + (hy_after - hy)) - own[0],
                own[2] - (hz + (ahead(hy, 1) - hy)),
            )
            for c in range(3):
                field[s, c, i] += own[c]
                residual[s, c, i] -= curls[c] - scaled * own[c]
            back_z[s], back_y[s] = curls[3], curls[4]
        for copy in copies_out(i):
            copy.start()

    @pl.loop(0, planes)
    def _(i):
        for copy in copies_out(i):
            copy.wait()


def correct(field, residual, permittivity, counts, own_line, own_depth, line, depth, updates):
    ns, _, cx, cy, cz = field.shape
    anywhere = pl.BlockSpec(memory_space=pl.ANY)
    whole = lambda x: pl.BlockSpec(x.shape, lambda g, *_: (0,) * x.ndim)
    y_lines = 5 * cx + 8
    grid_spec = pltpu.PrefetchScalarGridSpec(
        num_scalar_prefetch=1,
        grid=(1,),
        in_specs=[
            anywhere,
            anywhere,
            *[whole(x) for x in (permittivity, own_line, own_depth, line, depth, updates)],
        ],
        out_specs=[anywhere, anywhere],
        scratch_shapes=[
            pltpu.VMEM(updates.shape, jnp.float32),
            pltpu.VMEM(field.shape, jnp.float32),
            pltpu.VMEM(field.shape, jnp.float32),
            pltpu.VMEM((3 * cx * cy, ns * cz), jnp.float32),
            pltpu.VMEM((ns, 5 * cy, cz), jnp.float32),
            pltpu.VMEM((ns, y_lines, cz), jnp.float32),
            pltpu.VMEM((ns, cy, cz), jnp.float32),
            pltpu.VMEM((ns, cy, cz), jnp.float32),
            pltpu.SemaphoreType.DMA((2, cx)),
            pltpu.SemaphoreType.DMA((2, cx)),
        ],
    )
    return pl.pallas_call(
        correct_kernel,
        grid_spec=grid_spec,
        out_shape=[jax.ShapeDtypeStruct(field.shape, jnp.float32)] * 2,
        compiler_params=pltpu.CompilerParams(vmem_limit_bytes=58 * MIB),
        name="correct",
    )(counts, field, residual, permittivity, own_line, own_depth, line, depth, updates)


def block_rows_of(inverses, wide_count, block_rows):
    per_device = sum(inv.shape[0] * inv.shape[1] for inv in inverses) // block_rows
    table, base = [], 0
    for inv in inverses:
        per = inv.shape[1] // block_rows
        for f in range(inv.shape[0]):
            b = np.arange(per * wide_count)
            table.append(b // per * per_device + base + f * per + b % per)
        base += inv.shape[0] * per
    return np.concatenate(table).astype(np.int32)


def block_columns_of(inverses, narrow_count, block_rows):
    table, base = [], 0
    for inv in inverses:
        per = inv.shape[2] // block_rows
        for _ in range(inv.shape[0]):
            table.append(base + np.arange(per * narrow_count).reshape(narrow_count, per))
            base += per * narrow_count
    return np.concatenate(table, axis=1).astype(np.int32)


def to_all_wide(block, wide_count):
    spread = jnp.broadcast_to(block[None], (wide_count, *block.shape)).reshape(-1, *block.shape[1:])
    return lax.all_to_all(spread, "wide", 0, 0, tiled=True)


def on_device(solution, source_term, permittivity, inv_top, inv_mid, inv_low, sep_tile, sep_cell):
    wide_count, narrow_count = lax.axis_size("wide"), lax.axis_size("narrow")
    my_wide, my_narrow = lax.axis_index("wide"), lax.axis_index("narrow")
    ns, _, cx, cy, cz = solution.shape
    block_count, block_rows = sep_cell.shape
    capacity = max(2, 2 * block_count // (wide_count * narrow_count))
    inverses = (inv_top[None], inv_mid, inv_low)

    y_rows = lax.all_gather(outer_rows(solution), "narrow", axis=0, tiled=False)
    to_up, to_down = outer_planes(solution, y_rows)
    steps = [(w, w + 1) for w in range(wide_count - 1)]
    up = lax.ppermute(to_up, "wide", steps)
    down = lax.ppermute(to_down, "wide", [(b, a) for a, b in steps])
    inner, inner_lines = inner_residual(solution, source_term, permittivity, y_rows)

    block_tile = sep_tile[:, 0]
    block_ids = jnp.arange(block_count, dtype=jnp.int32)
    slot_rank = jnp.sum(
        jnp.logical_and(
            block_tile[:, None] == block_tile[None, :], block_ids[None, :] < block_ids[:, None]
        ).astype(jnp.int32),
        axis=1,
    )
    offsets = np.array(NEAR, np.int32)
    near_wide, near_narrow = my_wide + offsets[:, 0], my_narrow + offsets[:, 1]
    inside = (near_wide >= 0) & (near_wide < wide_count) & (near_narrow >= 0) & (near_narrow < narrow_count)
    near_tile = jnp.where(inside, near_wide * narrow_count + near_narrow, -1)
    named = block_tile[None, :] == near_tile[:, None]
    counts = jnp.sum(named.astype(jnp.int32), axis=1)
    slots = jnp.arange(capacity, dtype=jnp.int32)
    match = jnp.logical_and(named[:, None, :], slot_rank[None, None, :] == slots[None, :, None])
    near_ids = jnp.sum(jnp.where(match, block_ids[None, None, :], 0), axis=2)
    near_rows = jnp.sum(
        jnp.where(match, block_rows_of(inverses, wide_count, block_rows)[None, None, :], 0), axis=2
    )
    found = slots[None, :] < counts[:, None]
    cells = sep_cell.at[near_ids.reshape(-1)].get(mode="promise_in_bounds").reshape(len(NEAR), capacity, block_rows)
    depth = cells % cz
    row = cells // cz
    part, at_i, at_j = row // (cx * cy), row // cy % cx, row % cy
    rule = (
        (row, row >= 0),
        ((part - 1) * cy + at_j, (part >= 1) & (at_i == 0)),
        (part * cy + at_j, at_i == cx - 1),
        (part // 2 * cx + at_i, (part != 1) & (at_j == 0)),
        (part * cx + at_i, at_j == cy - 1),
        (jnp.zeros_like(row), (part == 0) & (at_i == cx - 1) & (at_j == 0)),
        (jnp.ones_like(row), (part == 1) & (at_i == 0) & (at_j == cy - 1)),
    )
    line = jnp.stack(
        [jnp.where(found[q, :, None] & keep[q], at[q], -1) for q, (at, keep) in enumerate(rule)]
    )
    arrives = (block_tile % narrow_count * wide_count + block_tile // narrow_count) * capacity + slot_rank
    table = block_columns_of(inverses, narrow_count, block_rows)
    held_at = jnp.sum(
        jnp.where(
            (table[:, :, None] == block_ids) & (np.arange(narrow_count)[:, None, None] == my_narrow), arrives, 0
        ),
        axis=(0, 2),
    )
    own_line, own_depth = line[0], depth[0]
    line, depth = line[1:].reshape(-1, block_rows), depth[1:].reshape(-1, block_rows)
    most = jnp.max(line.reshape(-1, min(NEAR_GROUP, capacity) * block_rows), axis=1)
    loads = jnp.concatenate([counts, most + 1, near_rows.reshape(-1)])

    residual, picked = outer_residual_and_gather(
        wide_count, solution, source_term, permittivity, counts, y_rows, up, down, inner, inner_lines, own_line, own_depth
    )
    column = lax.all_to_all(picked.reshape(-1, ns * block_rows), "wide", 0, 0, tiled=True)
    everyone = lax.all_gather(column, "narrow", axis=0, tiled=True)
    partial = fronts(held_at, everyone, inverses)
    rows = partial.shape[1]
    shares = lax.all_gather(partial, "narrow", axis=0, tiled=False)
    summed = jnp.sum(shares.astype(jnp.float32), axis=0).astype(jnp.bfloat16)
    summed = summed.transpose(1, 0, 2).reshape(rows, ns * block_rows)
    updates = to_all_wide(summed, wide_count)

    return tuple(correct(solution, residual, permittivity, loads, own_line, own_depth, line, depth, updates))


def solution(mesh):
    return jax.shard_map(
        on_device,
        mesh=mesh,
        in_specs=(
            P(None, None, "wide", "narrow", None),
            P(None, None, "wide", "narrow", None),
            P("wide", "narrow", None),
            P("wide", "narrow"),
            P(None, "wide", "narrow"),
            P(None, "wide", "narrow"),
            P(),
            P(),
        ),
        out_specs=(P(None, None, "wide", "narrow", None), P(None, None, "wide", "narrow", None)),
        check_vma=False,
    )
```

```python
import jax
import jax.numpy as jnp
import numpy as np
from jax import lax
from jax.experimental import pallas as pl
from jax.experimental.pallas import tpu as pltpu
from jax.sharding import PartitionSpec as P

OMEGA_SQ = 0.5
MIB = 1 << 20

NEAR = ((0, 0), (1, 0), (-1, 0), (0, 1), (0, -1), (-1, 1), (1, -1))


def iota(shape, dim):
    return lax.broadcasted_iota(jnp.int32, shape, dim)


def lane_blocks(x):
    return [x[:, at : at + 128] for at in range(0, x.shape[1], 128)]


def shifted(x, axis, step, edge):
    if axis == 1:
        size, blocks = 128, lane_blocks(x)
        fill = lane_blocks(jnp.broadcast_to(edge, x.shape))
        turned = [pltpu.roll(b, step % size, 1) for b in blocks]
        mask = iota((1, size), 1)
    else:
        size, tiles = 8, x.shape[0] // 8
        turned = pltpu.roll(x.reshape(tiles, size, x.shape[1]), step % size, 1)
        turned = [turned[t] for t in range(tiles)]
        filled = jnp.broadcast_to(edge, (size, x.shape[1])) if jnp.ndim(edge) == 0 or edge.shape[0] == 1 else edge
        fill = [filled[:size]] * tiles
        mask = iota((size, 1), 0)
    if step < 0:
        others = [*turned[1:], fill[-1]]
        mask = mask == size - 1
    else:
        others = [fill[0], *turned[:-1]]
        mask = mask == 0
    return jnp.concatenate([jnp.where(mask, o, t) for o, t in zip(others, turned, strict=True)], axis=axis)


def ahead(x, axis, edge=0.0):
    return shifted(x, axis, -1, edge)


def behind(x, axis, edge):
    return shifted(x, axis, 1, edge)


def staged(body, scalars, operands, small):
    def kernel(*refs):
        held, sem = refs[-1 - len(small) : -1], refs[-1]
        refs = list(refs[: -1 - len(small)])
        copies = []
        for k, n in enumerate(small):
            copies.append(pltpu.make_async_copy(refs[scalars + n], held[k], sem.at[k]))
            refs[scalars + n] = held[k]
        for copy in copies:
            copy.start()

        def ready():
            for copy in copies:
                copy.wait()

        body(ready, *refs)

    extra = [pltpu.VMEM(operands[n].shape, operands[n].dtype) for n in small]
    return kernel, [*extra, pltpu.SemaphoreType.DMA((len(small),))]


def rows_kernel(low_ref, high_ref, out_ref):
    top = high_ref.shape[3] - 1
    for s in range(out_ref.shape[0]):
        rows = [low_ref[s, 0, :, 0, :], low_ref[s, 2, :, 0, :], *(high_ref[s, c, :, top, :] for c in range(3))]
        for n, row in enumerate(rows):
            out_ref[s, n] = row.astype(out_ref.dtype)


def outer_rows(field):
    ns, _, cx, cy, cz = field.shape
    slab = (ns, 3, cx, 8, cz)
    return pl.pallas_call(
        rows_kernel,
        grid=(1,),
        in_specs=[
            pl.BlockSpec(slab, lambda g: (0, 0, 0, 0, 0)),
            pl.BlockSpec(slab, lambda g: (0, 0, 0, cy // 8 - 1, 0)),
        ],
        out_specs=pl.BlockSpec((ns, 5, cx, cz), lambda g: (0, 0, 0, 0)),
        out_shape=jax.ShapeDtypeStruct((ns, 5, cx, cz), jnp.bfloat16),
        compiler_params=pltpu.CompilerParams(vmem_limit_bytes=60 * MIB),
        name="outer_rows",
    )(field, field)


def beside(rows_ref):
    me, last = lax.axis_index("narrow"), rows_ref.shape[0] - 1
    return (jnp.maximum(me - 1, 0), me > 0), (jnp.minimum(me + 1, last), me < last)


def planes_kernel(first_ref, last_ref, rows_ref, up_ref, down_ref):
    planes, cy, dtype = rows_ref.shape[3], first_ref.shape[3], up_ref.dtype
    (before, has_before), (after, has_after) = beside(rows_ref)
    for s in range(up_ref.shape[0]):
        ex, ey, ez = (last_ref[s, c, 0] for c in range(3))
        past = jnp.where(has_after, rows_ref[after, s, 0].astype(jnp.float32)[planes - 1 :], 0.0)
        up_ref[s, :cy] = (ey + (ahead(ex, 0, past) - ex)).astype(dtype)
        up_ref[s, cy:] = (ez + (ahead(ex, 1) - ex)).astype(dtype)
        down_ref[s, :cy] = first_ref[s, 1, 0].astype(dtype)
        down_ref[s, cy : 2 * cy] = first_ref[s, 2, 0].astype(dtype)
        edge = jnp.where(has_before, rows_ref[before, s, 3].astype(jnp.float32)[:1], 0.0)
        down_ref[s, 2 * cy :] = jnp.broadcast_to(edge, (down_ref.shape[1] - 2 * cy, edge.shape[1])).astype(dtype)


def outer_planes(field, rows):
    ns, _, cx, cy, cz = field.shape
    plane = (ns, 3, 1, cy, cz)
    heights = (2 * cy, 2 * cy + 16)
    return pl.pallas_call(
        planes_kernel,
        grid=(1,),
        in_specs=[
            pl.BlockSpec(plane, lambda g: (0, 0, 0, 0, 0)),
            pl.BlockSpec(plane, lambda g: (0, 0, cx - 1, 0, 0)),
            pl.BlockSpec(rows.shape, lambda g: (0,) * 5),
        ],
        out_specs=[pl.BlockSpec((ns, h, cz), lambda g: (0, 0, 0)) for h in heights],
        out_shape=[jax.ShapeDtypeStruct((ns, h, cz), jnp.bfloat16) for h in heights],
        compiler_params=pltpu.CompilerParams(vmem_limit_bytes=60 * MIB),
        name="outer_planes",
    )(field, field, rows)


def curl_plane(own, beyond, back_z, back_y, y_row_x, y_row_z, y_edge_z, y_edge_x):
    ex, ey, ez = own
    hx = (ahead(ez, 0, y_row_z) - ez) - (ahead(ey, 1) - ey)
    hy = (ahead(ex, 1) - ex) - (beyond[1] - ez)
    hz = (beyond[0] - ey) - (ahead(ex, 0, y_row_x) - ex)
    cx = (hz - behind(hz, 0, y_edge_z)) - (hy - behind(hy, 1, ex))
    cy = (hx - behind(hx, 1, -ey)) - (hz - back_z)
    cz = (hy - back_y) - (hx - behind(hx, 0, y_edge_x))
    return cx, cy, cz, hz, hy


def magnetic(own, beyond, row_x):
    ex, ey, ez = own
    return (beyond[0] - ey) - (ahead(ex, 0, row_x) - ex), (ahead(ex, 1) - ex) - (beyond[1] - ez)


def spread_rows(rows_ref, scratch):
    before, after = beside(rows_ref)
    for s in range(scratch.shape[0]):
        for n in range(5):
            tile, there = after if n < 2 else before
            scratch[s, n] = jnp.where(there, rows_ref[tile, s, n].astype(jnp.float32), 0.0)


def residual_plane(s, i, own, beyond, back, rows, after, planes, at, scaled, lines):
    cy, cz = own[0].shape
    cx = rows.shape[2]
    row_x, row_z, ex, ey, ez = (rows[s, n, pl.ds(i, 1), :] for n in range(5))
    curls = curl_plane(
        own, beyond, back[0], back[1], row_x, row_z, (ex + (after - ey)) - own[0], own[2] - (ez + (ahead(ey, 1) - ey))
    )
    for c in range(3):
        value = planes[s, c, at] - (curls[c] - scaled * own[c])
        planes[s, c, at] = value
        first = pl.multiple_of((c * cx + i) * cy, 16)
        lines[pl.ds(first, cy), s * cz : (s + 1) * cz] = value.astype(jnp.bfloat16)
    return curls[3], curls[4]


def inner_kernel(
    sol_ref, src_ref, perm_ref, rows_ref, res_ref, out_ref,
    field, planes, lines, back_z, back_y, rows, field_sem, plane_sem, res_sem, line_sem,
):
    ns, _, cx, cy, _ = field.shape

    def field_copy(i):
        return pltpu.make_async_copy(sol_ref.at[:, :, i], field.at[:, :, i], field_sem.at[i])

    def plane_copy(i):
        return pltpu.make_async_copy(src_ref.at[:, :, i], planes.at[:, :, i], plane_sem.at[i])

    def res_copy(i):
        return pltpu.make_async_copy(planes.at[:, :, i], res_ref.at[:, :, i], res_sem.at[i])

    def line_copy(i, c):
        at = pl.ds(pl.multiple_of((c * cx + i) * cy, 16), cy)
        return pltpu.make_async_copy(lines.at[at], out_ref.at[at], line_sem.at[c, i])

    for i in range(cx):
        field_copy(i).start()
        if 0 < i < cx - 1:
            plane_copy(i).start()
    spread_rows(rows_ref, rows)
    field_copy(0).wait()
    field_copy(1).wait()
    for s in range(ns):
        first, second = ([field[s, c, i] for c in range(3)] for i in range(2))
        back_z[s], back_y[s] = magnetic(first, second[1:], rows[s, 0, :1])

    @pl.loop(1, cx - 1)
    def _(i):
        field_copy(i + 1).wait()
        plane_copy(i).wait()
        scaled = OMEGA_SQ * perm_ref[i].astype(jnp.float32)
        for s in range(ns):
            own = [field[s, c, i] for c in range(3)]
            beyond = [field[s, c + 1, i + 1] for c in range(2)]
            back_z[s], back_y[s] = residual_plane(
                s, i, own, beyond, (back_z[s], back_y[s]), rows, rows[s, 3, pl.ds(i + 1, 1), :], planes, i, scaled, lines
            )
        res_copy(i).start()
        for c in range(3):
            line_copy(i, c).start()

    @pl.loop(1, cx - 1)
    def _(i):
        res_copy(i).wait()
        for c in range(3):
            line_copy(i, c).wait()


def inner_residual(field, source, permittivity, y_rows):
    ns, _, cx, cy, cz = field.shape
    anywhere = pl.BlockSpec(memory_space=pl.ANY)
    dma = pltpu.SemaphoreType.DMA
    grid_spec = pl.GridSpec(
        grid=(1,),
        in_specs=[
            anywhere,
            anywhere,
            pl.BlockSpec((cx, cy, cz), lambda g: (0, 0, 0)),
            pl.BlockSpec(y_rows.shape, lambda g: (0,) * 5),
        ],
        out_specs=[anywhere, anywhere],
        scratch_shapes=[
            pltpu.VMEM(field.shape, jnp.float32),
            pltpu.VMEM(field.shape, jnp.float32),
            pltpu.VMEM((3 * cx * cy, ns * cz), jnp.bfloat16),
            pltpu.VMEM((ns, cy, cz), jnp.float32),
            pltpu.VMEM((ns, cy, cz), jnp.float32),
            pltpu.VMEM((ns, 5, cx, cz), jnp.float32),
            dma((cx,)),
            dma((cx,)),
            dma((cx,)),
            dma((3, cx)),
        ],
    )
    return pl.pallas_call(
        inner_kernel,
        grid_spec=grid_spec,
        out_shape=[
            jax.ShapeDtypeStruct(field.shape, jnp.float32),
            jax.ShapeDtypeStruct((3 * cx * cy, ns * cz), jnp.bfloat16),
        ],
        compiler_params=pltpu.CompilerParams(vmem_limit_bytes=60 * MIB),
        cost_estimate=pl.CostEstimate(flops=60 * field.size, bytes_accessed=14 * field.size, transcendentals=0),
        name="inner_residual",
    )(field, source, permittivity, y_rows)


def gather_kernel(
    ready, count_ref, sol_ref, src_ref, perm_ref, rows_ref, up_ref, down_ref, inner_ref, line_ref, depth_ref, _,
    res_ref, out_ref, field, planes, lines, turned, rows, got_ref, field_sem, plane_sem, line_sem,
):
    ns, _, cx, cy, cz = sol_ref.shape
    total = lines.shape[0]
    f32 = jnp.float32
    ends = (0, cx - 1)
    field_copies = [
        pltpu.make_async_copy(sol_ref.at[:, :, i], field.at[:, :, n], field_sem.at[n])
        for n, i in enumerate((0, 1, cx - 2, cx - 1))
    ]
    plane_copies = [
        pltpu.make_async_copy(src_ref.at[:, :, i], planes.at[:, :, n], plane_sem.at[n]) for n, i in enumerate(ends)
    ]
    line_copies = []
    for c in range(3):
        at = pl.ds((c * cx + 1) * cy, (cx - 2) * cy)
        line_copies.append(pltpu.make_async_copy(inner_ref.at[at], lines.at[at], line_sem.at[c]))
    res_copies = [
        pltpu.make_async_copy(planes.at[:, :, n], res_ref.at[:, :, i], plane_sem.at[n]) for n, i in enumerate(ends)
    ]
    for copy in field_copies[:2] + plane_copies[:1] + field_copies[2:] + plane_copies[1:] + line_copies:
        copy.start()
    ready()
    spread_rows(rows_ref, rows)
    got_ref[...] = jnp.zeros_like(got_ref)

    for copy in field_copies[:2] + plane_copies[:1]:
        copy.wait()
    scaled = OMEGA_SQ * perm_ref[0].astype(f32)
    for s in range(ns):
        own = [field[s, c, 0] for c in range(3)]
        back = own[1] - up_ref[s, :cy].astype(f32), up_ref[s, cy:].astype(f32) - own[2]
        beyond = [field[s, c + 1, 1] for c in range(2)]
        residual_plane(s, 0, own, beyond, back, rows, rows[s, 3, 1:2], planes, 0, scaled, lines)
    res_copies[0].start()

    for copy in field_copies[2:] + plane_copies[1:]:
        copy.wait()
    scaled = OMEGA_SQ * perm_ref[cx - 1].astype(f32)
    for s in range(ns):
        own = [field[s, c, 3] for c in range(3)]
        back = magnetic([field[s, c, 2] for c in range(3)], own[1:], rows[s, 0, cx - 2 : cx - 1])
        beyond = [down_ref[s, c * cy : (c + 1) * cy].astype(f32) for c in range(2)]
        after = down_ref[s, 2 * cy :].astype(f32)[:1]
        residual_plane(s, cx - 1, own, beyond, back, rows, after, planes, 1, scaled, lines)
    res_copies[1].start()

    for copy in line_copies:
        copy.wait()
    for a in range(total // 128):
        for b in range(ns * cz // 128):
            turned[b * 128 : (b + 1) * 128, a * 128 : (a + 1) * 128] = lines[
                a * 128 : (a + 1) * 128, b * 128 : (b + 1) * 128
            ].T
    group, width = got_ref.shape[1], line_ref.shape[1]

    @pl.loop(0, pl.cdiv(count_ref[0], group))
    def _(p):
        hot = (iota((total, width), 0) == line_ref[pl.ds(p, 1), :]).astype(f32).astype(jnp.bfloat16)
        got = jnp.dot(turned[...], hot, preferred_element_type=f32)
        at = iota((cz, width), 0) == depth_ref[pl.ds(p, 1), :]
        for s in range(ns):
            sums = jnp.sum(jnp.where(at, got[s * cz : (s + 1) * cz], 0.0), axis=0, keepdims=True)
            for h in range(group):
                got_ref[p, h : h + 1, s * 128 : (s + 1) * 128] = sums[:, h * 128 : (h + 1) * 128]

    picked = got_ref[...].reshape(out_ref.shape[1:]).astype(out_ref.dtype)
    for w in range(out_ref.shape[0]):
        out_ref[w] = picked
    for copy in res_copies:
        copy.wait()


def outer_residual_and_gather(copies, field, source, permittivity, counts, y_rows, up, down, residual, inner, line, depth):
    ns, _, cx, cy, cz = field.shape
    total = 3 * cx * cy
    groups, group = line.shape[0], line.shape[1] // 128
    operands = field, source, permittivity, y_rows, up, down, inner, line, depth, residual
    kernel, extra = staged(gather_kernel, 1, operands, (2, 3, 4, 5, 7, 8))
    anywhere = pl.BlockSpec(memory_space=pl.ANY)
    dma = pltpu.SemaphoreType.DMA
    grid_spec = pltpu.PrefetchScalarGridSpec(
        num_scalar_prefetch=1,
        grid=(1,),
        in_specs=[anywhere] * 10,
        out_specs=[anywhere, pl.BlockSpec((copies, groups * group, ns * 128), lambda g, *_: (0, 0, 0))],
        scratch_shapes=[
            pltpu.VMEM((ns, 3, 4, cy, cz), jnp.float32),
            pltpu.VMEM((ns, 3, 2, cy, cz), jnp.float32),
            pltpu.VMEM((total, ns * cz), jnp.bfloat16),
            pltpu.VMEM((ns * cz, total), jnp.bfloat16),
            pltpu.VMEM((ns, 5, cx, cz), jnp.float32),
            pltpu.VMEM((groups, group, ns * 128), jnp.float32),
            dma((4,)),
            dma((2,)),
            dma((3,)),
            *extra,
        ],
    )
    return pl.pallas_call(
        kernel,
        grid_spec=grid_spec,
        out_shape=[
            jax.ShapeDtypeStruct(field.shape, jnp.float32),
            jax.ShapeDtypeStruct((copies, groups * group, ns * 128), jnp.bfloat16),
        ],
        input_output_aliases={10: 0},
        compiler_params=pltpu.CompilerParams(vmem_limit_bytes=60 * MIB),
        name="outer_residual_gather",
    )(counts, *operands)


def fronts_kernel(ready, at_ref, given_ref, top_ref, mid_ref, low_ref, y_ref, top_buf, mid_buf, low_buf, given, x_buf, y_buf, sem):
    ns = y_buf.shape[0]
    jobs, base, column = [], 0, 0
    for w_ref, buf in ((top_ref, top_buf), (mid_ref, mid_buf), (low_ref, low_buf)):
        count, height, width = w_ref.shape
        rows = height
        while rows > 256 and rows * width * 2 > 4 * MIB:
            rows //= 2
        for f in range(count):
            for r in range(0, height, rows):
                at = pl.ds(r, rows)
                copy = pltpu.make_async_copy(w_ref.at[f, at], buf.at[f, at], sem.at[len(jobs)])
                jobs.append((copy, buf, f, at, slice(column, column + width), (base + r) // 128))
            base += height
            column += width
    jobs[0][0].start()
    ready()
    for job in jobs[1:]:
        job[0].start()
    given[...] = given_ref[...].astype(jnp.float32)
    for b in range(x_buf.shape[1] // 128):
        row = given[pl.ds(at_ref[b], 1), :]
        for s in range(ns):
            x_buf[s : s + 1, b * 128 : (b + 1) * 128] = row[:, s * 128 : (s + 1) * 128]
    for copy, buf, f, at, lanes, first in jobs:
        copy.wait()
        got = lax.dot_general(
            x_buf[:, lanes].astype(jnp.bfloat16),
            buf[f, at],
            (((1,), (1,)), ((), ())),
            preferred_element_type=jnp.float32,
        )
        for b in range(got.shape[1] // 128):
            for s in range(ns):
                y_buf[s, first + b : first + b + 1] = got[s : s + 1, b * 128 : (b + 1) * 128]
    y_ref[...] = y_buf[...].astype(y_ref.dtype)


def fronts(held_at, everyone, inverses):
    ns = everyone.shape[1] // 128
    blocks = sum(inv.shape[0] * inv.shape[1] for inv in inverses) // 128
    entries = sum(inv.size for inv in inverses)
    there = pl.BlockSpec(memory_space=pl.ANY)
    operands = everyone, *inverses
    kernel, extra = staged(fronts_kernel, 1, operands, (0,))
    grid_spec = pltpu.PrefetchScalarGridSpec(
        num_scalar_prefetch=1,
        grid=(1,),
        in_specs=[there] * 4,
        out_specs=pl.BlockSpec((ns, blocks, 128), lambda g, _: (0, 0, 0)),
        scratch_shapes=[
            *[pltpu.VMEM(inv.shape, inv.dtype) for inv in inverses],
            pltpu.VMEM(everyone.shape, jnp.float32),
            pltpu.VMEM((ns, held_at.shape[0] * 128), jnp.float32),
            pltpu.VMEM((ns, blocks, 128), jnp.float32),
            pltpu.SemaphoreType.DMA((64,)),
            *extra,
        ],
    )
    return pl.pallas_call(
        kernel,
        grid_spec=grid_spec,
        out_shape=jax.ShapeDtypeStruct((ns, blocks, 128), jnp.bfloat16),
        compiler_params=pltpu.CompilerParams(vmem_limit_bytes=60 * MIB),
        cost_estimate=pl.CostEstimate(flops=4 * entries, bytes_accessed=2 * entries, transcendentals=0),
        name="fronts",
    )(held_at, *operands)


def correct_kernel(
    count_ref, sol_ref, res_ref, perm_ref, own_line_ref, own_depth_ref, line_ref, depth_ref, given_ref,
    out_ref, new_ref, value_ref, field, residual, delta, x_halo, y_halo, back_z, back_y, in_sem, out_sem,
):
    ns, _, planes, cy, cz = sol_ref.shape
    f32, half = jnp.float32, jnp.bfloat16

    def copies_in(i):
        return [
            pltpu.make_async_copy(ref.at[:, :, i], buf.at[:, :, i], in_sem.at[n, i])
            for n, (ref, buf) in enumerate(((sol_ref, field), (res_ref, residual)))
        ]

    def copies_out(i):
        return [
            pltpu.make_async_copy(buf.at[:, :, i], ref.at[:, :, i], out_sem.at[n, i])
            for n, (ref, buf) in enumerate(((out_ref, field), (new_ref, residual)))
        ]

    for i in range(planes):
        for copy in copies_in(i):
            copy.start()
    chunks = line_ref.shape[0]
    capacity = chunks // (len(NEAR) - 1) * (line_ref.shape[1] // 128)

    def values_of(first, count):
        rows = [value_ref[pl.ds(count_ref[len(NEAR) + chunks + first + h], 1), :] for h in range(count)]
        return [jnp.concatenate([v[:, s * 128 : (s + 1) * 128] for v in rows], axis=1) for s in range(ns)]

    def times(a, b):
        return lax.dot_general(a, b, (((1,), (1,)), ((), ())), preferred_element_type=f32)

    value_ref[...] = given_ref[...].astype(f32)
    x_halo[...] = jnp.zeros_like(x_halo)
    y_halo[...] = jnp.zeros_like(y_halo)
    own_width = own_line_ref.shape[1]
    own_group = own_width // 128

    def own_part(p):
        values = values_of(p * own_group, own_group)
        hot = (iota((delta.shape[0], own_width), 0) == own_line_ref[pl.ds(p, 1), :]).astype(f32).astype(half)
        at = iota((cz, own_width), 0) == own_depth_ref[pl.ds(p, 1), :]
        return times(hot, jnp.concatenate([jnp.where(at, v, 0.0).astype(half) for v in values], axis=0))

    delta[...] = own_part(0)

    @pl.loop(1, pl.cdiv(count_ref[0], own_group))
    def _(p):
        delta[...] += own_part(p)

    width = line_ref.shape[1]
    group = width // 128
    place = (
        (x_halo, 0, 2 * cy),
        (x_halo, 2 * cy, 3 * cy),
        (y_halo, 0, 2 * planes),
        (y_halo, 2 * planes, 3 * planes),
        (y_halo, 5 * planes, 8),
        (y_halo, 5 * planes, 8),
    )
    for q, (target, first, height) in enumerate(place):

        @pl.loop(0, pl.cdiv(count_ref[q + 1], group))
        def _(p, q=q, target=target, first=first, height=height):
            row = q * (capacity // group) + p

            @pl.when(count_ref[len(NEAR) + row] > 0)
            def _():
                values = values_of((q + 1) * capacity + p * group, group)
                at = iota((height, width), 0) == line_ref[pl.ds(row, 1), :]
                hot = (iota((cz, width), 0) == depth_ref[pl.ds(row, 1), :]).astype(f32).astype(half)
                got = times(jnp.concatenate([jnp.where(at, v, 0.0) for v in values], axis=0).astype(half), hot)
                for s in range(ns):
                    target[s, first : first + height] += got[s * height : (s + 1) * height]

    def plane(s, c, i):
        return delta[pl.ds(pl.multiple_of((c * planes + i) * cy, 8), cy), s * cz : (s + 1) * cz]

    for s in range(ns):
        ex, ey, ez = (x_halo[s, (2 + c) * cy : (3 + c) * cy] for c in range(3))
        corner = y_halo[s, 5 * planes : 5 * planes + 1]
        back_z[s] = plane(s, 1, 0) - (ey + (ahead(ex, 0, corner) - ex))
        back_y[s] = (ez + (ahead(ex, 1) - ex)) - plane(s, 2, 0)

    @pl.loop(0, planes)
    def _(i):
        last = i == planes - 1
        after = jnp.minimum(i + 1, planes - 1)
        scaled = OMEGA_SQ * perm_ref[i].astype(f32)
        for copy in copies_in(i):
            copy.wait()
        for s in range(ns):
            own = [plane(s, c, i) for c in range(3)]
            beyond = [jnp.where(last, x_halo[s, c * cy : (c + 1) * cy], plane(s, c + 1, after)) for c in range(2)]
            y_row_x = y_halo[s, pl.ds(i, 1), :]
            y_row_z = y_halo[s, pl.ds(planes + i, 1), :]
            hx, hy, hz = (y_halo[s, pl.ds((2 + c) * planes + i, 1), :] for c in range(3))
            hy_after = jnp.where(
                last, y_halo[s, 5 * planes + 1 : 5 * planes + 2], y_halo[s, pl.ds(3 * planes + after, 1), :]
            )
            curls = curl_plane(
                own,
                beyond,
                back_z[s],
                back_y[s],
                y_row_x,
                y_row_z,
                (hx + (hy_after - hy)) - own[0],
                own[2] - (hz + (ahead(hy, 1) - hy)),
            )
            for c in range(3):
                field[s, c, i] += own[c]
                residual[s, c, i] -= curls[c] - scaled * own[c]
            back_z[s], back_y[s] = curls[3], curls[4]
        for copy in copies_out(i):
            copy.start()

    @pl.loop(0, planes)
    def _(i):
        for copy in copies_out(i):
            copy.wait()


def correct(field, residual, permittivity, counts, own_line, own_depth, line, depth, updates):
    ns, _, cx, cy, cz = field.shape
    anywhere = pl.BlockSpec(memory_space=pl.ANY)
    whole = lambda x: pl.BlockSpec(x.shape, lambda g, *_: (0,) * x.ndim)
    y_lines = 5 * cx + 8
    grid_spec = pltpu.PrefetchScalarGridSpec(
        num_scalar_prefetch=1,
        grid=(1,),
        in_specs=[
            anywhere,
            anywhere,
            *[whole(x) for x in (permittivity, own_line, own_depth, line, depth, updates)],
        ],
        out_specs=[anywhere, anywhere],
        scratch_shapes=[
            pltpu.VMEM(updates.shape, jnp.float32),
            pltpu.VMEM(field.shape, jnp.float32),
            pltpu.VMEM(field.shape, jnp.float32),
            pltpu.VMEM((3 * cx * cy, ns * cz), jnp.float32),
            pltpu.VMEM((ns, 5 * cy, cz), jnp.float32),
            pltpu.VMEM((ns, y_lines, cz), jnp.float32),
            pltpu.VMEM((ns, cy, cz), jnp.float32),
            pltpu.VMEM((ns, cy, cz), jnp.float32),
            pltpu.SemaphoreType.DMA((2, cx)),
            pltpu.SemaphoreType.DMA((2, cx)),
        ],
    )
    return pl.pallas_call(
        correct_kernel,
        grid_spec=grid_spec,
        out_shape=[jax.ShapeDtypeStruct(field.shape, jnp.float32)] * 2,
        compiler_params=pltpu.CompilerParams(vmem_limit_bytes=60 * MIB),
        name="correct",
    )(counts, field, residual, permittivity, own_line, own_depth, line, depth, updates)


def block_rows_of(inverses, wide_count, block_rows):
    per_device = sum(inv.shape[0] * inv.shape[1] for inv in inverses) // block_rows
    table, base = [], 0
    for inv in inverses:
        per = inv.shape[1] // block_rows
        for f in range(inv.shape[0]):
            b = np.arange(per * wide_count)
            table.append(b // per * per_device + base + f * per + b % per)
        base += inv.shape[0] * per
    return np.concatenate(table).astype(np.int32)


def block_columns_of(inverses, narrow_count, block_rows):
    table, base = [], 0
    for inv in inverses:
        per = inv.shape[2] // block_rows
        for _ in range(inv.shape[0]):
            table.append(base + np.arange(per * narrow_count).reshape(narrow_count, per))
            base += per * narrow_count
    return np.concatenate(table, axis=1).astype(np.int32)


def to_all_wide(block, wide_count):
    spread = jnp.broadcast_to(block[None], (wide_count, *block.shape)).reshape(-1, *block.shape[1:])
    return lax.all_to_all(spread, "wide", 0, 0, tiled=True)


def on_device(solution, source_term, permittivity, inv_top, inv_mid, inv_low, sep_tile, sep_cell):
    wide_count, narrow_count = lax.axis_size("wide"), lax.axis_size("narrow")
    my_wide, my_narrow = lax.axis_index("wide"), lax.axis_index("narrow")
    ns, _, cx, cy, cz = solution.shape
    block_count, block_rows = sep_cell.shape
    capacity = max(2, 2 * block_count // (wide_count * narrow_count))
    inverses = (inv_top[None], inv_mid, inv_low)

    y_rows = lax.all_gather(outer_rows(solution), "narrow", axis=0, tiled=False)
    to_up, to_down = outer_planes(solution, y_rows)
    steps = [(w, w + 1) for w in range(wide_count - 1)]
    up = lax.ppermute(to_up, "wide", steps)
    down = lax.ppermute(to_down, "wide", [(b, a) for a, b in steps])
    inner, inner_lines = inner_residual(solution, source_term, permittivity, y_rows)

    block_tile = sep_tile[:, 0]
    block_ids = jnp.arange(block_count, dtype=jnp.int32)
    slot_rank = jnp.sum(
        jnp.logical_and(
            block_tile[:, None] == block_tile[None, :], block_ids[None, :] < block_ids[:, None]
        ).astype(jnp.int32),
        axis=1,
    )
    offsets = np.array(NEAR, np.int32)
    near_wide, near_narrow = my_wide + offsets[:, 0], my_narrow + offsets[:, 1]
    inside = (near_wide >= 0) & (near_wide < wide_count) & (near_narrow >= 0) & (near_narrow < narrow_count)
    near_tile = jnp.where(inside, near_wide * narrow_count + near_narrow, -1)
    named = block_tile[None, :] == near_tile[:, None]
    counts = jnp.sum(named.astype(jnp.int32), axis=1)
    slots = jnp.arange(capacity, dtype=jnp.int32)
    match = jnp.logical_and(named[:, None, :], slot_rank[None, None, :] == slots[None, :, None])
    near_ids = jnp.sum(jnp.where(match, block_ids[None, None, :], 0), axis=2)
    near_rows = jnp.sum(
        jnp.where(match, block_rows_of(inverses, wide_count, block_rows)[None, None, :], 0), axis=2
    )
    found = slots[None, :] < counts[:, None]
    cells = sep_cell.at[near_ids.reshape(-1)].get(mode="promise_in_bounds").reshape(len(NEAR), capacity, block_rows)
    depth = cells % cz
    row = cells // cz
    part, at_i, at_j = row // (cx * cy), row // cy % cx, row % cy
    rule = (
        (row, row >= 0),
        ((part - 1) * cy + at_j, (part >= 1) & (at_i == 0)),
        (part * cy + at_j, at_i == cx - 1),
        (part // 2 * cx + at_i, (part != 1) & (at_j == 0)),
        (part * cx + at_i, at_j == cy - 1),
        (jnp.zeros_like(row), (part == 0) & (at_i == cx - 1) & (at_j == 0)),
        (jnp.ones_like(row), (part == 1) & (at_i == 0) & (at_j == cy - 1)),
    )
    line = jnp.stack(
        [jnp.where(found[q, :, None] & keep[q], at[q], -1) for q, (at, keep) in enumerate(rule)]
    )
    arrives = (block_tile % narrow_count * wide_count + block_tile // narrow_count) * capacity + slot_rank
    table = block_columns_of(inverses, narrow_count, block_rows)
    held_at = jnp.sum(
        jnp.where(
            (table[:, :, None] == block_ids) & (np.arange(narrow_count)[:, None, None] == my_narrow), arrives, 0
        ),
        axis=(0, 2),
    )
    own_width, width = min(8, capacity) * block_rows, min(4, capacity) * block_rows
    own_line, own_depth = line[0].reshape(-1, own_width), depth[0].reshape(-1, own_width)
    line, depth = line[1:].reshape(-1, width), depth[1:].reshape(-1, width)
    loads = jnp.concatenate([counts, jnp.max(line, axis=1) + 1, near_rows.reshape(-1)])

    residual, picked = outer_residual_and_gather(
        wide_count, solution, source_term, permittivity, counts, y_rows, up, down, inner, inner_lines, own_line, own_depth
    )
    column = lax.all_to_all(picked.reshape(-1, ns * block_rows), "wide", 0, 0, tiled=True)
    everyone = lax.all_gather(column, "narrow", axis=0, tiled=True)
    partial = fronts(held_at, everyone, inverses)
    rows = partial.shape[1]
    shares = lax.all_gather(partial, "narrow", axis=0, tiled=False)
    summed = jnp.sum(shares.astype(jnp.float32), axis=0).astype(jnp.bfloat16)
    summed = summed.transpose(1, 0, 2).reshape(rows, ns * block_rows)
    updates = to_all_wide(summed, wide_count)

    return tuple(correct(solution, residual, permittivity, loads, own_line, own_depth, line, depth, updates))


def solution(mesh):
    return jax.shard_map(
        on_device,
        mesh=mesh,
        in_specs=(
            P(None, None, "wide", "narrow", None),
            P(None, None, "wide", "narrow", None),
            P("wide", "narrow", None),
            P("wide", "narrow"),
            P(None, "wide", "narrow"),
            P(None, "wide", "narrow"),
            P(),
            P(),
        ),
        out_specs=(P(None, None, "wide", "narrow", None), P(None, None, "wide", "narrow", None)),
        check_vma=False,
    )
```
